256 devices in a mesh: ens: 8 (over z), polar: 2 (over core), azimuth: 16 (over y, x).
Axes of the slice: x: 4, y: 4, z: 8, core: 2. Of those that a mesh axis runs over, the one named last changes fastest.
Arguments:
- fields: bfloat16 [8, 16, 1440, 256], P('ens', 'polar', 'azimuth'), may hold values from -6 to 6
- basis_spectra: bfloat16 [9, 8, 5, 720], P(None, 'polar'), may hold values from -3 to 3
- support: int32 [8, 2], P('polar'), may hold values from 0 to 4, as said below
- weights: bfloat16 [9, 256, 256], replicated, may hold values from -0.125 to 0.125
- out_grad: bfloat16 [8, 8, 720, 256], P('ens', 'polar', 'azimuth'), may hold values from -6 to 6
Outputs:
- conv_out: bfloat16 [8, 8, 720, 256], P('ens', 'polar', 'azimuth')
- field_grad: bfloat16 [8, 16, 1440, 256], P('ens', 'polar', 'azimuth')
- weight_grad: float32 [9, 256, 256], P(None, 'azimuth')
The draws below stay inside these ranges and needn't reach their ends.
Inputs may be any that keep to these rules, and one draw needn't show every extreme that they name: Row o uses window rows support[o, 0] to support[o, 1]; support[o, 0] <= 2 <= support[o, 1]; rows o with o mod 4 equal to 0 or 3 use the whole window.
All inputs are finite; a program needn't handle non-finite values.
Results may differ from the reference program's by a relative error of at most 0.02.
Values may be sent and summed in bfloat16 or wider, within the bound.
No kernel may reach another device: no remote copies, remote signals or barrier semaphores. Data moves between devices by JAX's collectives and lax.ppermute only.
A program may use at most 64 MiB of HBM per device.

```python
import math
import jax
import jax.numpy as jnp
from jax import lax

C = 256
K = 9
WIN = 1440
SUPPORT = 5
WOUT = 720
MODES = 360
HOUT = 8
HIN = 16
MEMBERS = 8


def draw_support(key, part):
    rows_all = jnp.arange(HOUT, dtype=jnp.int32)
    centre = SUPPORT // 2
    low_rows = jax.random.randint(jax.random.fold_in(key, 11), (HOUT,), 0, centre + 1)
    high_rows = jax.random.randint(jax.random.fold_in(key, 12), (HOUT,), centre, SUPPORT)
    whole_rows = (rows_all % 4 == 0) | (rows_all % 4 == 3)
    low_rows = jnp.where(whole_rows, 0, low_rows)
    high_rows = jnp.where(whole_rows, SUPPORT - 1, high_rows)
    return jnp.stack([low_rows, high_rows], axis=1).astype(jnp.int32)


def level_of(key, shape, shards, smallest, top_value):
    def one(axis_at, blocks):
        draws = jax.random.uniform(jax.random.fold_in(jax.random.fold_in(key, 6), axis_at), (blocks,), jnp.float32, smallest / len(shards), top_value / len(shards))
        return jnp.repeat(jnp.exp(draws), shape[axis_at] // blocks).reshape((-1,) + (1,) * (len(shape) - axis_at - 1))

    loudness = one(*shards[0])
    for cut in shards[1:]:
        loudness = loudness * one(*cut)
    return loudness


def normal_values(stream_key, dims, spread, most, cuts=(), held_as=jnp.bfloat16):
    array = jax.random.normal(stream_key, dims, jnp.float32) * spread
    if len(cuts) > 0:
        array = level_of(stream_key, dims, cuts, -0.22, 0.18) * array
    return jnp.clip(array, min=-most, max=most).astype(held_as)


def setup_inputs(seed: int = 0) -> dict:
    keys = jax.random.split(jax.random.key(seed), 6)
    return {
        "fields": normal_values(keys[0], (MEMBERS, HIN, WIN, C), 1.0, 6.0, ((0, 8), (1, 2), (2, 16))),
        "basis_spectra": normal_values(keys[1], (K, HOUT, SUPPORT, WOUT), 0.45, 3.0, ((1, 2),)),
        "support": draw_support(jax.random.fold_in(keys[5], 71), 0),
        "weights": normal_values(keys[3], (K, C, C), (K * C) ** -0.5, 0.125),
        "out_grad": normal_values(keys[4], (MEMBERS, HOUT, WOUT, C), 1.0, 6.0, ((0, 8), (1, 2), (2, 16))),
    }


def make_tables(width_in, width_out):
    mode_count = width_out // 2
    longitude = jnp.arange(width_in, dtype=jnp.int32)
    frequency = jnp.arange(mode_count, dtype=jnp.int32)
    phases = (longitude[:, None] * frequency[None, :]) % width_in
    angles = phases.astype(jnp.float32) * (2.0 * math.pi / width_in)
    forward = jnp.concatenate([jnp.cos(angles), -jnp.sin(angles)], axis=1).astype(jnp.bfloat16)
    targets = jnp.arange(width_out, dtype=jnp.int32)
    phases_out = (frequency[:, None] * targets[None, :]) % width_out
    angles_out = phases_out.astype(jnp.float32) * (2.0 * math.pi / width_out)
    factors = jnp.where(frequency == 0, 1.0, 2.0).astype(jnp.float32)[:, None] / width_in
    inverse = jnp.concatenate([factors * jnp.cos(angles_out), -factors * jnp.sin(angles_out)], axis=0).astype(jnp.bfloat16)
    return forward, inverse


def mask_filters(filters, support):
    window = jnp.arange(filters.shape[2], dtype=jnp.int32)
    inside = (window[None, :] >= support[:, 0:1]) & (window[None, :] <= support[:, 1:2])
    return jnp.where(inside[None, :, :, None], filters, jnp.zeros_like(filters))


def combine_rows(masked, spectra, mode_count):
    outputs = masked.shape[1]
    total_re = jnp.zeros((masked.shape[0], outputs, spectra.shape[1], mode_count), jnp.float32)
    total_im = jnp.zeros_like(total_re)
    for offset in range(masked.shape[2]):
        rows_at = spectra[offset: offset + 2 * outputs - 1: 2]
        real_in = rows_at[None, :, :, :mode_count]
        imag_in = rows_at[None, :, :, mode_count:]
        filter_now = masked[:, :, offset, None, :].astype(jnp.float32)
        filter_re = filter_now[..., :mode_count]
        filter_im = filter_now[..., mode_count:]
        total_re = total_re + filter_re * real_in - filter_im * imag_in
        total_im = total_im + filter_re * imag_in + filter_im * real_in
    return jnp.concatenate([total_re, total_im], axis=-1)


def spread_rows(masked, grads, mode_count, rows_total):
    outputs = masked.shape[1]
    result = jnp.zeros((rows_total, grads.shape[2], grads.shape[3]), jnp.float32)
    grad_re = grads[..., :mode_count]
    grad_im = grads[..., mode_count:]
    for offset in range(masked.shape[2]):
        filter_now = masked[:, :, offset, None, :].astype(jnp.float32)
        filter_re = filter_now[..., :mode_count]
        filter_im = filter_now[..., mode_count:]
        back_re = jnp.sum(filter_re * grad_re + filter_im * grad_im, axis=0)
        back_im = jnp.sum(filter_re * grad_im - filter_im * grad_re, axis=0)
        result = result.at[offset: offset + 2 * outputs - 1: 2].add(jnp.concatenate([back_re, back_im], axis=-1))
    return result


def reference(fields, basis_spectra, support, weights, out_grad):
    forward, inverse = make_tables(WIN, WOUT)
    masked = mask_filters(basis_spectra, support)
    margin = SUPPORT // 2
    weights_wide = weights.astype(jnp.float32)
    inverse_wide = inverse.astype(jnp.float32)

    def member_pass(pair):
        field_one = jnp.swapaxes(pair[0], 1, 2)
        cotangent = pair[1]
        padded = jnp.pad(field_one, ((margin, margin), (0, 0), (0, 0)))
        rows_total = padded.shape[0]
        spectra = jnp.dot(padded.reshape(-1, WIN), forward, preferred_element_type=jnp.float32).reshape(rows_total, C, WOUT)
        mixed_spec = combine_rows(masked, spectra, MODES).astype(jnp.bfloat16)
        mixed_wide = mixed_spec.astype(jnp.float32)
        out_spec = jnp.einsum("khcm,kcd->hdm", mixed_wide, weights_wide).astype(jnp.bfloat16)
        conv_one = jnp.dot(out_spec.reshape(-1, WOUT), inverse, preferred_element_type=jnp.float32)
        conv_one = conv_one.reshape(HOUT, C, WOUT).astype(jnp.bfloat16)
        grad_spec = jnp.einsum("hvd,mv->hdm", cotangent.astype(jnp.float32), inverse_wide).astype(jnp.bfloat16)
        grad_wide = grad_spec.astype(jnp.float32)
        weight_part = jnp.einsum("khcm,hdm->kcd", mixed_wide, grad_wide)
        mixed_grad = jnp.einsum("kcd,hdm->khcm", weights_wide, grad_wide)
        spectra_grad = spread_rows(masked, mixed_grad, MODES, rows_total)[margin: margin + HIN].astype(jnp.bfloat16)
        field_one_grad = jnp.dot(spectra_grad.reshape(-1, WOUT), forward.T, preferred_element_type=jnp.float32)
        field_one_grad = field_one_grad.reshape(HIN, C, WIN).astype(jnp.bfloat16)
        return jnp.swapaxes(conv_one, 1, 2), jnp.swapaxes(field_one_grad, 1, 2), weight_part

    conv_out, field_grad, weight_parts = lax.map(member_pass, (fields, out_grad))
    weight_grad = jnp.sum(weight_parts, axis=0)
    return conv_out, field_grad, weight_grad
```

```python
import math

import jax
import jax.numpy as jnp
import numpy as np
from jax import lax
from jax.experimental import pallas as pl
from jax.experimental.pallas import tpu as pltpu
from jax.sharding import PartitionSpec as P

WIN, WOUT, MODES = 1440, 720, 360
K, C, SUPPORT = 9, 256, 5
HOUT, HIN = 8, 16
LANES, BANDS = 16, 2
SHARES = LANES * BANDS
M12, M16 = 12, 16
WPART, WROWS = 90, 96
VPART, VROWS = 45, 24
CHUNK_IN = WROWS + VROWS
CHUNK_MID = M16 + 2 * M12
F32, BF16 = jnp.float32, jnp.bfloat16
JOINT = ("polar", "azimuth")


def factor_tables():
    share = np.arange(SHARES)[:, None, None]
    col = np.arange(SHARES * 2 * M12).reshape(SHARES, 2, M12)
    mode = (12 * share + np.arange(M12)[None, None, :] + 0 * col).reshape(-1)
    imag = (np.arange(2)[None, :, None] + 0 * col).reshape(-1) == 1
    keep = mode < MODES
    alpha = 2 * math.pi * ((mode[None, :] * (WPART * np.arange(LANES)[:, None])) % WIN) / WIN
    beta = 2 * math.pi * ((mode[None, :] * np.arange(WROWS)[:, None]) % WIN) / WIN
    keep_w = keep[None, :] & (np.arange(WROWS)[:, None] < WPART)
    u1 = np.where(imag[None, :], -np.sin(alpha), np.cos(alpha))
    u2 = np.where(imag[None, :], -np.cos(alpha), -np.sin(alpha))
    f1 = np.where(keep_w, np.cos(beta), 0.0)
    f2 = np.where(keep_w, np.sin(beta), 0.0)
    wide = [a.astype(np.float32) for a in (u1, u2, f1, f2)]

    slot = np.arange(SHARES * M16)
    mode = 12 * (slot // M16) + slot % M16
    keep = (slot % M16 < M12) & (mode < MODES)
    scale = np.where(mode == 0, 1.0, 2.0) / WIN
    alpha = 2 * math.pi * ((mode[None, :] * (VPART * np.arange(LANES)[:, None])) % WOUT) / WOUT
    ca, sa = np.cos(alpha), np.sin(alpha)
    fs = []
    for part in range(2):
        v = VROWS * part + np.arange(VROWS)
        beta = 2 * math.pi * ((mode[None, :] * v[:, None]) % WOUT) / WOUT
        ok = keep[None, :] & (v[:, None] < VPART)
        fs.append(np.where(ok, scale * np.cos(beta), 0.0))
        fs.append(np.where(ok, scale * np.sin(beta), 0.0))
    narrow = [a.astype(np.float32) for a in (ca, sa, *fs)]
    return wide, narrow


def whole(shape):
    return pl.BlockSpec(shape, lambda *_: (0,) * len(shape))


def call(body, outs, name, flops=0, scratch=(), nbytes=1 << 20):
    def run(*args):
        return pl.pallas_call(
            body,
            out_shape=[jax.ShapeDtypeStruct(s, d) for s, d in outs],
            in_specs=[pl.BlockSpec(memory_space=pltpu.VMEM)] * len(args),
            out_specs=[pl.BlockSpec(memory_space=pltpu.VMEM)] * len(outs),
            scratch_shapes=list(scratch),
            name=name,
            cost_estimate=pl.CostEstimate(flops=flops, bytes_accessed=nbytes, transcendentals=0),
        )(*args)

    return run


def low_half(shape):
    return lax.broadcasted_iota(jnp.int32, shape, len(shape) - 1) < 64


def swap64(value):
    return pltpu.roll(value, 64, value.ndim - 1)


def dot(a, b):
    return jnp.dot(a, b, preferred_element_type=F32)


def pack_body(f_ref, g_ref, o_ref, pad_ref):
    for r in range(HIN // BANDS):
        for h in range(2):
            o_ref[2 * r + h, 0:WPART, :] = f_ref[r, :, 128 * h : 128 * h + 128]
            o_ref[2 * r + h, WPART:WROWS, :] = jnp.zeros((WROWS - WPART, 128), BF16)
    keep = low_half((VROWS, 128))
    for o in range(HOUT // BANDS):
        pad_ref[40:48, :] = jnp.zeros((8, C), F32)
        pad_ref[0:VPART, :] = g_ref[o].astype(F32)
        for i in range(2):
            top = pad_ref[0:24, 128 * i : 128 * i + 128]
            bottom = pad_ref[24:48, 128 * i : 128 * i + 128]
            even = jnp.where(keep, top, swap64(bottom))
            odd = jnp.where(keep, swap64(top), bottom)
            o_ref[4 * o + 2 * i, WROWS:CHUNK_IN, :] = even.astype(BF16)
            o_ref[4 * o + 2 * i + 1, WROWS:CHUNK_IN, :] = odd.astype(BF16)


def wide_table_body(u1, u2, f1, f2, tt_ref, t_ref):
    for b in range(LANES):
        block = u1[b : b + 1, :] * f1[...] + u2[b : b + 1, :] * f2[...]
        tt_ref[WROWS * b : WROWS * (b + 1), :] = block.astype(BF16)
    for i in range(12):
        for j in range(6):
            piece = tt_ref[128 * i : 128 * (i + 1), 128 * j : 128 * (j + 1)]
            t_ref[128 * j : 128 * (j + 1), 128 * i : 128 * (i + 1)] = piece.astype(F32).T.astype(BF16)


def narrow_table_body(ca, sa, f0c, f0s, f1c, f1s, v_ref, vt_ref):
    for part, (fc, fs) in enumerate(((f0c, f0s), (f1c, f1s))):
        for b in range(LANES):
            c, s = ca[b : b + 1, :], sa[b : b + 1, :]
            rows = slice(VROWS * b, VROWS * (b + 1))
            v_ref[2 * part, rows, :] = (c * fc[...] - s * fs[...]).astype(BF16)
            v_ref[2 * part + 1, rows, :] = (-(s * fc[...]) - c * fs[...]).astype(BF16)
    for n in range(4):
        for i in range(3):
            for j in range(4):
                piece = v_ref[n, 128 * i : 128 * (i + 1), 128 * j : 128 * (j + 1)]
                vt_ref[n, 128 * j : 128 * (j + 1), 128 * i : 128 * (i + 1)] = piece.astype(F32).T.astype(BF16)


def spectra_body(r_ref, t_ref, vt_ref, o_ref):
    x = r_ref[:, 0:WROWS, :].reshape(LANES * WROWS, 128)
    o_ref[:, M16:CHUNK_MID, :] = dot(t_ref[...], x).astype(BF16).reshape(SHARES, 2 * M12, 128)
    g = r_ref[:, WROWS:CHUNK_IN, :].reshape(LANES * VROWS, 128)
    re = dot(vt_ref[0], g) + swap64(dot(vt_ref[2], g))
    im = swap64(dot(vt_ref[1], g)) + dot(vt_ref[3], g)
    both = jnp.where(low_half(re.shape), re, im)
    o_ref[:, 0:M16, :] = both.astype(BF16).reshape(SHARES, M16, 128)


def mixing_body(b_ref, a_ref, at_ref, p_ref):
    rows, width = K * 16, HIN * 2 * M12
    row = lax.broadcasted_iota(jnp.int32, (120, width), 0)
    lane = lax.broadcasted_iota(jnp.int32, (120, width), 1)
    owner = (lax.broadcasted_iota(jnp.int32, (rows, width), 0) // 2) % HOUT
    total = jnp.zeros((rows, width), F32)
    for o in range(HOUT):
        shift = jnp.where(lane - row == 48 * (o - 1), 1.0, 0.0).astype(BF16)
        total = jnp.where(owner == o, dot(b_ref[...], shift), total)
    p_ref[...] = total
    mode = lax.broadcasted_iota(jnp.int32, (M16, width), 1) % M12
    same = lax.broadcasted_iota(jnp.int32, (M16, width), 0) == mode
    for i in range(rows):
        block = jnp.where(same, jnp.broadcast_to(p_ref[i : i + 1, :], (M16, width)), 0.0)
        a_ref[i // 16, M16 * (i % 16) : M16 * (i % 16 + 1), :] = block.astype(BF16)
    spot = lax.broadcasted_iota(jnp.int32, (16, 256), 1) // M16
    spread = jnp.where(lax.broadcasted_iota(jnp.int32, (16, 256), 0) == spot, 1.0, 0.0).astype(BF16)
    left = lax.broadcasted_iota(jnp.int32, (width, 256), 0) % M12
    right = lax.broadcasted_iota(jnp.int32, (width, 256), 1) % M16
    for k in range(K):
        part = p_ref[16 * k : 16 * (k + 1), :].astype(BF16)
        grown = lax.dot_general(part, spread, (((0,), (0,)), ((), ())), preferred_element_type=F32)
        at_ref[k] = jnp.where(left == right, grown, 0.0).astype(BF16)


def middle_body(band_ref, r_ref, a_ref, at_ref, w_ref, mine_ref, other_ref, o_ref, gs_ref, out_ref, sg_ref):
    keep = low_half((M16, 128))
    for o in range(HOUT):
        for i in range(2):
            first = r_ref[2 * o + i, 0, 0:M16, :].astype(F32)
            second = r_ref[2 * o + i, 1, 0:M16, :].astype(F32)
            cols = slice(128 * i, 128 * (i + 1))
            gs_ref[32 * o : 32 * o + 16, cols] = jnp.where(keep, first, swap64(second)).astype(BF16)
            gs_ref[32 * o + 16 : 32 * o + 32, cols] = jnp.where(keep, swap64(first), second).astype(BF16)
    rows = HIN * 2 * M12
    x = jnp.concatenate(
        [r_ref[:, h, M16:CHUNK_MID, :].reshape(rows, 128) for h in range(2)], axis=1
    )
    gs = gs_ref[...]
    low = band_ref[0, 0] == 0
    for k in range(K):
        mixed = dot(a_ref[k], x).astype(BF16)
        out_now = dot(mixed, w_ref[k])
        grad = lax.dot_general(mixed, gs, (((0,), (0,)), ((), ())), preferred_element_type=F32)
        left, right = grad[:, :128], grad[:, 128:]
        mine_ref[:, k] = jnp.where(low, left, right).astype(BF16).reshape(LANES, 16, 128)
        other_ref[:, k] = jnp.where(low, right, left).astype(BF16).reshape(LANES, 16, 128)
        back = lax.dot_general(gs, w_ref[k], (((1,), (1,)), ((), ())), preferred_element_type=F32)
        sg_now = dot(at_ref[k], back.astype(BF16))
        if k == 0:
            out_ref[...] = out_now
            sg_ref[...] = sg_now
        else:
            out_ref[...] += out_now
            sg_ref[...] += sg_now
    for o in range(HOUT):
        for i in range(2):
            cols = slice(128 * i, 128 * (i + 1))
            re = out_ref[32 * o : 32 * o + 16, cols]
            im = out_ref[32 * o + 16 : 32 * o + 32, cols]
            o_ref[4 * o + 2 * i, 0:M16, :] = jnp.where(keep, re, swap64(im)).astype(BF16)
            o_ref[4 * o + 2 * i + 1, 0:M16, :] = jnp.where(keep, swap64(re), im).astype(BF16)
    for r in range(HIN):
        for h in range(2):
            piece = sg_ref[24 * r : 24 * (r + 1), 128 * h : 128 * (h + 1)]
            o_ref[2 * r + h, M16:CHUNK_MID, :] = piece.astype(BF16)


def fields_body(r_ref, tt_ref, v_ref, o_ref):
    sg = r_ref[:, M16:CHUNK_MID, :].reshape(SHARES * 2 * M12, 128)
    o_ref[:, 0:WROWS, :] = dot(tt_ref[...], sg).astype(BF16).reshape(LANES, WROWS, 128)
    c = r_ref[:, 0:M16, :].reshape(SHARES * M16, 128)
    first = dot(v_ref[0], c) + swap64(dot(v_ref[1], c))
    second = swap64(dot(v_ref[2], c)) + dot(v_ref[3], c)
    both = jnp.where(low_half(first.shape), first, second)
    o_ref[:, WROWS:CHUNK_IN, :] = both.astype(BF16).reshape(LANES, VROWS, 128)


def unpack_body(r_ref, f_ref, c_ref):
    for r in range(HIN // BANDS):
        for h in range(2):
            f_ref[r, :, 128 * h : 128 * h + 128] = r_ref[2 * r + h, 0:WPART, :]
    keep = low_half((VROWS, 128))
    for o in range(HOUT // BANDS):
        for i in range(2):
            even = r_ref[4 * o + 2 * i, WROWS:CHUNK_IN, :].astype(F32)
            odd = r_ref[4 * o + 2 * i + 1, WROWS:CHUNK_IN, :].astype(F32)
            cols = slice(128 * i, 128 * (i + 1))
            c_ref[o, 0:VROWS, cols] = jnp.where(keep, even, swap64(odd)).astype(BF16)
            bottom = jnp.where(keep, swap64(even), odd).astype(BF16)
            c_ref[o, VROWS:VPART, cols] = bottom[0 : VPART - VROWS]


def mask_filters(filters, support):
    window = jnp.arange(filters.shape[2], dtype=jnp.int32)
    inside = (window[None, :] >= support[:, 0:1]) & (window[None, :] <= support[:, 1:2])
    return jnp.where(inside[None, :, :, None], filters, jnp.zeros_like(filters))


def filter_rows(basis_spectra, support):
    masked = mask_filters(basis_spectra, support)
    pairs = masked.reshape(K, HOUT // BANDS, SUPPORT, 2, MODES)
    pairs = jnp.pad(pairs, [(0, 0)] * 4 + [(0, SHARES * M12 - MODES)])
    pairs = pairs.reshape(K, HOUT // BANDS, SUPPORT, 2, BANDS, LANES * M12)
    start = lax.axis_index("azimuth") * M12
    here = lax.dynamic_slice_in_dim(pairs, start, M12, 5)
    here = jnp.moveaxis(here, 4, 0)
    here = lax.all_to_all(here, "polar", split_axis=0, concat_axis=0, tiled=True)
    here = jnp.moveaxis(here, 0, 1).reshape(K, HOUT, SUPPORT, 2, M12)
    re, im = here[:, :, :, 0], here[:, :, :, 1]
    rows = jnp.stack([jnp.stack([re, -im], axis=3), jnp.stack([im, re], axis=3)], axis=2)
    return rows.reshape(K * HOUT * 2, SUPPORT * 2 * M12)


def swap_bands(value):
    return lax.ppermute(value, "polar", [(0, 1), (1, 0)])


def local(fields, basis_spectra, support, weights, out_grad):
    members = lax.axis_size("ens")
    band = lax.axis_index("polar")
    wide, narrow = factor_tables()
    (sent,) = call(
        pack_body, [((LANES, CHUNK_IN, 128), BF16)], "pack", scratch=[pltpu.VMEM((48, C), F32)]
    )(fields[0], out_grad[0])
    landed = lax.all_to_all(sent, "azimuth", split_axis=0, concat_axis=0, tiled=True)

    tall, flat = call(
        wide_table_body, [((1536, 768), BF16), ((768, 1536), BF16)], "wide_table", nbytes=6 << 20
    )(*[jnp.asarray(a) for a in wide])
    inv, inv_t = call(
        narrow_table_body, [((4, 384, 512), BF16), ((4, 512, 384), BF16)], "narrow_table", nbytes=4 << 20
    )(*[jnp.asarray(a) for a in narrow])
    rows = filter_rows(basis_spectra, support)
    mix, mix_t = call(
        mixing_body,
        [((K, 256, 384), BF16), ((K, 384, 256), BF16)],
        "mixing",
        scratch=[pltpu.VMEM((K * 16, 384), F32)],
        nbytes=4 << 20,
    )(rows)

    (sent,) = call(spectra_body, [((SHARES, CHUNK_MID, 128), BF16)], "spectra", flops=600 << 20)(
        landed, flat, inv_t
    )
    landed = lax.all_to_all(sent, JOINT, split_axis=0, concat_axis=0, tiled=True)

    mine, other, sent = pl.pallas_call(
        middle_body,
        out_shape=[
            jax.ShapeDtypeStruct((LANES, K, 16, 128), BF16),
            jax.ShapeDtypeStruct((LANES, K, 16, 128), BF16),
            jax.ShapeDtypeStruct((SHARES, CHUNK_MID, 128), BF16),
        ],
        in_specs=[pl.BlockSpec(memory_space=pltpu.SMEM)] + [pl.BlockSpec(memory_space=pltpu.VMEM)] * 4,
        out_specs=[pl.BlockSpec(memory_space=pltpu.VMEM)] * 3,
        scratch_shapes=[
            pltpu.VMEM((256, 256), BF16),
            pltpu.VMEM((256, 256), F32),
            pltpu.VMEM((384, 256), F32),
        ],
        name="middle",
        cost_estimate=pl.CostEstimate(flops=2 << 30, bytes_accessed=6 << 20, transcendentals=0),
    )(band.astype(jnp.int32).reshape(1, 1), landed.reshape(HIN, 2, CHUNK_MID, 128), mix, mix_t, weights)
    landed = lax.all_to_all(sent, JOINT, split_axis=0, concat_axis=0, tiled=True)

    both = (mine.astype(F32) + swap_bands(other).astype(F32)).astype(BF16)
    parts = lax.all_to_all(both.reshape(LANES, K * 16, 128), "azimuth", split_axis=0, concat_axis=0, tiled=True)
    member = jnp.sum(parts.astype(F32), axis=0).astype(BF16)
    copies = jnp.broadcast_to(member[None], (members, K * 16, 128))
    copies = lax.all_to_all(copies, "ens", split_axis=0, concat_axis=0, tiled=True)
    half = jnp.sum(copies.astype(F32), axis=0)
    far = swap_bands(half)
    weight_grad = jnp.concatenate(
        [jnp.where(band == 0, half, far), jnp.where(band == 0, far, half)], axis=1
    ).reshape(K, 16, C)

    (sent,) = call(fields_body, [((LANES, CHUNK_IN, 128), BF16)], "fields", flops=600 << 20)(
        landed, tall, inv
    )
    landed = lax.all_to_all(sent, "azimuth", split_axis=0, concat_axis=0, tiled=True)
    field_grad, conv_out = call(
        unpack_body, [((8, WPART, C), BF16), ((4, VPART, C), BF16)], "unpack"
    )(landed)
    return (conv_out[None], field_grad[None], weight_grad)


def solution(mesh):
    placed = (
        P("ens", "polar", "azimuth", None),
        P(None, "polar", None, None),
        P("polar", None),
        P(),
        P("ens", "polar", "azimuth", None),
    )
    return jax.shard_map(
        local,
        mesh=mesh,
        in_specs=placed,
        out_specs=(
            P("ens", "polar", "azimuth", None),
            P("ens", "polar", "azimuth", None),
            P(None, "azimuth", None),
        ),
        check_vma=False,
    )
```

```python
import math

import jax
import jax.numpy as jnp
import numpy as np
from jax import lax
from jax.experimental import pallas as pl
from jax.experimental.pallas import tpu as pltpu
from jax.sharding import PartitionSpec as P

WIN, WOUT, MODES = 1440, 720, 360
K, C, SUPPORT = 9, 256, 5
HOUT, HIN = 8, 16
LANES, BANDS = 16, 2
SHARES = LANES * BANDS
HALF = LANES // 2
M12, M16 = 12, 16
WPART, WROWS = 90, 96
VPART, VROWS = 45, 24
CHUNK_IN = WROWS + VROWS
CHUNK_MID = M16 + 2 * M12
CHUNK_OUT = 2 * CHUNK_MID + 16 * K
F32, BF16 = jnp.float32, jnp.bfloat16
JOINT = ("polar", "azimuth")


def factor_tables():
    def build(slots, part, steps, period, scale):
        mode_all, keep, imag = slots
        parts = []
        for e in range(BANDS):
            mode = mode_all + e
            ok = keep & (mode < MODES)
            alpha = 2 * math.pi * ((mode[None, :] * (part * np.arange(HALF)[:, None])) % period) / period
            beta = 2 * math.pi * ((mode[None, :] * steps[:, None]) % period) / period
            ok = ok[None, :] & (steps[:, None] < part)
            size = np.where(mode == 0, 1.0, 2.0)[None, :] / WIN if scale else 1.0
            parts.append(
                (
                    np.where(imag[None, :], -np.sin(alpha), np.cos(alpha)),
                    np.where(imag[None, :], -np.cos(alpha), -np.sin(alpha)),
                    np.where(ok, size * np.cos(beta), 0.0),
                    np.where(ok, size * np.sin(beta), 0.0),
                )
            )
        return [np.stack(group).astype(np.float32) for group in zip(*parts)]

    a, ri, i = np.meshgrid(np.arange(LANES), np.arange(2), np.arange(M12), indexing="ij")
    slots = ((2 * (M12 * a + i)).reshape(-1), np.ones(a.size, bool), ri.reshape(-1) == 1)
    wide = build(slots, WPART, np.arange(WROWS), WIN, False)
    ri, a, i = np.meshgrid(np.arange(2), np.arange(LANES), np.arange(M16), indexing="ij")
    slots = ((2 * (M12 * a + i)).reshape(-1), i.reshape(-1) < M12, ri.reshape(-1) == 1)
    narrow = build(slots, VPART, np.arange(2 * VROWS), WOUT, True)
    return wide, narrow


def call(body, outs, name, flops=0, scratch=(), nbytes=1 << 20, vmem=16, smem=0):
    def run(*args):
        places = [pl.BlockSpec(memory_space=pltpu.SMEM)] * smem
        places += [pl.BlockSpec(memory_space=pltpu.VMEM)] * (len(args) - smem)
        return pl.pallas_call(
            body,
            out_shape=[jax.ShapeDtypeStruct(s, d) for s, d in outs],
            in_specs=places,
            out_specs=[pl.BlockSpec(memory_space=pltpu.VMEM)] * len(outs),
            scratch_shapes=list(scratch),
            name=name,
            compiler_params=pltpu.CompilerParams(vmem_limit_bytes=vmem << 20),
            cost_estimate=pl.CostEstimate(flops=flops, bytes_accessed=nbytes, transcendentals=0),
        )(*args)

    return run


def low_half(shape):
    return lax.broadcasted_iota(jnp.int32, shape, len(shape) - 1) < 64


def swap64(value):
    return pltpu.roll(value, 64, value.ndim - 1)


def dot(a, b):
    return jnp.dot(a, b, preferred_element_type=F32)


def one_hot(shape, row_of_column):
    row = lax.broadcasted_iota(jnp.int32, shape, 0)
    column = lax.broadcasted_iota(jnp.int32, shape, 1)
    return jnp.where(row == row_of_column(column), 1.0, 0.0).astype(BF16)


def row_of_latitude(column):
    return 16 * (column % 8) + column // 8


def row_of_output(column):
    return 48 * (column % 4) + column // 4


def pack_body(f_ref, g_ref, o_ref, flat_ref):
    for j in range(6):
        count = min(128, 8 * WPART - 128 * j)
        order = one_hot((128, count), row_of_latitude)
        block = dot(order, f_ref[128 * j : 128 * j + count, :]).astype(BF16)
        for r in range(8):
            for h in range(2):
                piece = block[16 * r : 16 * (r + 1), 128 * h : 128 * (h + 1)]
                o_ref[2 * r + h, 16 * j : 16 * (j + 1), :] = piece
    for v in range(VPART):
        flat_ref[4 * v : 4 * (v + 1), :] = g_ref[v].astype(F32)
    flat_ref[4 * VPART : 192, :] = jnp.zeros((192 - 4 * VPART, C), F32)
    rows = dot(one_hot((192, 192), row_of_output), flat_ref[...].astype(BF16))
    keep = low_half((VROWS, 128))
    for o in range(4):
        for i in range(2):
            cols = slice(128 * i, 128 * (i + 1))
            top, bottom = rows[48 * o : 48 * o + 24, cols], rows[48 * o + 24 : 48 * o + 48, cols]
            even = jnp.where(keep, top, swap64(bottom))
            odd = jnp.where(keep, swap64(top), bottom)
            o_ref[4 * o + 2 * i, WROWS:CHUNK_IN, :] = even.astype(BF16)
            o_ref[4 * o + 2 * i + 1, WROWS:CHUNK_IN, :] = odd.astype(BF16)


def flip(source, target, rows, columns):
    for i in range(rows // 128):
        for j in range(columns // 128):
            piece = source[128 * i : 128 * (i + 1), 128 * j : 128 * (j + 1)].astype(F32)
            target[128 * j : 128 * (j + 1), 128 * i : 128 * (i + 1)] = piece.T.astype(BF16)


def table_body(wu1, wu2, wf1, wf2, nu1, nu2, nf1, nf2, w_ref, wt_ref, v_ref, vt_ref):
    for e in range(BANDS):
        for b in range(HALF):
            one, two = wu1[e, b : b + 1, :], wu2[e, b : b + 1, :]
            block = one * wf1[e] + two * wf2[e]
            w_ref[e, WROWS * b : WROWS * (b + 1), :] = block.astype(BF16)
            one, two = nu1[e, b : b + 1, :], nu2[e, b : b + 1, :]
            for part in range(2):
                rows = slice(VROWS * part, VROWS * (part + 1))
                block = one * nf1[e, rows, :] + two * nf2[e, rows, :]
                start = VROWS * (HALF * part + b)
                v_ref[e, start : start + VROWS, :] = block.astype(BF16)
        flip(w_ref.at[e], wt_ref.at[e], HALF * WROWS, 2 * LANES * M12)
        flip(v_ref.at[e], vt_ref.at[e], 2 * HALF * VROWS, 2 * LANES * M16)


def spectra_body(r_ref, wt_ref, vt_ref, o_ref):
    left = r_ref[0:HALF, 0:WROWS, :].reshape(HALF * WROWS, 128).astype(F32)
    right = r_ref[HALF:LANES, 0:WROWS, :].reshape(HALF * WROWS, 128).astype(F32)
    g_left = r_ref[0:HALF, WROWS:CHUNK_IN, :].reshape(HALF * VROWS, 128).astype(F32)
    g_right = r_ref[HALF:LANES, WROWS:CHUNK_IN, :].reshape(HALF * VROWS, 128).astype(F32)
    keep = low_half((HALF * VROWS, 128))
    for e in range(BANDS):
        x = (left + right if e == 0 else left - right).astype(BF16)
        g = g_left + g_right if e == 0 else g_left - g_right
        turned = swap64(g)
        both = jnp.concatenate([jnp.where(keep, g, turned), jnp.where(keep, turned, g)], axis=0).astype(BF16)
        shares = slice(LANES * e, LANES * (e + 1))
        o_ref[shares, M16:CHUNK_MID, :] = dot(wt_ref[e], x).astype(BF16).reshape(LANES, 2 * M12, 128)
        got = dot(vt_ref[e], both)
        count = LANES * M16
        out = jnp.where(low_half((count, 128)), got[:count], got[count:])
        o_ref[shares, 0:M16, :] = out.astype(BF16).reshape(LANES, M16, 128)


def mixing_body(b_ref, a_ref, at_ref, p_ref):
    rows, width = K * 16, HIN * 2 * M12
    row = lax.broadcasted_iota(jnp.int32, (120, width), 0)
    lane = lax.broadcasted_iota(jnp.int32, (120, width), 1)
    owner = (lax.broadcasted_iota(jnp.int32, (rows, width), 0) // 2) % HOUT
    total = jnp.zeros((rows, width), F32)
    for o in range(HOUT):
        shift = jnp.where(lane - row == 48 * (o - 1), 1.0, 0.0).astype(BF16)
        total = jnp.where(owner == o, dot(b_ref[...], shift), total)
    p_ref[...] = total
    mode = lax.broadcasted_iota(jnp.int32, (M16, width), 1) % M12
    same = lax.broadcasted_iota(jnp.int32, (M16, width), 0) == mode
    for i in range(rows):
        block = jnp.where(same, jnp.broadcast_to(p_ref[i : i + 1, :], (M16, width)), 0.0)
        a_ref[i // 16, M16 * (i % 16) : M16 * (i % 16 + 1), :] = block.astype(BF16)
    spot = lax.broadcasted_iota(jnp.int32, (16, 256), 1) // M16
    spread = jnp.where(lax.broadcasted_iota(jnp.int32, (16, 256), 0) == spot, 1.0, 0.0).astype(BF16)
    left = lax.broadcasted_iota(jnp.int32, (width, 256), 0) % M12
    right = lax.broadcasted_iota(jnp.int32, (width, 256), 1) % M16
    for k in range(K):
        part = p_ref[16 * k : 16 * (k + 1), :].astype(BF16)
        grown = lax.dot_general(part, spread, (((0,), (0,)), ((), ())), preferred_element_type=F32)
        at_ref[k] = jnp.where(left == right, grown, 0.0).astype(BF16)


def middle_body(band_ref, r_ref, a_ref, at_ref, w_ref, mine_ref, other_ref, gs_ref, out_ref, sg_ref):
    keep = low_half((M16, 128))
    for o in range(HOUT):
        for i in range(2):
            first = r_ref[2 * o + i, 0, 0:M16, :].astype(F32)
            second = r_ref[2 * o + i, 1, 0:M16, :].astype(F32)
            cols = slice(128 * i, 128 * (i + 1))
            gs_ref[32 * o : 32 * o + 16, cols] = jnp.where(keep, first, swap64(second)).astype(BF16)
            gs_ref[32 * o + 16 : 32 * o + 32, cols] = jnp.where(keep, swap64(first), second).astype(BF16)
    rows = HIN * 2 * M12
    x = jnp.concatenate(
        [r_ref[:, h, M16:CHUNK_MID, :].reshape(rows, 128) for h in range(2)], axis=1
    )
    gs = gs_ref[...]
    low = band_ref[0, 0] == 0

    for k in range(K):
        mixed = dot(a_ref[k], x).astype(BF16)
        out_now = dot(mixed, w_ref[k])
        grad = lax.dot_general(mixed, gs, (((0,), (0,)), ((), ())), preferred_element_type=F32)
        where_to = (slice(None), slice(CHUNK_MID + 16 * k, CHUNK_MID + 16 * (k + 1)), slice(None))
        shape = (LANES, 16, 128)
        mine_ref[where_to] = jnp.where(low, grad[:, :128], grad[:, 128:]).astype(BF16).reshape(shape)
        other_ref[where_to] = jnp.where(low, grad[:, 128:], grad[:, :128]).astype(BF16).reshape(shape)
        back = lax.dot_general(gs, w_ref[k], (((1,), (1,)), ((), ())), preferred_element_type=F32)
        sg_now = dot(at_ref[k], back.astype(BF16))
        if k == 0:
            out_ref[...] = out_now
            sg_ref[...] = sg_now
        else:
            out_ref[...] += out_now
            sg_ref[...] += sg_now

    def output_rows(n):
        o, q = n // 4, n % 4
        cols = slice(128 * (q // 2), 128 * (q // 2 + 1))
        re = out_ref[32 * o : 32 * o + 16, cols]
        im = out_ref[32 * o + 16 : 32 * o + 32, cols]
        return jnp.where(keep, re, swap64(im)) if q % 2 == 0 else jnp.where(keep, swap64(re), im)

    def field_rows(n):
        r, h = n // 2, n % 2
        return sg_ref[24 * r : 24 * (r + 1), 128 * h : 128 * (h + 1)]

    for a in range(LANES):
        for rows, make in ((slice(0, M16), output_rows), (slice(M16, CHUNK_MID), field_rows)):
            first, second = make(a), make(a + LANES)
            mine_ref[a, rows, :] = jnp.where(low, first, second).astype(BF16)
            other_ref[a, rows, :] = jnp.where(low, second, first).astype(BF16)


def merge_body(band_ref, mine_ref, got_ref, o_ref):
    low = band_ref[0, 0] == 0
    for a in range(LANES):
        mine, got = mine_ref[a, 0:CHUNK_MID, :].astype(F32), got_ref[a, 0:CHUNK_MID, :].astype(F32)
        o_ref[a, 0:CHUNK_MID, :] = jnp.where(low, mine, got).astype(BF16)
        o_ref[a, CHUNK_MID : 2 * CHUNK_MID, :] = jnp.where(low, got, mine).astype(BF16)
        mine, got = mine_ref[a, CHUNK_MID:, :].astype(F32), got_ref[a, CHUNK_MID:, :].astype(F32)
        o_ref[a, 2 * CHUNK_MID :, :] = (mine + got).astype(BF16)


def fields_body(r_ref, w_ref, v_ref, o_ref):
    fields, outs = [], []
    for e in range(BANDS):
        start = CHUNK_MID * e
        sg = r_ref[:, start + M16 : start + CHUNK_MID, :].reshape(LANES * 2 * M12, 128)
        fields.append(dot(w_ref[e], sg))
        c = r_ref[:, start : start + M16, :].reshape(LANES * M16, 128).astype(F32)
        turned = swap64(c)
        keep = low_half(c.shape)
        both = jnp.concatenate([jnp.where(keep, c, turned), jnp.where(keep, turned, c)], axis=0).astype(BF16)
        got = dot(v_ref[e], both)
        count = HALF * VROWS
        outs.append(jnp.where(low_half((count, 128)), got[:count], got[count:]))
    for side in range(2):
        lanes = slice(HALF * side, HALF * (side + 1))
        field = fields[0] + fields[1] if side == 0 else fields[0] - fields[1]
        o_ref[lanes, 0:WROWS, :] = field.astype(BF16).reshape(HALF, WROWS, 128)
        out = outs[0] + outs[1] if side == 0 else outs[0] - outs[1]
        o_ref[lanes, WROWS:CHUNK_IN, :] = out.astype(BF16).reshape(HALF, VROWS, 128)


def unpack_body(r_ref, f_ref, c_ref, flat_ref):
    for j in range(6):
        count = min(128, 8 * WPART - 128 * j)
        halves = [
            jnp.concatenate([r_ref[2 * r + h, 16 * j : 16 * (j + 1), :] for r in range(8)], axis=0)
            for h in range(2)
        ]
        order = one_hot((128, count), row_of_latitude)
        block = lax.dot_general(
            order, jnp.concatenate(halves, axis=1), (((0,), (0,)), ((), ())), preferred_element_type=F32
        )
        f_ref[128 * j : 128 * j + count, :] = block.astype(BF16)
    keep = low_half((VROWS, 128))
    for o in range(4):
        for i in range(2):
            even = r_ref[4 * o + 2 * i, WROWS:CHUNK_IN, :].astype(F32)
            odd = r_ref[4 * o + 2 * i + 1, WROWS:CHUNK_IN, :].astype(F32)
            cols = slice(128 * i, 128 * (i + 1))
            flat_ref[48 * o : 48 * o + 24, cols] = jnp.where(keep, even, swap64(odd))
            flat_ref[48 * o + 24 : 48 * o + 48, cols] = jnp.where(keep, swap64(even), odd)
    rows = lax.dot_general(
        one_hot((192, 192), row_of_output),
        flat_ref[...].astype(BF16),
        (((0,), (0,)), ((), ())),
        preferred_element_type=F32,
    )
    for v in range(VPART):
        c_ref[v] = rows[4 * v : 4 * (v + 1), :].astype(BF16)


def mask_filters(filters, support):
    window = jnp.arange(filters.shape[2], dtype=jnp.int32)
    inside = (window[None, :] >= support[:, 0:1]) & (window[None, :] <= support[:, 1:2])
    return jnp.where(inside[None, :, :, None], filters, jnp.zeros_like(filters))


def swap_bands(value):
    return lax.ppermute(value, "polar", [(0, 1), (1, 0)])


def filter_rows(basis_spectra, support, low):
    masked = mask_filters(basis_spectra, support)
    pairs = masked.reshape(K, HOUT // BANDS, SUPPORT, 2, MODES)
    pairs = jnp.pad(pairs, [(0, 0)] * 4 + [(0, SHARES * M12 - MODES)])
    start = lax.axis_index("azimuth") * 2 * M12
    here = lax.dynamic_slice_in_dim(pairs, start, 2 * M12, 4).reshape(pairs.shape[:4] + (M12, 2))
    mine = jnp.where(low, here[..., 0], here[..., 1])
    got = swap_bands(jnp.where(low, here[..., 1], here[..., 0]))
    here = jnp.concatenate([jnp.where(low, mine, got), jnp.where(low, got, mine)], axis=1)
    re, im = here[:, :, :, 0], here[:, :, :, 1]
    rows = jnp.stack([jnp.stack([re, -im], axis=3), jnp.stack([im, re], axis=3)], axis=2)
    return rows.reshape(K * HOUT * 2, SUPPORT * 2 * M12)


def local(fields, basis_spectra, support, weights, out_grad):
    band = lax.axis_index("polar")
    low = band == 0
    spot = band.astype(jnp.int32).reshape(1, 1)
    wide, narrow = factor_tables()
    (sent,) = call(
        pack_body, [((LANES, CHUNK_IN, 128), BF16)], "pack", scratch=[pltpu.VMEM((192, C), F32)], vmem=8
    )(jnp.swapaxes(fields[0], 0, 1).reshape(8 * WPART, C), jnp.swapaxes(out_grad[0], 0, 1))
    landed = lax.all_to_all(sent, "azimuth", split_axis=0, concat_axis=0, tiled=True)

    filters, limits, sent = lax.optimization_barrier((basis_spectra, support, sent))
    rows = filter_rows(filters, limits, low)
    tables = [jnp.asarray(a) for a in wide + narrow]
    tables, sent = lax.optimization_barrier((tables, sent))
    tall, flat, inv, inv_t = call(
        table_body,
        [((2, 768, 384), BF16), ((2, 384, 768), BF16), ((2, 384, 512), BF16), ((2, 512, 384), BF16)],
        "tables",
        nbytes=5 << 20,
    )(*tables)
    mix, mix_t = call(
        mixing_body,
        [((K, 256, 384), BF16), ((K, 384, 256), BF16)],
        "mixing",
        scratch=[pltpu.VMEM((K * 16, 384), F32)],
        nbytes=4 << 20,
    )(rows)

    (sent,) = call(spectra_body, [((SHARES, CHUNK_MID, 128), BF16)], "spectra", flops=300 << 20)(
        landed, flat, inv_t
    )
    landed = lax.all_to_all(sent, JOINT, split_axis=0, concat_axis=0, tiled=True)

    chunk = (LANES, CHUNK_MID + 16 * K, 128)
    mine, other = call(
        middle_body,
        [(chunk, BF16), (chunk, BF16)],
        "middle",
        flops=2 << 30,
        nbytes=6 << 20,
        scratch=[pltpu.VMEM((256, 256), BF16), pltpu.VMEM((256, 256), F32), pltpu.VMEM((384, 256), F32)],
        smem=1,
        vmem=24,
    )(spot, landed.reshape(HIN, 2, CHUNK_MID, 128), mix, mix_t, weights)
    got = swap_bands(other)
    (sent,) = call(merge_body, [((LANES, CHUNK_OUT, 128), BF16)], "merge", nbytes=2 << 20, smem=1, vmem=8)(
        spot, mine, got
    )
    landed = lax.all_to_all(sent, "azimuth", split_axis=0, concat_axis=0, tiled=True)

    half = jnp.sum(landed[:, 2 * CHUNK_MID :, :].astype(F32), axis=0)
    for step in (1, 2, 4):
        half = half + lax.ppermute(half, "ens", [(i, i ^ step) for i in range(lax.axis_size("ens"))])
    far = swap_bands(half)
    weight_grad = jnp.concatenate([jnp.where(low, half, far), jnp.where(low, far, half)], axis=1)

    (sent,) = call(fields_body, [((LANES, CHUNK_IN, 128), BF16)], "fields", flops=300 << 20)(
        landed, tall, inv
    )
    landed = lax.all_to_all(sent, "azimuth", split_axis=0, concat_axis=0, tiled=True)
    field_grad, conv_out = call(
        unpack_body,
        [((8 * WPART, C), BF16), ((VPART, 4, C), BF16)],
        "unpack",
        scratch=[pltpu.VMEM((192, C), F32)],
        vmem=8,
    )(landed)
    field_grad = jnp.swapaxes(field_grad.reshape(WPART, 8, C), 0, 1)
    return (jnp.swapaxes(conv_out, 0, 1)[None], field_grad[None], weight_grad.reshape(K, 16, C))


def solution(mesh):
    placed = (
        P("ens", "polar", "azimuth", None),
        P(None, "polar", None, None),
        P("polar", None),
        P(),
        P("ens", "polar", "azimuth", None),
    )
    return jax.shard_map(
        local,
        mesh=mesh,
        in_specs=placed,
        out_specs=(
            P("ens", "polar", "azimuth", None),
            P("ens", "polar", "azimuth", None),
            P(None, "azimuth", None),
        ),
        check_vma=False,
    )
```

```python
import math

import jax
import jax.numpy as jnp
import numpy as np
from jax import lax
from jax.experimental import pallas as pl
from jax.experimental.pallas import tpu as pltpu
from jax.sharding import PartitionSpec as P


WIN, WOUT, MODES = 1440, 720, 360
K, C, SUPPORT = 9, 256, 5
HOUT, HIN = 8, 16
LANES, BANDS = 16, 2
SHARES = LANES * BANDS
HALF = LANES // 2
M12, M16 = 12, 16
WPART, WROWS = 90, 96
VPART, VROWS = 45, 24
CHUNK_IN = WROWS + VROWS
CHUNK_MID = M16 + 2 * M12
CHUNK_OUT = 2 * CHUNK_MID + 16 * K
F32, BF16 = jnp.float32, jnp.bfloat16
JOINT = ("polar", "azimuth")


def factor_tables():
    def build(slots, part, steps, period, scale):
        mode_all, keep, imag = slots
        parts = []
        for e in range(BANDS):
            mode = mode_all + e
            ok = keep & (mode < MODES)
            alpha = 2 * math.pi * ((mode[None, :] * (part * np.arange(HALF)[:, None])) % period) / period
            beta = 2 * math.pi * ((mode[None, :] * steps[:, None]) % period) / period
            ok = ok[None, :] & (steps[:, None] < part)
            size = np.where(mode == 0, 1.0, 2.0)[None, :] / WIN if scale else 1.0
            parts.append(
                (
                    np.where(imag[None, :], -np.sin(alpha), np.cos(alpha)),
                    np.where(imag[None, :], -np.cos(alpha), -np.sin(alpha)),
                    np.where(ok, size * np.cos(beta), 0.0),
                    np.where(ok, size * np.sin(beta), 0.0),
                )
            )
        return [np.stack(group).astype(np.float32) for group in zip(*parts)]

    a, ri, i = np.meshgrid(np.arange(LANES), np.arange(2), np.arange(M12), indexing="ij")
    slots = ((2 * (M12 * a + i)).reshape(-1), np.ones(a.size, bool), ri.reshape(-1) == 1)
    wide = build(slots, WPART, np.arange(WROWS), WIN, False)
    ri, a, i = np.meshgrid(np.arange(2), np.arange(LANES), np.arange(M16), indexing="ij")
    slots = ((2 * (M12 * a + i)).reshape(-1), i.reshape(-1) < M12, ri.reshape(-1) == 1)
    narrow = build(slots, VPART, np.arange(2 * VROWS), WOUT, True)
    return wide, narrow


HBM = pl.BlockSpec(memory_space=pltpu.HBM)
VMEM = pl.BlockSpec(memory_space=pltpu.VMEM)
SMEM = pl.BlockSpec(memory_space=pltpu.SMEM)


def call(body, places, outs, flops=0, scratch=(), nbytes=1 << 20, vmem=16):
    return pl.pallas_call(
        body,
        out_shape=[jax.ShapeDtypeStruct(s, d) for s, d in outs],
        in_specs=places,
        out_specs=[VMEM] * len(outs),
        scratch_shapes=list(scratch),
        compiler_params=pltpu.CompilerParams(vmem_limit_bytes=vmem << 20),
        cost_estimate=pl.CostEstimate(flops=flops, bytes_accessed=nbytes, transcendentals=0),
    )


def in_hbm(value):
    return pltpu.with_memory_space_constraint(value, pltpu.HBM)


def fetch(sources, targets, sems):
    copies = [pltpu.make_async_copy(s, t, sems.at[n]) for n, (s, t) in enumerate(zip(sources, targets))]
    for copy in copies:
        copy.start()
    return copies


def low_half(shape):
    return lax.broadcasted_iota(jnp.int32, shape, len(shape) - 1) < 64


def swap64(value):
    return pltpu.roll(value, 64, value.ndim - 1)


def dot(a, b):
    return jnp.dot(a, b, preferred_element_type=F32)


def one_hot(shape, row_of_column):
    row = lax.broadcasted_iota(jnp.int32, shape, 0)
    column = lax.broadcasted_iota(jnp.int32, shape, 1)
    return jnp.where(row == row_of_column(column), 1.0, 0.0).astype(BF16)


def row_of_latitude(column):
    return 16 * (column % 8) + column // 8


def row_of_output(column):
    return 48 * (column % 4) + column // 4


def pack_body(f_hbm, g_hbm, o_ref, f_ref, g_ref, flat_ref, sems):
    copies = fetch((f_hbm, g_hbm), (f_ref, g_ref), sems)
    copies[0].wait()
    for j in range(6):
        count = min(128, 8 * WPART - 128 * j)
        order = one_hot((128, count), row_of_latitude)
        block = dot(order, f_ref[128 * j : 128 * j + count, :]).astype(BF16)
        for r in range(8):
            for h in range(2):
                piece = block[16 * r : 16 * (r + 1), 128 * h : 128 * (h + 1)]
                o_ref[2 * r + h, 16 * j : 16 * (j + 1), :] = piece
    copies[1].wait()
    for v in range(VPART):
        flat_ref[4 * v : 4 * (v + 1), :] = g_ref[v].astype(F32)
    flat_ref[4 * VPART : 192, :] = jnp.zeros((192 - 4 * VPART, C), F32)
    rows = dot(one_hot((192, 192), row_of_output), flat_ref[...].astype(BF16))
    keep = low_half((VROWS, 128))
    for o in range(4):
        for i in range(2):
            cols = slice(128 * i, 128 * (i + 1))
            top, bottom = rows[48 * o : 48 * o + 24, cols], rows[48 * o + 24 : 48 * o + 48, cols]
            even = jnp.where(keep, top, swap64(bottom))
            odd = jnp.where(keep, swap64(top), bottom)
            o_ref[4 * o + 2 * i, WROWS:CHUNK_IN, :] = even.astype(BF16)
            o_ref[4 * o + 2 * i + 1, WROWS:CHUNK_IN, :] = odd.astype(BF16)


def flip(source, target, rows, columns):
    for i in range(rows // 128):
        for j in range(columns // 128):
            piece = source[128 * i : 128 * (i + 1), 128 * j : 128 * (j + 1)].astype(F32)
            target[128 * j : 128 * (j + 1), 128 * i : 128 * (i + 1)] = piece.T.astype(BF16)


def fill_tables(w, v, w_ref, v_ref):
    for e in range(BANDS):
        for b in range(HALF):
            one, two = w[0][e, b : b + 1, :], w[1][e, b : b + 1, :]
            block = one * w[2][e] + two * w[3][e]
            w_ref[e, WROWS * b : WROWS * (b + 1), :] = block.astype(BF16)
            one, two = v[0][e, b : b + 1, :], v[1][e, b : b + 1, :]
            for part in range(2):
                rows = slice(VROWS * part, VROWS * (part + 1))
                block = one * v[2][e, rows, :] + two * v[3][e, rows, :]
                start = VROWS * (HALF * part + b)
                v_ref[e, start : start + VROWS, :] = block.astype(BF16)


def table_body(*refs):
    factors, (w_ref, v_ref) = refs[:8], refs[8:10]
    held, sems = refs[10:18], refs[18]
    for copy in fetch(factors, held, sems):
        copy.wait()
    fill_tables(held[:4], held[4:], w_ref, v_ref)


def flipped_table_body(*refs):
    factors, (wt_ref, vt_ref) = refs[:8], refs[8:10]
    held, (w_ref, v_ref, sems) = refs[10:18], refs[18:]
    for copy in fetch(factors, held, sems):
        copy.wait()
    fill_tables(held[:4], held[4:], w_ref, v_ref)
    for e in range(BANDS):
        flip(w_ref.at[e], wt_ref.at[e], HALF * WROWS, 2 * LANES * M12)
        flip(v_ref.at[e], vt_ref.at[e], 2 * HALF * VROWS, 2 * LANES * M16)


def spectra_body(r_ref, wt_ref, vt_ref, o_ref):
    left = r_ref[0:HALF, 0:WROWS, :].reshape(HALF * WROWS, 128).astype(F32)
    right = r_ref[HALF:LANES, 0:WROWS, :].reshape(HALF * WROWS, 128).astype(F32)
    g_left = r_ref[0:HALF, WROWS:CHUNK_IN, :].reshape(HALF * VROWS, 128).astype(F32)
    g_right = r_ref[HALF:LANES, WROWS:CHUNK_IN, :].reshape(HALF * VROWS, 128).astype(F32)
    keep = low_half((HALF * VROWS, 128))
    for e in range(BANDS):
        x = (left + right if e == 0 else left - right).astype(BF16)
        g = g_left + g_right if e == 0 else g_left - g_right
        turned = swap64(g)
        both = jnp.concatenate([jnp.where(keep, g, turned), jnp.where(keep, turned, g)], axis=0).astype(BF16)
        shares = slice(LANES * e, LANES * (e + 1))
        o_ref[shares, M16:CHUNK_MID, :] = dot(wt_ref[e], x).astype(BF16).reshape(LANES, 2 * M12, 128)
        got = dot(vt_ref[e], both)
        count = LANES * M16
        out = jnp.where(low_half((count, 128)), got[:count], got[count:])
        o_ref[shares, 0:M16, :] = out.astype(BF16).reshape(LANES, M16, 128)


def filter_body(spot_ref, support_ref, p_hbm, mine_ref, other_ref, p_ref, flat_ref, sems):
    (copy,) = fetch((p_hbm,), (p_ref,), sems)
    rows = K * SUPPORT * 4
    band, start = spot_ref[0, 0], 2 * M12 * spot_ref[0, 1]
    line = lax.broadcasted_iota(jnp.int32, (WOUT, 128), 0)
    slot = lax.broadcasted_iota(jnp.int32, (WOUT, 128), 1)
    place = slot % 64
    parity = jnp.where(slot < 64, band, 1 - band)
    mode = start + 2 * (place % M12) + parity
    hit = (line == mode + MODES * (place // M12)) & (place < 2 * M12) & (mode < MODES)
    chosen = jnp.where(hit, 1.0, 0.0).astype(BF16)
    row = lax.broadcasted_iota(jnp.int32, (rows, 128), 0)
    window, output = (row // 4) % SUPPORT, row % 4
    first = jnp.zeros((rows, 128), jnp.int32)
    last = jnp.zeros((rows, 128), jnp.int32)
    for o in range(4):
        first = jnp.where(output == o, support_ref[o, 0], first)
        last = jnp.where(output == o, support_ref[o, 1], last)
    copy.wait()
    for n in range(K * SUPPORT):
        flat_ref[4 * n : 4 * (n + 1), :] = p_ref[n].astype(F32)
    got = dot(flat_ref[0:rows, :].astype(BF16), chosen)
    got = jnp.where((window >= first) & (window <= last), got, 0.0)
    mine_ref[...] = got.astype(BF16)
    other_ref[...] = swap64(got).astype(BF16)


def mixing_body(spot_ref, mine_ref, got_ref, a_ref, at_ref, p_ref):
    rows, width, count = K * 16, HIN * 2 * M12, K * SUPPORT * 4
    low = spot_ref[0, 0] == 0
    mine, got = mine_ref[...].astype(F32), got_ref[...].astype(F32)
    halves = (jnp.where(low, mine, got).astype(BF16), jnp.where(low, got, mine).astype(BF16))
    x = lax.broadcasted_iota(jnp.int32, (128, width), 0)
    lane = lax.broadcasted_iota(jnp.int32, (128, width), 1)
    same, cross = lane % M12, lane % (2 * M12) < M12
    straight = x == same + jnp.where(cross, 0, M12)
    turned = x == same + jnp.where(cross, M12, 0)
    tiles = (
        jnp.where(straight, jnp.where(cross, 1.0, -1.0), 0.0).astype(BF16),
        jnp.where(turned, 1.0, 0.0).astype(BF16),
    )
    row = lax.broadcasted_iota(jnp.int32, (count, width), 0)
    lane = lax.broadcasted_iota(jnp.int32, (count, width), 1)
    reach = 2 * (row % 4) + (row // 4) % SUPPORT - 2 - lane // (2 * M12)
    target = lax.broadcasted_iota(jnp.int32, (rows, count), 0)
    source = lax.broadcasted_iota(jnp.int32, (rows, count), 1)
    key = target - 16 * (source // 20) - 2 * (source % 4)
    total = jnp.zeros((rows, width), F32)
    for half in range(2):
        for ri in range(2):
            spread = dot(halves[half], tiles[ri])
            spread = jnp.where(reach == -8 * half, spread, 0.0).astype(BF16)
            collect = jnp.where(key == 8 * half + ri, 1.0, 0.0).astype(BF16)
            total = total + dot(collect, spread)
    p_ref[...] = total
    mode = lax.broadcasted_iota(jnp.int32, (M16, width), 1) % M12
    same = lax.broadcasted_iota(jnp.int32, (M16, width), 0) == mode
    for i in range(rows):
        block = jnp.where(same, jnp.broadcast_to(p_ref[i : i + 1, :], (M16, width)), 0.0)
        a_ref[i // 16, M16 * (i % 16) : M16 * (i % 16 + 1), :] = block.astype(BF16)
    spot = lax.broadcasted_iota(jnp.int32, (16, 256), 1) // M16
    spread = jnp.where(lax.broadcasted_iota(jnp.int32, (16, 256), 0) == spot, 1.0, 0.0).astype(BF16)
    left = lax.broadcasted_iota(jnp.int32, (width, 256), 0) % M12
    right = lax.broadcasted_iota(jnp.int32, (width, 256), 1) % M16
    for k in range(K):
        part = p_ref[16 * k : 16 * (k + 1), :].astype(BF16)
        grown = lax.dot_general(part, spread, (((0,), (0,)), ((), ())), preferred_element_type=F32)
        at_ref[k] = jnp.where(left == right, grown, 0.0).astype(BF16)


def middle_body(
    band_ref, r_ref, a_hbm, at_hbm, w_hbm, mine_ref, other_ref, gs_ref, out_ref, sg_ref, a_ref, at_ref, w_ref, sems
):
    copies = [
        fetch((a_hbm.at[k], w_hbm.at[k], at_hbm.at[k]), (a_ref.at[k], w_ref.at[k], at_ref.at[k]), sems.at[k])
        for k in range(K)
    ]
    keep = low_half((M16, 128))
    for o in range(HOUT):
        for i in range(2):
            first = r_ref[2 * o + i, 0, 0:M16, :].astype(F32)
            second = r_ref[2 * o + i, 1, 0:M16, :].astype(F32)
            cols = slice(128 * i, 128 * (i + 1))
            gs_ref[32 * o : 32 * o + 16, cols] = jnp.where(keep, first, swap64(second)).astype(BF16)
            gs_ref[32 * o + 16 : 32 * o + 32, cols] = jnp.where(keep, swap64(first), second).astype(BF16)
    rows = HIN * 2 * M12
    x = jnp.concatenate(
        [r_ref[:, h, M16:CHUNK_MID, :].reshape(rows, 128) for h in range(2)], axis=1
    )
    gs = gs_ref[...]
    low = band_ref[0, 0] == 0

    for k in range(K):
        for copy in copies[k]:
            copy.wait()
        mixed = dot(a_ref[k], x).astype(BF16)
        out_now = dot(mixed, w_ref[k])
        grad = lax.dot_general(mixed, gs, (((0,), (0,)), ((), ())), preferred_element_type=F32)
        where_to = (slice(None), slice(CHUNK_MID + 16 * k, CHUNK_MID + 16 * (k + 1)), slice(None))
        shape = (LANES, 16, 128)
        mine_ref[where_to] = jnp.where(low, grad[:, :128], grad[:, 128:]).astype(BF16).reshape(shape)
        other_ref[where_to] = jnp.where(low, grad[:, 128:], grad[:, :128]).astype(BF16).reshape(shape)
        back = lax.dot_general(gs, w_ref[k], (((1,), (1,)), ((), ())), preferred_element_type=F32)
        sg_now = dot(at_ref[k], back.astype(BF16))
        if k == 0:
            out_ref[...] = out_now
            sg_ref[...] = sg_now
        else:
            out_ref[...] += out_now
            sg_ref[...] += sg_now

    def output_rows(n):
        o, q = n // 4, n % 4
        cols = slice(128 * (q // 2), 128 * (q // 2 + 1))
        re = out_ref[32 * o : 32 * o + 16, cols]
        im = out_ref[32 * o + 16 : 32 * o + 32, cols]
        return jnp.where(keep, re, swap64(im)) if q % 2 == 0 else jnp.where(keep, swap64(re), im)

    def field_rows(n):
        r, h = n // 2, n % 2
        return sg_ref[24 * r : 24 * (r + 1), 128 * h : 128 * (h + 1)]

    for a in range(LANES):
        for rows, make in ((slice(0, M16), output_rows), (slice(M16, CHUNK_MID), field_rows)):
            first, second = make(a), make(a + LANES)
            mine_ref[a, rows, :] = jnp.where(low, first, second).astype(BF16)
            other_ref[a, rows, :] = jnp.where(low, second, first).astype(BF16)


def merge_body(band_ref, mine_ref, got_ref, o_ref):
    low = band_ref[0, 0] == 0
    for a in range(LANES):
        mine, got = mine_ref[a, 0:CHUNK_MID, :].astype(F32), got_ref[a, 0:CHUNK_MID, :].astype(F32)
        o_ref[a, 0:CHUNK_MID, :] = jnp.where(low, mine, got).astype(BF16)
        o_ref[a, CHUNK_MID : 2 * CHUNK_MID, :] = jnp.where(low, got, mine).astype(BF16)
        mine, got = mine_ref[a, CHUNK_MID:, :].astype(F32), got_ref[a, CHUNK_MID:, :].astype(F32)
        o_ref[a, 2 * CHUNK_MID :, :] = (mine + got).astype(BF16)


def fields_body(r_ref, w_ref, v_ref, o_ref):
    fields, outs = [], []
    for e in range(BANDS):
        start = CHUNK_MID * e
        sg = r_ref[:, start + M16 : start + CHUNK_MID, :].reshape(LANES * 2 * M12, 128)
        fields.append(dot(w_ref[e], sg))
        c = r_ref[:, start : start + M16, :].reshape(LANES * M16, 128).astype(F32)
        turned = swap64(c)
        keep = low_half(c.shape)
        both = jnp.concatenate([jnp.where(keep, c, turned), jnp.where(keep, turned, c)], axis=0).astype(BF16)
        got = dot(v_ref[e], both)
        count = HALF * VROWS
        outs.append(jnp.where(low_half((count, 128)), got[:count], got[count:]))
    for side in range(2):
        lanes = slice(HALF * side, HALF * (side + 1))
        field = fields[0] + fields[1] if side == 0 else fields[0] - fields[1]
        o_ref[lanes, 0:WROWS, :] = field.astype(BF16).reshape(HALF, WROWS, 128)
        out = outs[0] + outs[1] if side == 0 else outs[0] - outs[1]
        o_ref[lanes, WROWS:CHUNK_IN, :] = out.astype(BF16).reshape(HALF, VROWS, 128)


def unpack_body(r_ref, f_ref, c_ref, flat_ref):
    for j in range(6):
        count = min(128, 8 * WPART - 128 * j)
        halves = [
            jnp.concatenate([r_ref[2 * r + h, 16 * j : 16 * (j + 1), :] for r in range(8)], axis=0)
            for h in range(2)
        ]
        order = one_hot((128, count), row_of_latitude)
        block = lax.dot_general(
            order, jnp.concatenate(halves, axis=1), (((0,), (0,)), ((), ())), preferred_element_type=F32
        )
        f_ref[128 * j : 128 * j + count, :] = block.astype(BF16)
    keep = low_half((VROWS, 128))
    for o in range(4):
        for i in range(2):
            even = r_ref[4 * o + 2 * i, WROWS:CHUNK_IN, :].astype(F32)
            odd = r_ref[4 * o + 2 * i + 1, WROWS:CHUNK_IN, :].astype(F32)
            cols = slice(128 * i, 128 * (i + 1))
            flat_ref[48 * o : 48 * o + 24, cols] = jnp.where(keep, even, swap64(odd))
            flat_ref[48 * o + 24 : 48 * o + 48, cols] = jnp.where(keep, swap64(even), odd)
    rows = lax.dot_general(
        one_hot((192, 192), row_of_output),
        flat_ref[...].astype(BF16),
        (((0,), (0,)), ((), ())),
        preferred_element_type=F32,
    )
    for v in range(VPART):
        c_ref[v] = rows[4 * v : 4 * (v + 1), :].astype(BF16)


def swap_bands(value):
    return lax.ppermute(value, "polar", [(0, 1), (1, 0)])


def local(fields, basis_spectra, support, weights, out_grad):
    band = lax.axis_index("polar").astype(jnp.int32)
    low = band == 0
    spot = jnp.stack([band, lax.axis_index("azimuth").astype(jnp.int32)]).reshape(1, 2)
    wide, narrow = factor_tables()
    dma = pltpu.SemaphoreType.DMA
    (sent,) = call(
        pack_body,
        [HBM, HBM],
        [((LANES, CHUNK_IN, 128), BF16)],
        scratch=[
            pltpu.VMEM((8 * WPART, C), BF16),
            pltpu.VMEM((VPART, 4, C), BF16),
            pltpu.VMEM((192, C), F32),
            dma((2,)),
        ],
    )(
        in_hbm(jnp.swapaxes(fields[0], 0, 1).reshape(8 * WPART, C)), in_hbm(jnp.swapaxes(out_grad[0], 0, 1))
    )
    landed = lax.all_to_all(sent, "azimuth", split_axis=0, concat_axis=0, tiled=True)

    filters, limits, sent = lax.optimization_barrier((basis_spectra, support, sent))
    mine, other = call(
        filter_body,
        [SMEM, SMEM, HBM],
        [((K * SUPPORT * 4, 128), BF16)] * 2,
        scratch=[pltpu.VMEM((K * SUPPORT, 4, WOUT), BF16), pltpu.VMEM((184, WOUT), F32), dma((1,))],
    )(spot, limits, in_hbm(jnp.swapaxes(filters, 1, 2).reshape(K * SUPPORT, 4, WOUT)))
    got = swap_bands(other)
    factors = [a for a in wide + narrow]
    held = [pltpu.VMEM(a.shape, F32) for a in factors]
    factors, sent = lax.optimization_barrier(([jnp.asarray(a) for a in factors], sent))
    flat, inv_t = call(
        flipped_table_body,
        [HBM] * 8,
        [((2, 384, 768), BF16), ((2, 512, 384), BF16)],
        nbytes=5 << 20,
        scratch=held + [pltpu.VMEM((2, 768, 384), BF16), pltpu.VMEM((2, 384, 512), BF16), dma((8,))],
    )(*[in_hbm(a) for a in factors])

    landed, mine, got = lax.optimization_barrier((landed, mine, got))
    (sent,) = call(spectra_body, [VMEM] * 3, [((SHARES, CHUNK_MID, 128), BF16)], flops=300 << 20)(landed, flat, inv_t)
    landed = lax.all_to_all(sent, JOINT, split_axis=0, concat_axis=0, tiled=True)
    mine, got, sent = lax.optimization_barrier((mine, got, sent))
    mix, mix_t = call(
        mixing_body,
        [SMEM, VMEM, VMEM],
        [((K, 256, 384), BF16), ((K, 384, 256), BF16)],
        scratch=[pltpu.VMEM((K * 16, 384), F32)],
        nbytes=4 << 20,
    )(spot, mine, got)

    chunk = (LANES, CHUNK_MID + 16 * K, 128)
    mine, other = call(
        middle_body,
        [SMEM, VMEM, HBM, HBM, HBM],
        [(chunk, BF16), (chunk, BF16)],
        flops=2 << 30,
        nbytes=6 << 20,
        scratch=[
            pltpu.VMEM((256, 256), BF16),
            pltpu.VMEM((256, 256), F32),
            pltpu.VMEM((384, 256), F32),
            pltpu.VMEM((K, 256, 384), BF16),
            pltpu.VMEM((K, 384, 256), BF16),
            pltpu.VMEM((K, 256, 256), BF16),
            dma((K, 3)),
        ],
        vmem=32,
    )(spot, landed.reshape(HIN, 2, CHUNK_MID, 128), in_hbm(mix), in_hbm(mix_t), in_hbm(weights))
    got = swap_bands(other)
    (sent,) = call(merge_body, [SMEM, VMEM, VMEM], [((LANES, CHUNK_OUT, 128), BF16)], nbytes=2 << 20)(spot, mine, got)
    landed = lax.all_to_all(sent, "azimuth", split_axis=0, concat_axis=0, tiled=True)

    factors, sent = lax.optimization_barrier((factors, sent))
    tall, inv = call(
        table_body,
        [HBM] * 8,
        [((2, 768, 384), BF16), ((2, 384, 512), BF16)],
        nbytes=5 << 20,
        scratch=held + [dma((8,))],
    )(*[in_hbm(a) for a in factors])

    landed, tall, inv = lax.optimization_barrier((landed, tall, inv))

    def exchange(value, step):
        return value + lax.ppermute(value, "ens", [(i, i ^ step) for i in range(lax.axis_size("ens"))])

    half = jnp.sum(landed[:, 2 * CHUNK_MID :, :].astype(F32), axis=0)
    half = exchange(half, 1)
    half = exchange(half, 2)
    half = exchange(half, 4)
    far = swap_bands(half)
    (sent,) = call(fields_body, [VMEM] * 3, [((LANES, CHUNK_IN, 128), BF16)], flops=300 << 20)(landed, tall, inv)
    landed = lax.all_to_all(sent, "azimuth", split_axis=0, concat_axis=0, tiled=True)
    weight_grad = jnp.concatenate([jnp.where(low, half, far), jnp.where(low, far, half)], axis=1)
    field_grad, conv_out = call(
        unpack_body, [VMEM], [((8 * WPART, C), BF16), ((VPART, 4, C), BF16)], scratch=[pltpu.VMEM((192, C), F32)]
    )(landed)
    field_grad = jnp.swapaxes(field_grad.reshape(WPART, 8, C), 0, 1)
    return (jnp.swapaxes(conv_out, 0, 1)[None], field_grad[None], weight_grad.reshape(K, 16, C))


def solution(mesh):
    placed = (
        P("ens", "polar", "azimuth", None),
        P(None, "polar", None, None),
        P("polar", None),
        P(),
        P("ens", "polar", "azimuth", None),
    )
    return jax.shard_map(
        local,
        mesh=mesh,
        in_specs=placed,
        out_specs=(
            P("ens", "polar", "azimuth", None),
            P("ens", "polar", "azimuth", None),
            P(None, "azimuth", None),
        ),
        check_vma=False,
    )
```

```python
import math

import jax
import jax.numpy as jnp
import numpy as np
from jax import lax
from jax.experimental import pallas as pl
from jax.experimental.pallas import tpu as pltpu
from jax.sharding import PartitionSpec as P


WIN, WOUT, MODES = 1440, 720, 360
K, C, SUPPORT = 9, 256, 5
HOUT, HIN = 8, 16
LANES, BANDS = 16, 2
SHARES = LANES * BANDS
HALF = LANES // 2
M12, M16 = 12, 16
WPART, WROWS = 90, 96
VPART, VROWS = 45, 24
CHUNK_IN = WROWS + VROWS
CHUNK_MID = M16 + 2 * M12
CHUNK_OUT = 2 * CHUNK_MID + 16 * K
F32, BF16 = jnp.float32, jnp.bfloat16
JOINT = ("polar", "azimuth")


def factor_tables():
    def build(slots, part, steps, period, scale):
        mode_all, keep, imag = slots
        parts = []
        for e in range(BANDS):
            mode = mode_all + e
            ok = keep & (mode < MODES)
            alpha = 2 * math.pi * ((mode[None, :] * (part * np.arange(HALF)[:, None])) % period) / period
            beta = 2 * math.pi * ((mode[None, :] * steps[:, None]) % period) / period
            ok = ok[None, :] & (steps[:, None] < part)
            size = np.where(mode == 0, 1.0, 2.0)[None, :] / WIN if scale else 1.0
            parts.append(
                (
                    np.where(imag[None, :], -np.sin(alpha), np.cos(alpha)),
                    np.where(imag[None, :], -np.cos(alpha), -np.sin(alpha)),
                    np.where(ok, size * np.cos(beta), 0.0),
                    np.where(ok, size * np.sin(beta), 0.0),
                )
            )
        return [np.stack(group).astype(np.float32) for group in zip(*parts)]

    a, ri, i = np.meshgrid(np.arange(LANES), np.arange(2), np.arange(M12), indexing="ij")
    slots = ((2 * (M12 * a + i)).reshape(-1), np.ones(a.size, bool), ri.reshape(-1) == 1)
    wide = build(slots, WPART, np.arange(WROWS), WIN, False)
    ri, a, i = np.meshgrid(np.arange(2), np.arange(LANES), np.arange(M16), indexing="ij")
    slots = ((2 * (M12 * a + i)).reshape(-1), i.reshape(-1) < M12, ri.reshape(-1) == 1)
    narrow = build(slots, VPART, np.arange(2 * VROWS), WOUT, True)
    return wide, narrow


HBM = pl.BlockSpec(memory_space=pltpu.HBM)
VMEM = pl.BlockSpec(memory_space=pltpu.VMEM)
SMEM = pl.BlockSpec(memory_space=pltpu.SMEM)


def call(body, places, outs, flops=0, scratch=(), nbytes=1 << 20, vmem=16):
    return pl.pallas_call(
        body,
        out_shape=[jax.ShapeDtypeStruct(s, d) for s, d in outs],
        in_specs=places,
        out_specs=[VMEM] * len(outs),
        scratch_shapes=list(scratch),
        compiler_params=pltpu.CompilerParams(vmem_limit_bytes=vmem << 20),
        cost_estimate=pl.CostEstimate(flops=flops, bytes_accessed=nbytes, transcendentals=0),
    )


def in_hbm(value):
    return pltpu.with_memory_space_constraint(value, pltpu.HBM)


def fetch(sources, targets, sems):
    copies = [pltpu.make_async_copy(s, t, sems.at[n]) for n, (s, t) in enumerate(zip(sources, targets))]
    for copy in copies:
        copy.start()
    return copies


def low_half(shape):
    return lax.broadcasted_iota(jnp.int32, shape, len(shape) - 1) < 64


def swap64(value):
    return pltpu.roll(value, 64, value.ndim - 1)


def dot(a, b):
    return jnp.dot(a, b, preferred_element_type=F32)


def one_hot(shape, row_of_column):
    row = lax.broadcasted_iota(jnp.int32, shape, 0)
    column = lax.broadcasted_iota(jnp.int32, shape, 1)
    return jnp.where(row == row_of_column(column), 1.0, 0.0).astype(BF16)


def row_of_latitude(column):
    return 16 * (column % 8) + column // 8


def row_of_output(column):
    return 48 * (column % 4) + column // 4


def pack_body(f_hbm, g_hbm, o_ref, f_ref, g_ref, flat_ref, sems):
    copies = fetch((f_hbm, g_hbm), (f_ref, g_ref), sems)
    copies[0].wait()
    for j in range(6):
        count = min(128, 8 * WPART - 128 * j)
        order = one_hot((128, count), row_of_latitude)
        block = dot(order, f_ref[128 * j : 128 * j + count, :]).astype(BF16)
        for r in range(8):
            for h in range(2):
                piece = block[16 * r : 16 * (r + 1), 128 * h : 128 * (h + 1)]
                o_ref[2 * r + h, 16 * j : 16 * (j + 1), :] = piece
    copies[1].wait()
    for v in range(VPART):
        flat_ref[4 * v : 4 * (v + 1), :] = g_ref[v].astype(F32)
    flat_ref[4 * VPART : 192, :] = jnp.zeros((192 - 4 * VPART, C), F32)
    rows = dot(one_hot((192, 192), row_of_output), flat_ref[...].astype(BF16))
    keep = low_half((VROWS, 128))
    for o in range(4):
        for i in range(2):
            cols = slice(128 * i, 128 * (i + 1))
            top, bottom = rows[48 * o : 48 * o + 24, cols], rows[48 * o + 24 : 48 * o + 48, cols]
            even = jnp.where(keep, top, swap64(bottom))
            odd = jnp.where(keep, swap64(top), bottom)
            o_ref[4 * o + 2 * i, WROWS:CHUNK_IN, :] = even.astype(BF16)
            o_ref[4 * o + 2 * i + 1, WROWS:CHUNK_IN, :] = odd.astype(BF16)


def flip(source, target, rows, columns):
    for i in range(rows // 128):
        for j in range(columns // 128):
            piece = source[128 * i : 128 * (i + 1), 128 * j : 128 * (j + 1)].astype(F32)
            target[128 * j : 128 * (j + 1), 128 * i : 128 * (i + 1)] = piece.T.astype(BF16)


def fill_tables(w, v, w_ref, v_ref):
    for e in range(BANDS):
        for b in range(HALF):
            one, two = w[0][e, b : b + 1, :], w[1][e, b : b + 1, :]
            block = one * w[2][e] + two * w[3][e]
            w_ref[e, WROWS * b : WROWS * (b + 1), :] = block.astype(BF16)
            one, two = v[0][e, b : b + 1, :], v[1][e, b : b + 1, :]
            for part in range(2):
                rows = slice(VROWS * part, VROWS * (part + 1))
                block = one * v[2][e, rows, :] + two * v[3][e, rows, :]
                start = VROWS * (HALF * part + b)
                v_ref[e, start : start + VROWS, :] = block.astype(BF16)


def table_body(*refs):
    factors, (w_ref, v_ref) = refs[:8], refs[8:10]
    held, sems = refs[10:18], refs[18]
    for copy in fetch(factors, held, sems):
        copy.wait()
    fill_tables(held[:4], held[4:], w_ref, v_ref)


def flipped_table_body(*refs):
    factors, (wt_ref, vt_ref) = refs[:8], refs[8:10]
    held, (w_ref, v_ref, sems) = refs[10:18], refs[18:]
    for copy in fetch(factors, held, sems):
        copy.wait()
    fill_tables(held[:4], held[4:], w_ref, v_ref)
    for e in range(BANDS):
        flip(w_ref.at[e], wt_ref.at[e], HALF * WROWS, 2 * LANES * M12)
        flip(v_ref.at[e], vt_ref.at[e], 2 * HALF * VROWS, 2 * LANES * M16)


def spectra_body(r_ref, wt_ref, vt_ref, o_ref):
    left = r_ref[0:HALF, 0:WROWS, :].reshape(HALF * WROWS, 128).astype(F32)
    right = r_ref[HALF:LANES, 0:WROWS, :].reshape(HALF * WROWS, 128).astype(F32)
    g_left = r_ref[0:HALF, WROWS:CHUNK_IN, :].reshape(HALF * VROWS, 128).astype(F32)
    g_right = r_ref[HALF:LANES, WROWS:CHUNK_IN, :].reshape(HALF * VROWS, 128).astype(F32)
    keep = low_half((HALF * VROWS, 128))
    for e in range(BANDS):
        x = (left + right if e == 0 else left - right).astype(BF16)
        g = g_left + g_right if e == 0 else g_left - g_right
        turned = swap64(g)
        both = jnp.concatenate([jnp.where(keep, g, turned), jnp.where(keep, turned, g)], axis=0).astype(BF16)
        shares = slice(LANES * e, LANES * (e + 1))
        o_ref[shares, M16:CHUNK_MID, :] = dot(wt_ref[e], x).astype(BF16).reshape(LANES, 2 * M12, 128)
        got = dot(vt_ref[e], both)
        count = LANES * M16
        out = jnp.where(low_half((count, 128)), got[:count], got[count:])
        o_ref[shares, 0:M16, :] = out.astype(BF16).reshape(LANES, M16, 128)


def filter_body(spot_ref, support_ref, p_hbm, mine_ref, other_ref, p_ref, flat_ref, sems):
    (copy,) = fetch((p_hbm,), (p_ref,), sems)
    rows = K * SUPPORT * 4
    band, start = spot_ref[0, 0], 2 * M12 * spot_ref[0, 1]
    line = lax.broadcasted_iota(jnp.int32, (WOUT, 128), 0)
    slot = lax.broadcasted_iota(jnp.int32, (WOUT, 128), 1)
    place = slot % 64
    parity = jnp.where(slot < 64, band, 1 - band)
    mode = start + 2 * (place % M12) + parity
    hit = (line == mode + MODES * (place // M12)) & (place < 2 * M12) & (mode < MODES)
    chosen = jnp.where(hit, 1.0, 0.0).astype(BF16)
    row = lax.broadcasted_iota(jnp.int32, (rows, 128), 0)
    window, output = (row // 4) % SUPPORT, row % 4
    first = jnp.zeros((rows, 128), jnp.int32)
    last = jnp.zeros((rows, 128), jnp.int32)
    for o in range(4):
        first = jnp.where(output == o, support_ref[o, 0], first)
        last = jnp.where(output == o, support_ref[o, 1], last)
    copy.wait()
    for n in range(K * SUPPORT):
        flat_ref[4 * n : 4 * (n + 1), :] = p_ref[n].astype(F32)
    got = dot(flat_ref[0:rows, :].astype(BF16), chosen)
    got = jnp.where((window >= first) & (window <= last), got, 0.0)
    mine_ref[...] = got.astype(BF16)
    other_ref[...] = swap64(got).astype(BF16)


def mixing_body(spot_ref, mine_ref, got_ref, p_ref):
    rows, width, count = K * 16, HIN * 2 * M12, K * SUPPORT * 4
    low = spot_ref[0, 0] == 0
    mine, got = mine_ref[...].astype(F32), got_ref[...].astype(F32)
    halves = (jnp.where(low, mine, got).astype(BF16), jnp.where(low, got, mine).astype(BF16))
    x = lax.broadcasted_iota(jnp.int32, (128, width), 0)
    lane = lax.broadcasted_iota(jnp.int32, (128, width), 1)
    same, cross = lane % M12, lane % (2 * M12) < M12
    straight = x == same + jnp.where(cross, 0, M12)
    turned = x == same + jnp.where(cross, M12, 0)
    tiles = (
        jnp.where(straight, jnp.where(cross, 1.0, -1.0), 0.0).astype(BF16),
        jnp.where(turned, 1.0, 0.0).astype(BF16),
    )
    row = lax.broadcasted_iota(jnp.int32, (count, width), 0)
    lane = lax.broadcasted_iota(jnp.int32, (count, width), 1)
    reach = 2 * (row % 4) + (row // 4) % SUPPORT - 2 - lane // (2 * M12)
    target = lax.broadcasted_iota(jnp.int32, (rows, count), 0)
    source = lax.broadcasted_iota(jnp.int32, (rows, count), 1)
    key = target - 16 * (source // 20) - 2 * (source % 4)
    total = jnp.zeros((rows, width), F32)
    for half in range(2):
        for ri in range(2):
            spread = dot(halves[half], tiles[ri])
            spread = jnp.where(reach == -8 * half, spread, 0.0).astype(BF16)
            collect = jnp.where(key == 8 * half + ri, 1.0, 0.0).astype(BF16)
            total = total + dot(collect, spread)
    p_ref[...] = total


def row_of_share(column):
    return 16 * (column % 16) + column // 16


def middle_body(band_ref, r_ref, p_ref, w_hbm, mine_ref, other_ref, gs_ref, out_ref, sg_ref, w_ref, sems):
    copies = fetch([w_hbm.at[k] for k in range(K)], [w_ref.at[k] for k in range(K)], sems)
    keep = low_half((M16, 128))
    for o in range(HOUT):
        for i in range(2):
            first = r_ref[2 * o + i, 0, 0:M16, :].astype(F32)
            second = r_ref[2 * o + i, 1, 0:M16, :].astype(F32)
            cols = slice(128 * i, 128 * (i + 1))
            gs_ref[32 * o : 32 * o + 16, cols] = jnp.where(keep, first, swap64(second)).astype(BF16)
            gs_ref[32 * o + 16 : 32 * o + 32, cols] = jnp.where(keep, swap64(first), second).astype(BF16)
    used = M12 * 16
    gs = dot(one_hot((used, 256), row_of_share), gs_ref[...]).astype(BF16)
    width = HIN * 2 * M12
    x = jnp.concatenate(
        [r_ref[:, h, M16:CHUNK_MID, :].reshape(width, 128) for h in range(2)], axis=1
    )
    lane_mode = lax.broadcasted_iota(jnp.int32, (16, width), 1) % M12
    diagonal = (
        lax.broadcasted_iota(jnp.int32, (width, used), 0) % M12
        == lax.broadcasted_iota(jnp.int32, (width, used), 1) // 16
    )
    spread = one_hot((16, used), lambda column: column % 16)
    low = band_ref[0, 0] == 0

    for k in range(K):
        placed = p_ref[16 * k : 16 * (k + 1), :]
        blocks = [jnp.where(lane_mode == m, placed, 0.0).astype(BF16) for m in range(M12)]
        mixed = dot(jnp.concatenate(blocks, axis=0), x).astype(BF16)
        copies[k].wait()
        out_now = dot(mixed, w_ref[k])
        grad = lax.dot_general(mixed, gs, (((0,), (0,)), ((), ())), preferred_element_type=F32)
        where_to = (slice(None), slice(CHUNK_MID + 16 * k, CHUNK_MID + 16 * (k + 1)), slice(None))
        shape = (LANES, 16, 128)
        mine_ref[where_to] = jnp.where(low, grad[:, :128], grad[:, 128:]).astype(BF16).reshape(shape)
        other_ref[where_to] = jnp.where(low, grad[:, 128:], grad[:, :128]).astype(BF16).reshape(shape)
        back = lax.dot_general(gs, w_ref[k], (((1,), (1,)), ((), ())), preferred_element_type=F32)
        grown = lax.dot_general(
            placed.astype(BF16), spread, (((0,), (0,)), ((), ())), preferred_element_type=F32
        )
        sg_now = dot(jnp.where(diagonal, grown, 0.0).astype(BF16), back.astype(BF16))
        if k == 0:
            out_ref[...] = out_now
            sg_ref[...] = sg_now
        else:
            out_ref[...] += out_now
            sg_ref[...] += sg_now

    ordered = lax.dot_general(
        one_hot((used, 256), row_of_share),
        out_ref[...].astype(BF16),
        (((0,), (0,)), ((), ())),
        preferred_element_type=F32,
    )

    def output_rows(n):
        o, q = n // 4, n % 4
        cols = slice(128 * (q // 2), 128 * (q // 2 + 1))
        re = ordered[32 * o : 32 * o + 16, cols]
        im = ordered[32 * o + 16 : 32 * o + 32, cols]
        return jnp.where(keep, re, swap64(im)) if q % 2 == 0 else jnp.where(keep, swap64(re), im)

    def field_rows(n):
        r, h = n // 2, n % 2
        return sg_ref[24 * r : 24 * (r + 1), 128 * h : 128 * (h + 1)]

    for a in range(LANES):
        for rows, make in ((slice(0, M16), output_rows), (slice(M16, CHUNK_MID), field_rows)):
            first, second = make(a), make(a + LANES)
            mine_ref[a, rows, :] = jnp.where(low, first, second).astype(BF16)
            other_ref[a, rows, :] = jnp.where(low, second, first).astype(BF16)


def merge_body(band_ref, mine_ref, got_ref, o_ref):
    low = band_ref[0, 0] == 0
    for a in range(LANES):
        mine, got = mine_ref[a, 0:CHUNK_MID, :].astype(F32), got_ref[a, 0:CHUNK_MID, :].astype(F32)
        o_ref[a, 0:CHUNK_MID, :] = jnp.where(low, mine, got).astype(BF16)
        o_ref[a, CHUNK_MID : 2 * CHUNK_MID, :] = jnp.where(low, got, mine).astype(BF16)
        mine, got = mine_ref[a, CHUNK_MID:, :].astype(F32), got_ref[a, CHUNK_MID:, :].astype(F32)
        o_ref[a, 2 * CHUNK_MID :, :] = (mine + got).astype(BF16)


def fields_body(r_ref, w_ref, v_ref, o_ref):
    fields, outs = [], []
    for e in range(BANDS):
        start = CHUNK_MID * e
        sg = r_ref[:, start + M16 : start + CHUNK_MID, :].reshape(LANES * 2 * M12, 128)
        fields.append(dot(w_ref[e], sg))
        c = r_ref[:, start : start + M16, :].reshape(LANES * M16, 128).astype(F32)
        turned = swap64(c)
        keep = low_half(c.shape)
        both = jnp.concatenate([jnp.where(keep, c, turned), jnp.where(keep, turned, c)], axis=0).astype(BF16)
        got = dot(v_ref[e], both)
        count = HALF * VROWS
        outs.append(jnp.where(low_half((count, 128)), got[:count], got[count:]))
    for side in range(2):
        lanes = slice(HALF * side, HALF * (side + 1))
        field = fields[0] + fields[1] if side == 0 else fields[0] - fields[1]
        o_ref[lanes, 0:WROWS, :] = field.astype(BF16).reshape(HALF, WROWS, 128)
        out = outs[0] + outs[1] if side == 0 else outs[0] - outs[1]
        o_ref[lanes, WROWS:CHUNK_IN, :] = out.astype(BF16).reshape(HALF, VROWS, 128)


def unpack_body(r_ref, f_ref, c_ref, flat_ref):
    for j in range(6):
        count = min(128, 8 * WPART - 128 * j)
        halves = [
            jnp.concatenate([r_ref[2 * r + h, 16 * j : 16 * (j + 1), :] for r in range(8)], axis=0)
            for h in range(2)
        ]
        order = one_hot((128, count), row_of_latitude)
        block = lax.dot_general(
            order, jnp.concatenate(halves, axis=1), (((0,), (0,)), ((), ())), preferred_element_type=F32
        )
        f_ref[128 * j : 128 * j + count, :] = block.astype(BF16)
    keep = low_half((VROWS, 128))
    for o in range(4):
        for i in range(2):
            even = r_ref[4 * o + 2 * i, WROWS:CHUNK_IN, :].astype(F32)
            odd = r_ref[4 * o + 2 * i + 1, WROWS:CHUNK_IN, :].astype(F32)
            cols = slice(128 * i, 128 * (i + 1))
            flat_ref[48 * o : 48 * o + 24, cols] = jnp.where(keep, even, swap64(odd))
            flat_ref[48 * o + 24 : 48 * o + 48, cols] = jnp.where(keep, swap64(even), odd)
    rows = lax.dot_general(
        one_hot((192, 192), row_of_output),
        flat_ref[...].astype(BF16),
        (((0,), (0,)), ((), ())),
        preferred_element_type=F32,
    )
    for v in range(VPART):
        c_ref[v] = rows[4 * v : 4 * (v + 1), :].astype(BF16)


def swap_bands(value):
    return lax.ppermute(value, "polar", [(0, 1), (1, 0)])


def local(fields, basis_spectra, support, weights, out_grad):
    band = lax.axis_index("polar").astype(jnp.int32)
    low = band == 0
    spot = jnp.stack([band, lax.axis_index("azimuth").astype(jnp.int32)]).reshape(1, 2)
    wide, narrow = factor_tables()
    dma = pltpu.SemaphoreType.DMA
    (sent,) = call(
        pack_body,
        [HBM, HBM],
        [((LANES, CHUNK_IN, 128), BF16)],
        scratch=[
            pltpu.VMEM((8 * WPART, C), BF16),
            pltpu.VMEM((VPART, 4, C), BF16),
            pltpu.VMEM((192, C), F32),
            dma((2,)),
        ],
    )(
        in_hbm(jnp.swapaxes(fields[0], 0, 1).reshape(8 * WPART, C)), in_hbm(jnp.swapaxes(out_grad[0], 0, 1))
    )
    landed = lax.all_to_all(sent, "azimuth", split_axis=0, concat_axis=0, tiled=True)

    filters, limits, sent = lax.optimization_barrier((basis_spectra, support, sent))
    mine, other = call(
        filter_body,
        [SMEM, SMEM, HBM],
        [((K * SUPPORT * 4, 128), BF16)] * 2,
        scratch=[pltpu.VMEM((K * SUPPORT, 4, WOUT), BF16), pltpu.VMEM((184, WOUT), F32), dma((1,))],
    )(spot, limits, in_hbm(jnp.swapaxes(filters, 1, 2).reshape(K * SUPPORT, 4, WOUT)))
    got = swap_bands(other)
    factors = [a for a in wide + narrow]
    held = [pltpu.VMEM(a.shape, F32) for a in factors]
    factors, sent = lax.optimization_barrier(([jnp.asarray(a) for a in factors], sent))
    flat, inv_t = call(
        flipped_table_body,
        [HBM] * 8,
        [((2, 384, 768), BF16), ((2, 512, 384), BF16)],
        nbytes=5 << 20,
        scratch=held + [pltpu.VMEM((2, 768, 384), BF16), pltpu.VMEM((2, 384, 512), BF16), dma((8,))],
    )(*[in_hbm(a) for a in factors])

    landed, mine, got = lax.optimization_barrier((landed, mine, got))
    (sent,) = call(spectra_body, [VMEM] * 3, [((SHARES, CHUNK_MID, 128), BF16)], flops=300 << 20)(landed, flat, inv_t)
    landed = lax.all_to_all(sent, JOINT, split_axis=0, concat_axis=0, tiled=True)
    mine, got, sent = lax.optimization_barrier((mine, got, sent))
    (placed,) = call(mixing_body, [SMEM, VMEM, VMEM], [((K * 16, HIN * 2 * M12), F32)])(spot, mine, got)

    chunk = (LANES, CHUNK_MID + 16 * K, 128)
    mine, other = call(
        middle_body,
        [SMEM, VMEM, VMEM, HBM],
        [(chunk, BF16), (chunk, BF16)],
        flops=2 << 30,
        nbytes=3 << 20,
        scratch=[
            pltpu.VMEM((256, 256), BF16),
            pltpu.VMEM((192, 256), F32),
            pltpu.VMEM((384, 256), F32),
            pltpu.VMEM((K, 256, 256), BF16),
            dma((K,)),
        ],
    )(spot, landed.reshape(HIN, 2, CHUNK_MID, 128), placed, in_hbm(weights))
    got = swap_bands(other)
    (sent,) = call(merge_body, [SMEM, VMEM, VMEM], [((LANES, CHUNK_OUT, 128), BF16)], nbytes=2 << 20)(spot, mine, got)
    landed = lax.all_to_all(sent, "azimuth", split_axis=0, concat_axis=0, tiled=True)

    factors, sent = lax.optimization_barrier((factors, sent))
    tall, inv = call(
        table_body,
        [HBM] * 8,
        [((2, 768, 384), BF16), ((2, 384, 512), BF16)],
        nbytes=5 << 20,
        scratch=held + [dma((8,))],
    )(*[in_hbm(a) for a in factors])

    landed, tall, inv = lax.optimization_barrier((landed, tall, inv))

    members = lax.axis_size("ens")

    def partner(value, member_bit, band_bit):
        pairs = [(i, i ^ (2 * member_bit + band_bit)) for i in range(2 * members)]
        return lax.ppermute(value, ("ens", "polar"), pairs)

    half = jnp.sum(landed[:, 2 * CHUNK_MID :, :].astype(F32), axis=0)
    half = half + partner(half, 4, 0)
    half = half + partner(half, 2, 0)
    far = partner(half, 1, 1)
    near = partner(half, 1, 0)
    far = far + partner(half, 0, 1)
    half = half + near
    (sent,) = call(fields_body, [VMEM] * 3, [((LANES, CHUNK_IN, 128), BF16)], flops=300 << 20)(landed, tall, inv)
    landed = lax.all_to_all(sent, "azimuth", split_axis=0, concat_axis=0, tiled=True)
    weight_grad = jnp.concatenate([jnp.where(low, half, far), jnp.where(low, far, half)], axis=1)
    field_grad, conv_out = call(
        unpack_body, [VMEM], [((8 * WPART, C), BF16), ((VPART, 4, C), BF16)], scratch=[pltpu.VMEM((192, C), F32)]
    )(landed)
    field_grad = jnp.swapaxes(field_grad.reshape(WPART, 8, C), 0, 1)
    return (jnp.swapaxes(conv_out, 0, 1)[None], field_grad[None], weight_grad.reshape(K, 16, C))


def solution(mesh):
    placed = (
        P("ens", "polar", "azimuth", None),
        P(None, "polar", None, None),
        P("polar", None),
        P(),
        P("ens", "polar", "azimuth", None),
    )
    return jax.shard_map(
        local,
        mesh=mesh,
        in_specs=placed,
        out_specs=(
            P("ens", "polar", "azimuth", None),
            P("ens", "polar", "azimuth", None),
            P(None, "azimuth", None),
        ),
        check_vma=False,
    )
```

```python
import math

import jax
import jax.numpy as jnp
import numpy as np
from jax import lax
from jax.experimental import pallas as pl
from jax.experimental.pallas import tpu as pltpu
from jax.sharding import PartitionSpec as P


WIN, WOUT, MODES = 1440, 720, 360
K, C, SUPPORT = 9, 256, 5
HOUT, HIN = 8, 16
LANES, BANDS = 16, 2
SHARES = LANES * BANDS
HALF = LANES // 2
M12, M16 = 12, 16
WPART, WROWS = 90, 96
VPART, VROWS = 45, 24
CHUNK_IN = WROWS + VROWS
CHUNK_MID = M16 + 2 * M12
CHUNK_OUT = 2 * CHUNK_MID + 16 * K
F32, BF16 = jnp.float32, jnp.bfloat16
JOINT = ("polar", "azimuth")


def factor_tables():
    def build(slots, part, steps, period, scale):
        mode_all, keep, imag = slots
        parts = []
        for e in range(BANDS):
            mode = mode_all + e
            ok = keep & (mode < MODES)
            alpha = 2 * math.pi * ((mode[None, :] * (part * np.arange(HALF)[:, None])) % period) / period
            beta = 2 * math.pi * ((mode[None, :] * steps[:, None]) % period) / period
            ok = ok[None, :] & (steps[:, None] < part)
            size = np.where(mode == 0, 1.0, 2.0)[None, :] / WIN if scale else 1.0
            parts.append(
                (
                    np.where(imag[None, :], -np.sin(alpha), np.cos(alpha)),
                    np.where(imag[None, :], -np.cos(alpha), -np.sin(alpha)),
                    np.where(ok, size * np.cos(beta), 0.0),
                    np.where(ok, size * np.sin(beta), 0.0),
                )
            )
        return [np.stack(group).astype(np.float32) for group in zip(*parts)]

    a, ri, i = np.meshgrid(np.arange(LANES), np.arange(2), np.arange(M12), indexing="ij")
    slots = ((2 * (M12 * a + i)).reshape(-1), np.ones(a.size, bool), ri.reshape(-1) == 1)
    wide = build(slots, WPART, np.arange(WROWS), WIN, False)
    ri, a, i = np.meshgrid(np.arange(2), np.arange(LANES), np.arange(M16), indexing="ij")
    slots = ((2 * (M12 * a + i)).reshape(-1), i.reshape(-1) < M12, ri.reshape(-1) == 1)
    narrow = build(slots, VPART, np.arange(2 * VROWS), WOUT, True)
    return wide, narrow


HBM = pl.BlockSpec(memory_space=pltpu.HBM)
VMEM = pl.BlockSpec(memory_space=pltpu.VMEM)
SMEM = pl.BlockSpec(memory_space=pltpu.SMEM)


def call(body, places, outs, flops=0, scratch=(), nbytes=1 << 20, vmem=16, out_place=VMEM):
    return pl.pallas_call(
        body,
        out_shape=[jax.ShapeDtypeStruct(s, d) for s, d in outs],
        in_specs=places,
        out_specs=[out_place] * len(outs),
        scratch_shapes=list(scratch),
        compiler_params=pltpu.CompilerParams(vmem_limit_bytes=vmem << 20),
        cost_estimate=pl.CostEstimate(flops=flops, bytes_accessed=nbytes, transcendentals=0),
    )


def in_hbm(value):
    return pltpu.with_memory_space_constraint(value, pltpu.HBM)


def fetch(sources, targets, sems):
    copies = [pltpu.make_async_copy(s, t, sems.at[n]) for n, (s, t) in enumerate(zip(sources, targets))]
    for copy in copies:
        copy.start()
    return copies


def low_half(shape):
    return lax.broadcasted_iota(jnp.int32, shape, len(shape) - 1) < 64


def swap64(value):
    return pltpu.roll(value, 64, value.ndim - 1)


def dot(a, b):
    return jnp.dot(a, b, preferred_element_type=F32)


def one_hot(shape, row_of_column):
    row = lax.broadcasted_iota(jnp.int32, shape, 0)
    column = lax.broadcasted_iota(jnp.int32, shape, 1)
    return jnp.where(row == row_of_column(column), 1.0, 0.0).astype(BF16)


def row_of_latitude(column):
    return 16 * (column % 8) + column // 8


def row_of_output(column):
    return 48 * (column % 4) + column // 4


def pack_body(f_hbm, g_hbm, o_ref, f_ref, g_ref, flat_ref, sems):
    copies = fetch((f_hbm, g_hbm), (f_ref, g_ref), sems)
    copies[0].wait()
    for j in range(6):
        count = min(128, 8 * WPART - 128 * j)
        order = one_hot((128, count), row_of_latitude)
        block = dot(order, f_ref[128 * j : 128 * j + count, :]).astype(BF16)
        for r in range(8):
            for h in range(2):
                piece = block[16 * r : 16 * (r + 1), 128 * h : 128 * (h + 1)]
                o_ref[2 * r + h, 16 * j : 16 * (j + 1), :] = piece
    copies[1].wait()
    for v in range(VPART):
        flat_ref[4 * v : 4 * (v + 1), :] = g_ref[v].astype(F32)
    flat_ref[4 * VPART : 192, :] = jnp.zeros((192 - 4 * VPART, C), F32)
    rows = dot(one_hot((192, 192), row_of_output), flat_ref[...].astype(BF16))
    keep = low_half((VROWS, 128))
    for o in range(4):
        for i in range(2):
            cols = slice(128 * i, 128 * (i + 1))
            top, bottom = rows[48 * o : 48 * o + 24, cols], rows[48 * o + 24 : 48 * o + 48, cols]
            even = jnp.where(keep, top, swap64(bottom))
            odd = jnp.where(keep, swap64(top), bottom)
            o_ref[4 * o + 2 * i, WROWS:CHUNK_IN, :] = even.astype(BF16)
            o_ref[4 * o + 2 * i + 1, WROWS:CHUNK_IN, :] = odd.astype(BF16)


def flip(source, target, rows, columns):
    for i in range(rows // 128):
        for j in range(columns // 128):
            piece = source[128 * i : 128 * (i + 1), 128 * j : 128 * (j + 1)].astype(F32)
            target[128 * j : 128 * (j + 1), 128 * i : 128 * (i + 1)] = piece.T.astype(BF16)


def fill_tables(w, v, w_ref, v_ref):
    for e in range(BANDS):
        for b in range(HALF):
            one, two = w[0][e, b : b + 1, :], w[1][e, b : b + 1, :]
            block = one * w[2][e] + two * w[3][e]
            w_ref[e, WROWS * b : WROWS * (b + 1), :] = block.astype(BF16)
            one, two = v[0][e, b : b + 1, :], v[1][e, b : b + 1, :]
            for part in range(2):
                rows = slice(VROWS * part, VROWS * (part + 1))
                block = one * v[2][e, rows, :] + two * v[3][e, rows, :]
                start = VROWS * (HALF * part + b)
                v_ref[e, start : start + VROWS, :] = block.astype(BF16)


def table_body(*refs):
    factors, (w_ref, v_ref) = refs[:8], refs[8:10]
    held, sems = refs[10:18], refs[18]
    for copy in fetch(factors, held, sems):
        copy.wait()
    fill_tables(held[:4], held[4:], w_ref, v_ref)


def flipped_table_body(*refs):
    factors, (wt_ref, vt_ref) = refs[:8], refs[8:10]
    held, (w_ref, v_ref, sems) = refs[10:18], refs[18:]
    for copy in fetch(factors, held, sems):
        copy.wait()
    fill_tables(held[:4], held[4:], w_ref, v_ref)
    for e in range(BANDS):
        flip(w_ref.at[e], wt_ref.at[e], HALF * WROWS, 2 * LANES * M12)
        flip(v_ref.at[e], vt_ref.at[e], 2 * HALF * VROWS, 2 * LANES * M16)


def spectra_body(r_ref, wt_ref, vt_ref, o_ref):
    left = r_ref[0:HALF, 0:WROWS, :].reshape(HALF * WROWS, 128).astype(F32)
    right = r_ref[HALF:LANES, 0:WROWS, :].reshape(HALF * WROWS, 128).astype(F32)
    g_left = r_ref[0:HALF, WROWS:CHUNK_IN, :].reshape(HALF * VROWS, 128).astype(F32)
    g_right = r_ref[HALF:LANES, WROWS:CHUNK_IN, :].reshape(HALF * VROWS, 128).astype(F32)
    keep = low_half((HALF * VROWS, 128))
    for e in range(BANDS):
        x = (left + right if e == 0 else left - right).astype(BF16)
        g = g_left + g_right if e == 0 else g_left - g_right
        turned = swap64(g)
        both = jnp.concatenate([jnp.where(keep, g, turned), jnp.where(keep, turned, g)], axis=0).astype(BF16)
        shares = slice(LANES * e, LANES * (e + 1))
        o_ref[shares, M16:CHUNK_MID, :] = dot(wt_ref[e], x).astype(BF16).reshape(LANES, 2 * M12, 128)
        got = dot(vt_ref[e], both)
        count = LANES * M16
        out = jnp.where(low_half((count, 128)), got[:count], got[count:])
        o_ref[shares, 0:M16, :] = out.astype(BF16).reshape(LANES, M16, 128)


def filter_body(spot_ref, support_ref, p_hbm, mine_ref, other_ref, p_ref, flat_ref, sems):
    (copy,) = fetch((p_hbm,), (p_ref,), sems)
    rows = K * SUPPORT * 4
    band, start = spot_ref[0, 0], 2 * M12 * spot_ref[0, 1]
    line = lax.broadcasted_iota(jnp.int32, (WOUT, 128), 0)
    slot = lax.broadcasted_iota(jnp.int32, (WOUT, 128), 1)
    place = slot % 64
    parity = jnp.where(slot < 64, band, 1 - band)
    mode = start + 2 * (place % M12) + parity
    hit = (line == mode + MODES * (place // M12)) & (place < 2 * M12) & (mode < MODES)
    chosen = jnp.where(hit, 1.0, 0.0).astype(BF16)
    row = lax.broadcasted_iota(jnp.int32, (rows, 128), 0)
    window, output = (row // 4) % SUPPORT, row % 4
    first = jnp.zeros((rows, 128), jnp.int32)
    last = jnp.zeros((rows, 128), jnp.int32)
    for o in range(4):
        first = jnp.where(output == o, support_ref[o, 0], first)
        last = jnp.where(output == o, support_ref[o, 1], last)
    copy.wait()
    for n in range(K * SUPPORT):
        flat_ref[4 * n : 4 * (n + 1), :] = p_ref[n].astype(F32)
    got = dot(flat_ref[0:rows, :].astype(BF16), chosen)
    got = jnp.where((window >= first) & (window <= last), got, 0.0)
    mine_ref[...] = got.astype(BF16)
    other_ref[...] = swap64(got).astype(BF16)


def mixing_body(spot_ref, mine_ref, got_ref, p_ref, at_ref):
    rows, width, count = K * 16, HIN * 2 * M12, K * SUPPORT * 4
    low = spot_ref[0, 0] == 0
    mine, got = mine_ref[...].astype(F32), got_ref[...].astype(F32)
    halves = (jnp.where(low, mine, got).astype(BF16), jnp.where(low, got, mine).astype(BF16))
    x = lax.broadcasted_iota(jnp.int32, (128, width), 0)
    lane = lax.broadcasted_iota(jnp.int32, (128, width), 1)
    same, cross = lane % M12, lane % (2 * M12) < M12
    straight = x == same + jnp.where(cross, 0, M12)
    turned = x == same + jnp.where(cross, M12, 0)
    tiles = (
        jnp.where(straight, jnp.where(cross, 1.0, -1.0), 0.0).astype(BF16),
        jnp.where(turned, 1.0, 0.0).astype(BF16),
    )
    row = lax.broadcasted_iota(jnp.int32, (count, width), 0)
    lane = lax.broadcasted_iota(jnp.int32, (count, width), 1)
    reach = 2 * (row % 4) + (row // 4) % SUPPORT - 2 - lane // (2 * M12)
    target = lax.broadcasted_iota(jnp.int32, (rows, count), 0)
    source = lax.broadcasted_iota(jnp.int32, (rows, count), 1)
    key = target - 16 * (source // 20) - 2 * (source % 4)
    total = jnp.zeros((rows, width), F32)
    for half in range(2):
        for ri in range(2):
            spread = dot(halves[half], tiles[ri])
            spread = jnp.where(reach == -8 * half, spread, 0.0).astype(BF16)
            collect = jnp.where(key == 8 * half + ri, 1.0, 0.0).astype(BF16)
            total = total + dot(collect, spread)
    p_ref[...] = total
    used = 16 * M12
    for k in range(0, K, 2):
        pair = min(2, K - k)
        row = lax.broadcasted_iota(jnp.int32, (16 * pair, used * pair), 0)
        column = lax.broadcasted_iota(jnp.int32, (16 * pair, used * pair), 1)
        spread = jnp.where(row == 16 * (column // used) + column % 16, 1.0, 0.0).astype(BF16)
        row = lax.broadcasted_iota(jnp.int32, (width, used * pair), 0) % M12
        column = (lax.broadcasted_iota(jnp.int32, (width, used * pair), 1) // 16) % M12
        grown = lax.dot_general(
            p_ref[16 * k : 16 * (k + pair), :].astype(BF16),
            spread,
            (((0,), (0,)), ((), ())),
            preferred_element_type=F32,
        )
        at_ref[:, used * k : used * (k + pair)] = jnp.where(row == column, grown, 0.0).astype(BF16)


def row_of_share(column):
    return 16 * (column % 16) + column // 16


def middle_body(
    band_ref, r_ref, p_ref, at_ref, w_hbm, mine_ref, other_ref, gs_ref, sg_ref, w_ref, mixed_ref, back_ref, sems
):
    copies = fetch([w_hbm.at[k] for k in range(K)], [w_ref.at[k] for k in range(K)], sems)
    keep = low_half((M16, 128))
    for o in range(HOUT):
        for i in range(2):
            first = r_ref[2 * o + i, 0, 0:M16, :].astype(F32)
            second = r_ref[2 * o + i, 1, 0:M16, :].astype(F32)
            cols = slice(128 * i, 128 * (i + 1))
            gs_ref[32 * o : 32 * o + 16, cols] = jnp.where(keep, first, swap64(second)).astype(BF16)
            gs_ref[32 * o + 16 : 32 * o + 32, cols] = jnp.where(keep, swap64(first), second).astype(BF16)
    used = M12 * 16
    gs = dot(one_hot((used, 256), row_of_share), gs_ref[...]).astype(BF16)
    width = HIN * 2 * M12
    x = jnp.concatenate(
        [r_ref[:, h, M16:CHUNK_MID, :].reshape(width, 128) for h in range(2)], axis=1
    )
    lane_mode = lax.broadcasted_iota(jnp.int32, (16, width), 1) % M12
    low = band_ref[0, 0] == 0

    for k in range(K):
        placed = p_ref[16 * k : 16 * (k + 1), :]
        blocks = [jnp.where(lane_mode == m, placed, 0.0).astype(BF16) for m in range(M12)]
        mixed = dot(jnp.concatenate(blocks, axis=0), x).astype(BF16)
        mixed_ref[:, C * k : C * (k + 1)] = mixed
        grad = lax.dot_general(mixed, gs, (((0,), (0,)), ((), ())), preferred_element_type=F32)
        where_to = (slice(None), slice(CHUNK_MID + 16 * k, CHUNK_MID + 16 * (k + 1)), slice(None))
        shape = (LANES, 16, 128)
        mine_ref[where_to] = jnp.where(low, grad[:, :128], grad[:, 128:]).astype(BF16).reshape(shape)
        other_ref[where_to] = jnp.where(low, grad[:, 128:], grad[:, :128]).astype(BF16).reshape(shape)
        copies[k].wait()
        back = lax.dot_general(gs, w_ref[k], (((1,), (1,)), ((), ())), preferred_element_type=F32)
        back_ref[used * k : used * (k + 1), :] = back.astype(BF16)
    out = dot(mixed_ref[...], w_ref[...].reshape(K * C, C)).astype(BF16)
    sg_ref[...] = dot(at_ref[...], back_ref[...])
    ordered = lax.dot_general(
        one_hot((used, 256), row_of_share),
        out,
        (((0,), (0,)), ((), ())),
        preferred_element_type=F32,
    )

    def output_rows(n):
        o, q = n // 4, n % 4
        cols = slice(128 * (q // 2), 128 * (q // 2 + 1))
        re = ordered[32 * o : 32 * o + 16, cols]
        im = ordered[32 * o + 16 : 32 * o + 32, cols]
        return jnp.where(keep, re, swap64(im)) if q % 2 == 0 else jnp.where(keep, swap64(re), im)

    def field_rows(n):
        r, h = n // 2, n % 2
        return sg_ref[24 * r : 24 * (r + 1), 128 * h : 128 * (h + 1)]

    for a in range(LANES):
        for rows, make in ((slice(0, M16), output_rows), (slice(M16, CHUNK_MID), field_rows)):
            first, second = make(a), make(a + LANES)
            mine_ref[a, rows, :] = jnp.where(low, first, second).astype(BF16)
            other_ref[a, rows, :] = jnp.where(low, second, first).astype(BF16)


def merge_body(band_ref, mine_ref, got_ref, o_hbm, o_ref, sems):
    low = band_ref[0, 0] == 0
    copies = []
    for a in range(LANES):
        mine, got = mine_ref[a, 0:CHUNK_MID, :].astype(F32), got_ref[a, 0:CHUNK_MID, :].astype(F32)
        o_ref[a, 0:CHUNK_MID, :] = jnp.where(low, mine, got).astype(BF16)
        o_ref[a, CHUNK_MID : 2 * CHUNK_MID, :] = jnp.where(low, got, mine).astype(BF16)
        mine, got = mine_ref[a, CHUNK_MID:, :].astype(F32), got_ref[a, CHUNK_MID:, :].astype(F32)
        o_ref[a, 2 * CHUNK_MID :, :] = (mine + got).astype(BF16)
        if a % 4 == 3:
            part = slice(a - 3, a + 1)
            copies.append(pltpu.make_async_copy(o_ref.at[part], o_hbm.at[part], sems.at[a // 4]))
            copies[-1].start()
    for copy in copies:
        copy.wait()


def fields_body(r_ref, w_ref, v_ref, o_ref):
    fields, outs = [], []
    for e in range(BANDS):
        start = CHUNK_MID * e
        sg = r_ref[:, start + M16 : start + CHUNK_MID, :].reshape(LANES * 2 * M12, 128)
        fields.append(dot(w_ref[e], sg))
        c = r_ref[:, start : start + M16, :].reshape(LANES * M16, 128).astype(F32)
        turned = swap64(c)
        keep = low_half(c.shape)
        both = jnp.concatenate([jnp.where(keep, c, turned), jnp.where(keep, turned, c)], axis=0).astype(BF16)
        got = dot(v_ref[e], both)
        count = HALF * VROWS
        outs.append(jnp.where(low_half((count, 128)), got[:count], got[count:]))
    for side in range(2):
        lanes = slice(HALF * side, HALF * (side + 1))
        field = fields[0] + fields[1] if side == 0 else fields[0] - fields[1]
        o_ref[lanes, 0:WROWS, :] = field.astype(BF16).reshape(HALF, WROWS, 128)
        out = outs[0] + outs[1] if side == 0 else outs[0] - outs[1]
        o_ref[lanes, WROWS:CHUNK_IN, :] = out.astype(BF16).reshape(HALF, VROWS, 128)


def unpack_body(r_ref, f_ref, c_ref, flat_ref):
    for j in range(6):
        count = min(128, 8 * WPART - 128 * j)
        halves = [
            jnp.concatenate([r_ref[2 * r + h, 16 * j : 16 * (j + 1), :] for r in range(8)], axis=0)
            for h in range(2)
        ]
        order = one_hot((128, count), row_of_latitude)
        block = lax.dot_general(
            order, jnp.concatenate(halves, axis=1), (((0,), (0,)), ((), ())), preferred_element_type=F32
        )
        f_ref[128 * j : 128 * j + count, :] = block.astype(BF16)
    keep = low_half((VROWS, 128))
    for o in range(4):
        for i in range(2):
            even = r_ref[4 * o + 2 * i, WROWS:CHUNK_IN, :].astype(F32)
            odd = r_ref[4 * o + 2 * i + 1, WROWS:CHUNK_IN, :].astype(F32)
            cols = slice(128 * i, 128 * (i + 1))
            flat_ref[48 * o : 48 * o + 24, cols] = jnp.where(keep, even, swap64(odd))
            flat_ref[48 * o + 24 : 48 * o + 48, cols] = jnp.where(keep, swap64(even), odd)
    rows = lax.dot_general(
        one_hot((192, 192), row_of_output),
        flat_ref[...].astype(BF16),
        (((0,), (0,)), ((), ())),
        preferred_element_type=F32,
    )
    for v in range(VPART):
        c_ref[v] = rows[4 * v : 4 * (v + 1), :].astype(BF16)


def swap_bands(value):
    return lax.ppermute(value, "polar", [(0, 1), (1, 0)])


def local(fields, basis_spectra, support, weights, out_grad):
    band = lax.axis_index("polar").astype(jnp.int32)
    low = band == 0
    spot = jnp.stack([band, lax.axis_index("azimuth").astype(jnp.int32)]).reshape(1, 2)
    wide, narrow = factor_tables()
    dma = pltpu.SemaphoreType.DMA
    (sent,) = call(
        pack_body,
        [HBM, HBM],
        [((LANES, CHUNK_IN, 128), BF16)],
        scratch=[
            pltpu.VMEM((8 * WPART, C), BF16),
            pltpu.VMEM((VPART, 4, C), BF16),
            pltpu.VMEM((192, C), F32),
            dma((2,)),
        ],
    )(
        in_hbm(jnp.swapaxes(fields[0], 0, 1).reshape(8 * WPART, C)), in_hbm(jnp.swapaxes(out_grad[0], 0, 1))
    )
    landed = lax.all_to_all(sent, "azimuth", split_axis=0, concat_axis=0, tiled=True)

    filters, limits, sent = lax.optimization_barrier((basis_spectra, support, sent))
    mine, other = call(
        filter_body,
        [SMEM, SMEM, HBM],
        [((K * SUPPORT * 4, 128), BF16)] * 2,
        scratch=[pltpu.VMEM((K * SUPPORT, 4, WOUT), BF16), pltpu.VMEM((184, WOUT), F32), dma((1,))],
    )(spot, limits, in_hbm(jnp.swapaxes(filters, 1, 2).reshape(K * SUPPORT, 4, WOUT)))
    got = swap_bands(other)
    factors = [a for a in wide + narrow]
    held = [pltpu.VMEM(a.shape, F32) for a in factors]
    factors, sent = lax.optimization_barrier(([jnp.asarray(a) for a in factors], sent))
    flat, inv_t = call(
        flipped_table_body,
        [HBM] * 8,
        [((2, 384, 768), BF16), ((2, 512, 384), BF16)],
        nbytes=5 << 20,
        scratch=held + [pltpu.VMEM((2, 768, 384), BF16), pltpu.VMEM((2, 384, 512), BF16), dma((8,))],
    )(*[in_hbm(a) for a in factors])

    landed, mine, got = lax.optimization_barrier((landed, mine, got))
    (sent,) = call(spectra_body, [VMEM] * 3, [((SHARES, CHUNK_MID, 128), BF16)], flops=300 << 20)(landed, flat, inv_t)
    landed = lax.all_to_all(sent, JOINT, split_axis=0, concat_axis=0, tiled=True)
    mine, got, sent = lax.optimization_barrier((mine, got, sent))
    placed, mix_t = call(
        mixing_body, [SMEM, VMEM, VMEM], [((K * 16, HIN * 2 * M12), F32), ((HIN * 2 * M12, K * 192), BF16)]
    )(spot, mine, got)

    chunk = (LANES, CHUNK_MID + 16 * K, 128)
    mine, other = call(
        middle_body,
        [SMEM, VMEM, VMEM, VMEM, HBM],
        [(chunk, BF16), (chunk, BF16)],
        flops=2 << 30,
        nbytes=3 << 20,
        scratch=[
            pltpu.VMEM((256, 256), BF16),
            pltpu.VMEM((384, 256), F32),
            pltpu.VMEM((K, 256, 256), BF16),
            pltpu.VMEM((192, K * C), BF16),
            pltpu.VMEM((K * 192, 256), BF16),
            dma((K,)),
        ],
    )(spot, landed.reshape(HIN, 2, CHUNK_MID, 128), placed, mix_t, in_hbm(weights))
    got = swap_bands(other)
    (sent,) = call(
        merge_body,
        [SMEM, VMEM, VMEM],
        [((LANES, CHUNK_OUT, 128), BF16)],
        nbytes=2 << 20,
        scratch=[pltpu.VMEM((LANES, CHUNK_OUT, 128), BF16), dma((4,))],
        out_place=HBM,
    )(spot, mine, got)
    landed = lax.all_to_all(sent, "azimuth", split_axis=0, concat_axis=0, tiled=True)

    factors, sent = lax.optimization_barrier((factors, sent))
    tall, inv = call(
        table_body,
        [HBM] * 8,
        [((2, 768, 384), BF16), ((2, 384, 512), BF16)],
        nbytes=5 << 20,
        scratch=held + [dma((8,))],
    )(*[in_hbm(a) for a in factors])

    landed, tall, inv = lax.optimization_barrier((landed, tall, inv))

    members = lax.axis_size("ens")

    def partner(value, member_bit, band_bit):
        pairs = [(i, i ^ (2 * member_bit + band_bit)) for i in range(2 * members)]
        return lax.ppermute(value, ("ens", "polar"), pairs)

    half = jnp.sum(landed[:, 2 * CHUNK_MID :, :].astype(F32), axis=0).astype(BF16)
    got = partner(half, 1, 0)
    half = (half.astype(F32) + got.astype(F32)).astype(BF16)
    got = partner(half, 4, 0)
    half = (half.astype(F32) + got.astype(F32)).astype(BF16)
    cross = partner(half, 2, 1)
    near = partner(half, 2, 0)
    far = partner(half, 0, 1)
    far = far.astype(F32) + cross.astype(F32)
    half = half.astype(F32) + near.astype(F32)
    (sent,) = call(fields_body, [VMEM] * 3, [((LANES, CHUNK_IN, 128), BF16)], flops=300 << 20)(landed, tall, inv)
    landed = lax.all_to_all(sent, "azimuth", split_axis=0, concat_axis=0, tiled=True)
    weight_grad = jnp.concatenate([jnp.where(low, half, far), jnp.where(low, far, half)], axis=1)
    field_grad, conv_out = call(
        unpack_body, [VMEM], [((8 * WPART, C), BF16), ((VPART, 4, C), BF16)], scratch=[pltpu.VMEM((192, C), F32)]
    )(landed)
    field_grad = jnp.swapaxes(field_grad.reshape(WPART, 8, C), 0, 1)
    return (jnp.swapaxes(conv_out, 0, 1)[None], field_grad[None], weight_grad.reshape(K, 16, C))


def solution(mesh):
    placed = (
        P("ens", "polar", "azimuth", None),
        P(None, "polar", None, None),
        P("polar", None),
        P(),
        P("ens", "polar", "azimuth", None),
    )
    return jax.shard_map(
        local,
        mesh=mesh,
        in_specs=placed,
        out_specs=(
            P("ens", "polar", "azimuth", None),
            P("ens", "polar", "azimuth", None),
            P(None, "azimuth", None),
        ),
        check_vma=False,
    )
```

```python
import math

import jax
import jax.numpy as jnp
import numpy as np
from jax import lax
from jax.experimental import pallas as pl
from jax.experimental.pallas import tpu as pltpu
from jax.sharding import PartitionSpec as P


WIN, WOUT, MODES = 1440, 720, 360
K, C, SUPPORT = 9, 256, 5
HOUT, HIN = 8, 16
LANES, BANDS = 16, 2
SHARES = LANES * BANDS
HALF = LANES // 2
M12, M16 = 12, 16
WPART, WROWS = 90, 96
VPART, VROWS = 45, 24
CHUNK_IN = WROWS + VROWS
CHUNK_MID = M16 + 2 * M12
CHUNK_OUT = 2 * CHUNK_MID + 16 * K
F32, BF16 = jnp.float32, jnp.bfloat16
JOINT = ("polar", "azimuth")


def factor_tables():
    def build(slots, part, steps, period, scale):
        mode_all, keep, imag = slots
        parts = []
        for e in range(BANDS):
            mode = mode_all + e
            ok = keep & (mode < MODES)
            alpha = 2 * math.pi * ((mode[None, :] * (part * np.arange(HALF)[:, None])) % period) / period
            beta = 2 * math.pi * ((mode[None, :] * steps[:, None]) % period) / period
            ok = ok[None, :] & (steps[:, None] < part)
            size = np.where(mode == 0, 1.0, 2.0)[None, :] / WIN if scale else 1.0
            parts.append(
                (
                    np.where(imag[None, :], -np.sin(alpha), np.cos(alpha)),
                    np.where(imag[None, :], -np.cos(alpha), -np.sin(alpha)),
                    np.where(ok, size * np.cos(beta), 0.0),
                    np.where(ok, size * np.sin(beta), 0.0),
                )
            )
        return [np.stack(group).astype(np.float32) for group in zip(*parts)]

    a, ri, i = np.meshgrid(np.arange(LANES), np.arange(2), np.arange(M12), indexing="ij")
    slots = ((2 * (M12 * a + i)).reshape(-1), np.ones(a.size, bool), ri.reshape(-1) == 1)
    wide = build(slots, WPART, np.arange(WROWS), WIN, False)
    ri, a, i = np.meshgrid(np.arange(2), np.arange(LANES), np.arange(M16), indexing="ij")
    slots = ((2 * (M12 * a + i)).reshape(-1), i.reshape(-1) < M12, ri.reshape(-1) == 1)
    narrow = build(slots, VPART, np.arange(2 * VROWS), WOUT, True)
    return wide, narrow


HBM = pl.BlockSpec(memory_space=pltpu.HBM)
VMEM = pl.BlockSpec(memory_space=pltpu.VMEM)
SMEM = pl.BlockSpec(memory_space=pltpu.SMEM)


def call(body, places, outs, flops=0, scratch=(), nbytes=1 << 20, vmem=16, out_place=VMEM):
    return pl.pallas_call(
        body,
        out_shape=[jax.ShapeDtypeStruct(s, d) for s, d in outs],
        in_specs=places,
        out_specs=[out_place] * len(outs),
        scratch_shapes=list(scratch),
        compiler_params=pltpu.CompilerParams(vmem_limit_bytes=vmem << 20),
        cost_estimate=pl.CostEstimate(flops=flops, bytes_accessed=nbytes, transcendentals=0),
    )


def in_hbm(value):
    return pltpu.with_memory_space_constraint(value, pltpu.HBM)


def fetch(sources, targets, sems):
    copies = [pltpu.make_async_copy(s, t, sems.at[n]) for n, (s, t) in enumerate(zip(sources, targets))]
    for copy in copies:
        copy.start()
    return copies


def low_half(shape):
    return lax.broadcasted_iota(jnp.int32, shape, len(shape) - 1) < 64


def swap64(value):
    return pltpu.roll(value, 64, value.ndim - 1)


def dot(a, b):
    return jnp.dot(a, b, preferred_element_type=F32)


def one_hot(shape, row_of_column):
    row = lax.broadcasted_iota(jnp.int32, shape, 0)
    column = lax.broadcasted_iota(jnp.int32, shape, 1)
    return jnp.where(row == row_of_column(column), 1.0, 0.0).astype(BF16)


def row_of_latitude(column):
    return 16 * (column % 8) + column // 8


def row_of_output(column):
    return 48 * (column % 4) + column // 4


def pack_body(f_hbm, g_hbm, o_ref, f_ref, g_ref, flat_ref, sems):
    copies = fetch((f_hbm, g_hbm), (f_ref, g_ref), sems)
    copies[0].wait()
    for j in range(6):
        count = min(128, 8 * WPART - 128 * j)
        order = one_hot((128, count), row_of_latitude)
        block = dot(order, f_ref[128 * j : 128 * j + count, :]).astype(BF16)
        for r in range(8):
            for h in range(2):
                piece = block[16 * r : 16 * (r + 1), 128 * h : 128 * (h + 1)]
                o_ref[2 * r + h, 16 * j : 16 * (j + 1), :] = piece
    copies[1].wait()
    for v in range(VPART):
        flat_ref[4 * v : 4 * (v + 1), :] = g_ref[v].astype(F32)
    flat_ref[4 * VPART : 192, :] = jnp.zeros((192 - 4 * VPART, C), F32)
    rows = dot(one_hot((192, 192), row_of_output), flat_ref[...].astype(BF16))
    keep = low_half((VROWS, 128))
    for o in range(4):
        for i in range(2):
            cols = slice(128 * i, 128 * (i + 1))
            top, bottom = rows[48 * o : 48 * o + 24, cols], rows[48 * o + 24 : 48 * o + 48, cols]
            even = jnp.where(keep, top, swap64(bottom))
            odd = jnp.where(keep, swap64(top), bottom)
            o_ref[4 * o + 2 * i, WROWS:CHUNK_IN, :] = even.astype(BF16)
            o_ref[4 * o + 2 * i + 1, WROWS:CHUNK_IN, :] = odd.astype(BF16)


def flip(source, target, rows, columns):
    for i in range(rows // 128):
        for j in range(columns // 128):
            piece = source[128 * i : 128 * (i + 1), 128 * j : 128 * (j + 1)].astype(F32)
            target[128 * j : 128 * (j + 1), 128 * i : 128 * (i + 1)] = piece.T.astype(BF16)


def fill_tables(w, v, w_ref, v_ref):
    for e in range(BANDS):
        for b in range(HALF):
            one, two = w[0][e, b : b + 1, :], w[1][e, b : b + 1, :]
            block = one * w[2][e] + two * w[3][e]
            w_ref[e, WROWS * b : WROWS * (b + 1), :] = block.astype(BF16)
            one, two = v[0][e, b : b + 1, :], v[1][e, b : b + 1, :]
            for part in range(2):
                rows = slice(VROWS * part, VROWS * (part + 1))
                block = one * v[2][e, rows, :] + two * v[3][e, rows, :]
                start = VROWS * (HALF * part + b)
                v_ref[e, start : start + VROWS, :] = block.astype(BF16)


def table_body(*refs):
    factors, (w_ref, v_ref) = refs[:8], refs[8:10]
    held, sems = refs[10:18], refs[18]
    for copy in fetch(factors, held, sems):
        copy.wait()
    fill_tables(held[:4], held[4:], w_ref, v_ref)


def flipped_table_body(*refs):
    factors, (wt_ref, vt_ref) = refs[:8], refs[8:10]
    held, (w_ref, v_ref, sems) = refs[10:18], refs[18:]
    for copy in fetch(factors, held, sems):
        copy.wait()
    fill_tables(held[:4], held[4:], w_ref, v_ref)
    for e in range(BANDS):
        flip(w_ref.at[e], wt_ref.at[e], HALF * WROWS, 2 * LANES * M12)
        flip(v_ref.at[e], vt_ref.at[e], 2 * HALF * VROWS, 2 * LANES * M16)


def spectra_body(r_ref, wt_ref, vt_ref, o_ref):
    left = r_ref[0:HALF, 0:WROWS, :].reshape(HALF * WROWS, 128).astype(F32)
    right = r_ref[HALF:LANES, 0:WROWS, :].reshape(HALF * WROWS, 128).astype(F32)
    g_left = r_ref[0:HALF, WROWS:CHUNK_IN, :].reshape(HALF * VROWS, 128).astype(F32)
    g_right = r_ref[HALF:LANES, WROWS:CHUNK_IN, :].reshape(HALF * VROWS, 128).astype(F32)
    keep = low_half((HALF * VROWS, 128))
    for e in range(BANDS):
        x = (left + right if e == 0 else left - right).astype(BF16)
        g = g_left + g_right if e == 0 else g_left - g_right
        turned = swap64(g)
        both = jnp.concatenate([jnp.where(keep, g, turned), jnp.where(keep, turned, g)], axis=0).astype(BF16)
        shares = slice(LANES * e, LANES * (e + 1))
        o_ref[shares, M16:CHUNK_MID, :] = dot(wt_ref[e], x).astype(BF16).reshape(LANES, 2 * M12, 128)
        got = dot(vt_ref[e], both)
        count = LANES * M16
        out = jnp.where(low_half((count, 128)), got[:count], got[count:])
        o_ref[shares, 0:M16, :] = out.astype(BF16).reshape(LANES, M16, 128)


def filter_body(spot_ref, support_ref, p_hbm, mine_ref, other_ref, p_ref, flat_ref, sems):
    (copy,) = fetch((p_hbm,), (p_ref,), sems)
    rows = K * SUPPORT * 4
    band, start = spot_ref[0, 0], 2 * M12 * spot_ref[0, 1]
    line = lax.broadcasted_iota(jnp.int32, (WOUT, 128), 0)
    slot = lax.broadcasted_iota(jnp.int32, (WOUT, 128), 1)
    place = slot % 64
    parity = jnp.where(slot < 64, band, 1 - band)
    mode = start + 2 * (place % M12) + parity
    hit = (line == mode + MODES * (place // M12)) & (place < 2 * M12) & (mode < MODES)
    chosen = jnp.where(hit, 1.0, 0.0).astype(BF16)
    row = lax.broadcasted_iota(jnp.int32, (rows, 128), 0)
    window, output = (row // 4) % SUPPORT, row % 4
    first = jnp.zeros((rows, 128), jnp.int32)
    last = jnp.zeros((rows, 128), jnp.int32)
    for o in range(4):
        first = jnp.where(output == o, support_ref[o, 0], first)
        last = jnp.where(output == o, support_ref[o, 1], last)
    copy.wait()
    for n in range(K * SUPPORT):
        flat_ref[4 * n : 4 * (n + 1), :] = p_ref[n].astype(F32)
    got = dot(flat_ref[0:rows, :].astype(BF16), chosen)
    got = jnp.where((window >= first) & (window <= last), got, 0.0)
    mine_ref[...] = got.astype(BF16)
    other_ref[...] = swap64(got).astype(BF16)


def mixing_body(spot_ref, mine_ref, got_ref, w_hbm, p_ref, w_ref, sems):
    (copy,) = fetch((w_hbm,), (w_ref,), sems)
    rows, width, count = K * 16, HIN * 2 * M12, K * SUPPORT * 4
    low = spot_ref[0, 0] == 0
    mine, got = mine_ref[...].astype(F32), got_ref[...].astype(F32)
    halves = (jnp.where(low, mine, got).astype(BF16), jnp.where(low, got, mine).astype(BF16))
    x = lax.broadcasted_iota(jnp.int32, (128, width), 0)
    lane = lax.broadcasted_iota(jnp.int32, (128, width), 1)
    same, cross = lane % M12, lane % (2 * M12) < M12
    straight = x == same + jnp.where(cross, 0, M12)
    turned = x == same + jnp.where(cross, M12, 0)
    tiles = (
        jnp.where(straight, jnp.where(cross, 1.0, -1.0), 0.0).astype(BF16),
        jnp.where(turned, 1.0, 0.0).astype(BF16),
    )
    row = lax.broadcasted_iota(jnp.int32, (count, width), 0)
    lane = lax.broadcasted_iota(jnp.int32, (count, width), 1)
    reach = 2 * (row % 4) + (row // 4) % SUPPORT - 2 - lane // (2 * M12)
    target = lax.broadcasted_iota(jnp.int32, (rows, count), 0)
    source = lax.broadcasted_iota(jnp.int32, (rows, count), 1)
    key = target - 16 * (source // 20) - 2 * (source % 4)
    total = jnp.zeros((rows, width), F32)
    for half in range(2):
        for ri in range(2):
            spread = dot(halves[half], tiles[ri])
            spread = jnp.where(reach == -8 * half, spread, 0.0).astype(BF16)
            collect = jnp.where(key == 8 * half + ri, 1.0, 0.0).astype(BF16)
            total = total + dot(collect, spread)
    p_ref[...] = total
    copy.wait()


def row_of_share(column):
    return 16 * (column % 16) + column // 16


def middle_body(band_ref, r_ref, p_ref, w_ref, mine_ref, other_ref, gs_ref, out_ref, sg_ref):
    keep = low_half((M16, 128))
    for o in range(HOUT):
        for i in range(2):
            first = r_ref[2 * o + i, 0, 0:M16, :].astype(F32)
            second = r_ref[2 * o + i, 1, 0:M16, :].astype(F32)
            cols = slice(128 * i, 128 * (i + 1))
            gs_ref[32 * o : 32 * o + 16, cols] = jnp.where(keep, first, swap64(second)).astype(BF16)
            gs_ref[32 * o + 16 : 32 * o + 32, cols] = jnp.where(keep, swap64(first), second).astype(BF16)
    used = M12 * 16
    gs = dot(one_hot((used, 256), row_of_share), gs_ref[...]).astype(BF16)
    width = HIN * 2 * M12
    x = jnp.concatenate(
        [r_ref[:, h, M16:CHUNK_MID, :].reshape(width, 128) for h in range(2)], axis=1
    )
    lane_mode = lax.broadcasted_iota(jnp.int32, (16, width), 1) % M12
    diagonal = (
        lax.broadcasted_iota(jnp.int32, (width, used), 0) % M12
        == lax.broadcasted_iota(jnp.int32, (width, used), 1) // 16
    )
    spread = one_hot((16, used), lambda column: column % 16)
    low = band_ref[0, 0] == 0

    for k in range(K):
        placed = p_ref[16 * k : 16 * (k + 1), :]
        blocks = [jnp.where(lane_mode == m, placed, 0.0).astype(BF16) for m in range(M12)]
        mixed = dot(jnp.concatenate(blocks, axis=0), x).astype(BF16)
        out_now = dot(mixed, w_ref[k])
        grad = lax.dot_general(mixed, gs, (((0,), (0,)), ((), ())), preferred_element_type=F32)
        where_to = (slice(None), slice(CHUNK_MID + 16 * k, CHUNK_MID + 16 * (k + 1)), slice(None))
        shape = (LANES, 16, 128)
        mine_ref[where_to] = jnp.where(low, grad[:, :128], grad[:, 128:]).astype(BF16).reshape(shape)
        other_ref[where_to] = jnp.where(low, grad[:, 128:], grad[:, :128]).astype(BF16).reshape(shape)
        back = lax.dot_general(gs, w_ref[k], (((1,), (1,)), ((), ())), preferred_element_type=F32)
        grown = lax.dot_general(
            placed.astype(BF16), spread, (((0,), (0,)), ((), ())), preferred_element_type=F32
        )
        sg_now = dot(jnp.where(diagonal, grown, 0.0).astype(BF16), back.astype(BF16))
        if k == 0:
            out_ref[...] = out_now
            sg_ref[...] = sg_now
        else:
            out_ref[...] += out_now
            sg_ref[...] += sg_now

    ordered = lax.dot_general(
        one_hot((used, 256), row_of_share),
        out_ref[...].astype(BF16),
        (((0,), (0,)), ((), ())),
        preferred_element_type=F32,
    )

    def output_rows(n):
        o, q = n // 4, n % 4
        cols = slice(128 * (q // 2), 128 * (q // 2 + 1))
        re = ordered[32 * o : 32 * o + 16, cols]
        im = ordered[32 * o + 16 : 32 * o + 32, cols]
        return jnp.where(keep, re, swap64(im)) if q % 2 == 0 else jnp.where(keep, swap64(re), im)

    def field_rows(n):
        r, h = n // 2, n % 2
        return sg_ref[24 * r : 24 * (r + 1), 128 * h : 128 * (h + 1)]

    for a in range(LANES):
        for rows, make in ((slice(0, M16), output_rows), (slice(M16, CHUNK_MID), field_rows)):
            first, second = make(a), make(a + LANES)
            mine_ref[a, rows, :] = jnp.where(low, first, second).astype(BF16)
            other_ref[a, rows, :] = jnp.where(low, second, first).astype(BF16)


def merge_body(band_ref, mine_ref, got_ref, o_hbm, o_ref, sems):
    low = band_ref[0, 0] == 0
    copies = []
    for a in range(LANES):
        mine, got = mine_ref[a, 0:CHUNK_MID, :].astype(F32), got_ref[a, 0:CHUNK_MID, :].astype(F32)
        o_ref[a, 0:CHUNK_MID, :] = jnp.where(low, mine, got).astype(BF16)
        o_ref[a, CHUNK_MID : 2 * CHUNK_MID, :] = jnp.where(low, got, mine).astype(BF16)
        mine, got = mine_ref[a, CHUNK_MID:, :].astype(F32), got_ref[a, CHUNK_MID:, :].astype(F32)
        o_ref[a, 2 * CHUNK_MID :, :] = (mine + got).astype(BF16)
        if a % 4 == 3:
            part = slice(a - 3, a + 1)
            copies.append(pltpu.make_async_copy(o_ref.at[part], o_hbm.at[part], sems.at[a // 4]))
            copies[-1].start()
    for copy in copies:
        copy.wait()


def fields_body(r_ref, w_ref, v_ref, o_ref):
    fields, outs = [], []
    for e in range(BANDS):
        start = CHUNK_MID * e
        sg = r_ref[:, start + M16 : start + CHUNK_MID, :].reshape(LANES * 2 * M12, 128)
        fields.append(dot(w_ref[e], sg))
        c = r_ref[:, start : start + M16, :].reshape(LANES * M16, 128).astype(F32)
        turned = swap64(c)
        keep = low_half(c.shape)
        both = jnp.concatenate([jnp.where(keep, c, turned), jnp.where(keep, turned, c)], axis=0).astype(BF16)
        got = dot(v_ref[e], both)
        count = HALF * VROWS
        outs.append(jnp.where(low_half((count, 128)), got[:count], got[count:]))
    for side in range(2):
        lanes = slice(HALF * side, HALF * (side + 1))
        field = fields[0] + fields[1] if side == 0 else fields[0] - fields[1]
        o_ref[lanes, 0:WROWS, :] = field.astype(BF16).reshape(HALF, WROWS, 128)
        out = outs[0] + outs[1] if side == 0 else outs[0] - outs[1]
        o_ref[lanes, WROWS:CHUNK_IN, :] = out.astype(BF16).reshape(HALF, VROWS, 128)


def unpack_body(r_ref, f_ref, c_ref, flat_ref):
    for j in range(6):
        count = min(128, 8 * WPART - 128 * j)
        halves = [
            jnp.concatenate([r_ref[2 * r + h, 16 * j : 16 * (j + 1), :] for r in range(8)], axis=0)
            for h in range(2)
        ]
        order = one_hot((128, count), row_of_latitude)
        block = lax.dot_general(
            order, jnp.concatenate(halves, axis=1), (((0,), (0,)), ((), ())), preferred_element_type=F32
        )
        f_ref[128 * j : 128 * j + count, :] = block.astype(BF16)
    keep = low_half((VROWS, 128))
    for o in range(4):
        for i in range(2):
            even = r_ref[4 * o + 2 * i, WROWS:CHUNK_IN, :].astype(F32)
            odd = r_ref[4 * o + 2 * i + 1, WROWS:CHUNK_IN, :].astype(F32)
            cols = slice(128 * i, 128 * (i + 1))
            flat_ref[48 * o : 48 * o + 24, cols] = jnp.where(keep, even, swap64(odd))
            flat_ref[48 * o + 24 : 48 * o + 48, cols] = jnp.where(keep, swap64(even), odd)
    rows = lax.dot_general(
        one_hot((192, 192), row_of_output),
        flat_ref[...].astype(BF16),
        (((0,), (0,)), ((), ())),
        preferred_element_type=F32,
    )
    for v in range(VPART):
        c_ref[v] = rows[4 * v : 4 * (v + 1), :].astype(BF16)


def swap_bands(value):
    return lax.ppermute(value, "polar", [(0, 1), (1, 0)])


def local(fields, basis_spectra, support, weights, out_grad):
    band = lax.axis_index("polar").astype(jnp.int32)
    low = band == 0
    spot = jnp.stack([band, lax.axis_index("azimuth").astype(jnp.int32)]).reshape(1, 2)
    wide, narrow = factor_tables()
    dma = pltpu.SemaphoreType.DMA
    (sent,) = call(
        pack_body,
        [HBM, HBM],
        [((LANES, CHUNK_IN, 128), BF16)],
        scratch=[
            pltpu.VMEM((8 * WPART, C), BF16),
            pltpu.VMEM((VPART, 4, C), BF16),
            pltpu.VMEM((192, C), F32),
            dma((2,)),
        ],
    )(
        in_hbm(jnp.swapaxes(fields[0], 0, 1).reshape(8 * WPART, C)), in_hbm(jnp.swapaxes(out_grad[0], 0, 1))
    )
    landed = lax.all_to_all(sent, "azimuth", split_axis=0, concat_axis=0, tiled=True)

    filters, limits, sent = lax.optimization_barrier((basis_spectra, support, sent))
    mine, other = call(
        filter_body,
        [SMEM, SMEM, HBM],
        [((K * SUPPORT * 4, 128), BF16)] * 2,
        scratch=[pltpu.VMEM((K * SUPPORT, 4, WOUT), BF16), pltpu.VMEM((184, WOUT), F32), dma((1,))],
    )(spot, limits, in_hbm(jnp.swapaxes(filters, 1, 2).reshape(K * SUPPORT, 4, WOUT)))
    got = swap_bands(other)
    factors = [a for a in wide + narrow]
    held = [pltpu.VMEM(a.shape, F32) for a in factors]
    factors, sent = lax.optimization_barrier(([jnp.asarray(a) for a in factors], sent))
    flat, inv_t = call(
        flipped_table_body,
        [HBM] * 8,
        [((2, 384, 768), BF16), ((2, 512, 384), BF16)],
        nbytes=5 << 20,
        scratch=held + [pltpu.VMEM((2, 768, 384), BF16), pltpu.VMEM((2, 384, 512), BF16), dma((8,))],
    )(*[in_hbm(a) for a in factors])

    landed, mine, got = lax.optimization_barrier((landed, mine, got))
    (sent,) = call(spectra_body, [VMEM] * 3, [((SHARES, CHUNK_MID, 128), BF16)], flops=300 << 20)(landed, flat, inv_t)
    landed = lax.all_to_all(sent, JOINT, split_axis=0, concat_axis=0, tiled=True)
    mine, got, sent = lax.optimization_barrier((mine, got, sent))
    placed, staged = call(
        mixing_body, [SMEM, VMEM, VMEM, HBM], [((K * 16, HIN * 2 * M12), F32), ((K, C, C), BF16)], scratch=[dma((1,))]
    )(spot, mine, got, in_hbm(weights))

    chunk = (LANES, CHUNK_MID + 16 * K, 128)
    mine, other = call(
        middle_body,
        [SMEM, VMEM, VMEM, VMEM],
        [(chunk, BF16), (chunk, BF16)],
        flops=2 << 30,
        nbytes=3 << 20,
        scratch=[
            pltpu.VMEM((256, 256), BF16),
            pltpu.VMEM((192, 256), F32),
            pltpu.VMEM((384, 256), F32),
        ],
    )(spot, landed.reshape(HIN, 2, CHUNK_MID, 128), placed, staged)
    got = swap_bands(other)
    (sent,) = call(
        merge_body,
        [SMEM, VMEM, VMEM],
        [((LANES, CHUNK_OUT, 128), BF16)],
        nbytes=2 << 20,
        scratch=[pltpu.VMEM((LANES, CHUNK_OUT, 128), BF16), dma((4,))],
        out_place=HBM,
    )(spot, mine, got)
    landed = lax.all_to_all(sent, "azimuth", split_axis=0, concat_axis=0, tiled=True)

    factors, sent = lax.optimization_barrier((factors, sent))
    tall, inv = call(
        table_body,
        [HBM] * 8,
        [((2, 768, 384), BF16), ((2, 384, 512), BF16)],
        nbytes=5 << 20,
        scratch=held + [dma((8,))],
    )(*[in_hbm(a) for a in factors])

    landed, tall, inv = lax.optimization_barrier((landed, tall, inv))

    members = lax.axis_size("ens")

    def send(value, offset_even, offset_odd):
        offsets = (offset_even, offset_odd)
        pairs = [(i, (i + offsets[i % 2]) % members) for i in range(members)]
        return lax.ppermute(value, "ens", pairs)

    half = jnp.sum(landed[:, 2 * CHUNK_MID :, :].astype(F32), axis=0).astype(BF16)
    got = send(half, 1, -1)
    pair = (half.astype(F32) + got.astype(F32)).astype(BF16)
    beside = send(pair, -1, 1)
    across = send(beside, 2, -2)
    behind = send(beside, 1, -1)
    half = (pair.astype(F32) + across.astype(F32)) + (beside.astype(F32) + behind.astype(F32))
    far = swap_bands(half)
    (sent,) = call(fields_body, [VMEM] * 3, [((LANES, CHUNK_IN, 128), BF16)], flops=300 << 20)(landed, tall, inv)
    landed = lax.all_to_all(sent, "azimuth", split_axis=0, concat_axis=0, tiled=True)
    weight_grad = jnp.concatenate([jnp.where(low, half, far), jnp.where(low, far, half)], axis=1)
    field_grad, conv_out = call(
        unpack_body, [VMEM], [((8 * WPART, C), BF16), ((VPART, 4, C), BF16)], scratch=[pltpu.VMEM((192, C), F32)]
    )(landed)
    field_grad = jnp.swapaxes(field_grad.reshape(WPART, 8, C), 0, 1)
    return (jnp.swapaxes(conv_out, 0, 1)[None], field_grad[None], weight_grad.reshape(K, 16, C))


def solution(mesh):
    placed = (
        P("ens", "polar", "azimuth", None),
        P(None, "polar", None, None),
        P("polar", None),
        P(),
        P("ens", "polar", "azimuth", None),
    )
    return jax.shard_map(
        local,
        mesh=mesh,
        in_specs=placed,
        out_specs=(
            P("ens", "polar", "azimuth", None),
            P("ens", "polar", "azimuth", None),
            P(None, "azimuth", None),
        ),
        check_vma=False,
    )
```

```python
import math

import jax
import jax.numpy as jnp
import numpy as np
from jax import lax
from jax.experimental import pallas as pl
from jax.experimental.pallas import tpu as pltpu
from jax.sharding import PartitionSpec as P


WIN, WOUT, MODES = 1440, 720, 360
K, C, SUPPORT = 9, 256, 5
HOUT, HIN = 8, 16
LANES, BANDS = 16, 2
SHARES = LANES * BANDS
HALF = LANES // 2
M12, M16 = 12, 16
WPART, WROWS = 90, 96
VPART, VROWS = 45, 24
CHUNK_IN = WROWS + VROWS
CHUNK_MID = M16 + 2 * M12
CHUNK_OUT = 2 * CHUNK_MID + 16 * K
F32, BF16 = jnp.float32, jnp.bfloat16
JOINT = ("polar", "azimuth")


def factor_tables():
    def build(slots, part, steps, period, scale):
        mode_all, keep, imag = slots
        parts = []
        for e in range(BANDS):
            mode = mode_all + e
            ok = keep & (mode < MODES)
            alpha = 2 * math.pi * ((mode[None, :] * (part * np.arange(HALF)[:, None])) % period) / period
            beta = 2 * math.pi * ((mode[None, :] * steps[:, None]) % period) / period
            ok = ok[None, :] & (steps[:, None] < part)
            size = np.where(mode == 0, 1.0, 2.0)[None, :] / WIN if scale else 1.0
            parts.append(
                (
                    np.where(imag[None, :], -np.sin(alpha), np.cos(alpha)),
                    np.where(imag[None, :], -np.cos(alpha), -np.sin(alpha)),
                    np.where(ok, size * np.cos(beta), 0.0),
                    np.where(ok, size * np.sin(beta), 0.0),
                )
            )
        return [np.stack(group).astype(np.float32) for group in zip(*parts)]

    a, ri, i = np.meshgrid(np.arange(LANES), np.arange(2), np.arange(M12), indexing="ij")
    slots = ((2 * (M12 * a + i)).reshape(-1), np.ones(a.size, bool), ri.reshape(-1) == 1)
    wide = build(slots, WPART, np.arange(WROWS), WIN, False)
    ri, a, i = np.meshgrid(np.arange(2), np.arange(LANES), np.arange(M16), indexing="ij")
    slots = ((2 * (M12 * a + i)).reshape(-1), i.reshape(-1) < M12, ri.reshape(-1) == 1)
    narrow = build(slots, VPART, np.arange(2 * VROWS), WOUT, True)
    return wide, narrow


HBM = pl.BlockSpec(memory_space=pltpu.HBM)
VMEM = pl.BlockSpec(memory_space=pltpu.VMEM)
SMEM = pl.BlockSpec(memory_space=pltpu.SMEM)


def call(body, places, outs, flops=0, scratch=(), nbytes=1 << 20, vmem=16, out_place=VMEM):
    return pl.pallas_call(
        body,
        out_shape=[jax.ShapeDtypeStruct(s, d) for s, d in outs],
        in_specs=places,
        out_specs=[out_place] * len(outs),
        scratch_shapes=list(scratch),
        compiler_params=pltpu.CompilerParams(vmem_limit_bytes=vmem << 20),
        cost_estimate=pl.CostEstimate(flops=flops, bytes_accessed=nbytes, transcendentals=0),
    )


def in_hbm(value):
    return pltpu.with_memory_space_constraint(value, pltpu.HBM)


def fetch(sources, targets, sems):
    copies = [pltpu.make_async_copy(s, t, sems.at[n]) for n, (s, t) in enumerate(zip(sources, targets))]
    for copy in copies:
        copy.start()
    return copies


def low_half(shape):
    return lax.broadcasted_iota(jnp.int32, shape, len(shape) - 1) < 64


def swap64(value):
    return pltpu.roll(value, 64, value.ndim - 1)


def dot(a, b):
    return jnp.dot(a, b, preferred_element_type=F32)


def one_hot(shape, row_of_column):
    row = lax.broadcasted_iota(jnp.int32, shape, 0)
    column = lax.broadcasted_iota(jnp.int32, shape, 1)
    return jnp.where(row == row_of_column(column), 1.0, 0.0).astype(BF16)


def row_of_latitude(column):
    return 16 * (column % 8) + column // 8


def row_of_output(column):
    return 48 * (column % 4) + column // 4


def pack_body(f_hbm, g_hbm, o_hbm, f_ref, g_ref, flat_ref, o_ref, sems, out_sems):
    starts = [(128 * j, min(128, 8 * WPART - 128 * j)) for j in range(6)]
    sources = [f_hbm.at[pl.ds(start, count)] for start, count in starts]
    targets = [f_ref.at[pl.ds(start, count)] for start, count in starts]
    copies = fetch(sources + [g_hbm], targets + [g_ref], sems)
    sent = []

    def send(rows, sem):
        sent.append(pltpu.make_async_copy(o_ref.at[:, rows], o_hbm.at[:, rows], out_sems.at[sem]))
        sent[-1].start()

    for j, (start, count) in enumerate(starts):
        order = one_hot((128, count), row_of_latitude)
        copies[j].wait()
        block = dot(order, f_ref[start : start + count, :]).astype(BF16)
        for r in range(8):
            for h in range(2):
                piece = block[16 * r : 16 * (r + 1), 128 * h : 128 * (h + 1)]
                o_ref[2 * r + h, 16 * j : 16 * (j + 1), :] = piece
        if j % 2 == 1:
            send(pl.ds(16 * (j - 1), 32), j // 2)
    copies[6].wait()
    for v in range(VPART):
        flat_ref[4 * v : 4 * (v + 1), :] = g_ref[v].astype(F32)
    flat_ref[4 * VPART : 192, :] = jnp.zeros((192 - 4 * VPART, C), F32)
    rows = dot(one_hot((192, 192), row_of_output), flat_ref[...].astype(BF16))
    keep = low_half((VROWS, 128))
    for o in range(4):
        for i in range(2):
            cols = slice(128 * i, 128 * (i + 1))
            top, bottom = rows[48 * o : 48 * o + 24, cols], rows[48 * o + 24 : 48 * o + 48, cols]
            even = jnp.where(keep, top, swap64(bottom))
            odd = jnp.where(keep, swap64(top), bottom)
            o_ref[4 * o + 2 * i, WROWS:CHUNK_IN, :] = even.astype(BF16)
            o_ref[4 * o + 2 * i + 1, WROWS:CHUNK_IN, :] = odd.astype(BF16)
    send(pl.ds(WROWS, VROWS), 3)
    for copy in sent:
        copy.wait()


def flip(source, target, rows, columns):
    for i in range(rows // 128):
        for j in range(columns // 128):
            piece = source[128 * i : 128 * (i + 1), 128 * j : 128 * (j + 1)].astype(F32)
            target[128 * j : 128 * (j + 1), 128 * i : 128 * (i + 1)] = piece.T.astype(BF16)


def fill_tables(w, v, w_ref, v_ref):
    for e in range(BANDS):
        for b in range(HALF):
            one, two = w[0][e, b : b + 1, :], w[1][e, b : b + 1, :]
            block = one * w[2][e] + two * w[3][e]
            w_ref[e, WROWS * b : WROWS * (b + 1), :] = block.astype(BF16)
            one, two = v[0][e, b : b + 1, :], v[1][e, b : b + 1, :]
            for part in range(2):
                rows = slice(VROWS * part, VROWS * (part + 1))
                block = one * v[2][e, rows, :] + two * v[3][e, rows, :]
                start = VROWS * (HALF * part + b)
                v_ref[e, start : start + VROWS, :] = block.astype(BF16)


def table_body(*refs):
    factors, (w_ref, v_ref) = refs[:8], refs[8:10]
    held, sems = refs[10:18], refs[18]
    for copy in fetch(factors, held, sems):
        copy.wait()
    fill_tables(held[:4], held[4:], w_ref, v_ref)


def flipped_table_body(*refs):
    factors, (wt_ref, vt_ref) = refs[:8], refs[8:10]
    held, (w_ref, v_ref, sems) = refs[10:18], refs[18:]
    for copy in fetch(factors, held, sems):
        copy.wait()
    fill_tables(held[:4], held[4:], w_ref, v_ref)
    for e in range(BANDS):
        flip(w_ref.at[e], wt_ref.at[e], HALF * WROWS, 2 * LANES * M12)
        flip(v_ref.at[e], vt_ref.at[e], 2 * HALF * VROWS, 2 * LANES * M16)


def spectra_body(r_ref, wt_ref, vt_ref, o_ref):
    left = r_ref[0:HALF, 0:WROWS, :].reshape(HALF * WROWS, 128).astype(F32)
    right = r_ref[HALF:LANES, 0:WROWS, :].reshape(HALF * WROWS, 128).astype(F32)
    g_left = r_ref[0:HALF, WROWS:CHUNK_IN, :].reshape(HALF * VROWS, 128).astype(F32)
    g_right = r_ref[HALF:LANES, WROWS:CHUNK_IN, :].reshape(HALF * VROWS, 128).astype(F32)
    keep = low_half((HALF * VROWS, 128))
    for e in range(BANDS):
        x = (left + right if e == 0 else left - right).astype(BF16)
        g = g_left + g_right if e == 0 else g_left - g_right
        turned = swap64(g)
        both = jnp.concatenate([jnp.where(keep, g, turned), jnp.where(keep, turned, g)], axis=0).astype(BF16)
        shares = slice(LANES * e, LANES * (e + 1))
        o_ref[shares, M16:CHUNK_MID, :] = dot(wt_ref[e], x).astype(BF16).reshape(LANES, 2 * M12, 128)
        got = dot(vt_ref[e], both)
        count = LANES * M16
        out = jnp.where(low_half((count, 128)), got[:count], got[count:])
        o_ref[shares, 0:M16, :] = out.astype(BF16).reshape(LANES, M16, 128)


def filter_body(spot_ref, support_ref, p_hbm, mine_ref, other_ref, p_ref, flat_ref, sems):
    (copy,) = fetch((p_hbm,), (p_ref,), sems)
    rows = K * SUPPORT * 4
    band, start = spot_ref[0, 0], 2 * M12 * spot_ref[0, 1]
    line = lax.broadcasted_iota(jnp.int32, (WOUT, 128), 0)
    slot = lax.broadcasted_iota(jnp.int32, (WOUT, 128), 1)
    place = slot % 64
    parity = jnp.where(slot < 64, band, 1 - band)
    mode = start + 2 * (place % M12) + parity
    hit = (line == mode + MODES * (place // M12)) & (place < 2 * M12) & (mode < MODES)
    chosen = jnp.where(hit, 1.0, 0.0).astype(BF16)
    row = lax.broadcasted_iota(jnp.int32, (rows, 128), 0)
    window, output = (row // 4) % SUPPORT, row % 4
    first = jnp.zeros((rows, 128), jnp.int32)
    last = jnp.zeros((rows, 128), jnp.int32)
    for o in range(4):
        first = jnp.where(output == o, support_ref[o, 0], first)
        last = jnp.where(output == o, support_ref[o, 1], last)
    copy.wait()
    for n in range(K * SUPPORT):
        flat_ref[4 * n : 4 * (n + 1), :] = p_ref[n].astype(F32)
    got = dot(flat_ref[0:rows, :].astype(BF16), chosen)
    got = jnp.where((window >= first) & (window <= last), got, 0.0)
    mine_ref[...] = got.astype(BF16)
    other_ref[...] = swap64(got).astype(BF16)


def mixing_body(spot_ref, mine_ref, got_ref, w_hbm, p_ref, w_ref, sems):
    (copy,) = fetch((w_hbm,), (w_ref,), sems)
    rows, width, count = K * 16, HIN * 2 * M12, K * SUPPORT * 4
    low = spot_ref[0, 0] == 0
    mine, got = mine_ref[...].astype(F32), got_ref[...].astype(F32)
    halves = (jnp.where(low, mine, got).astype(BF16), jnp.where(low, got, mine).astype(BF16))
    x = lax.broadcasted_iota(jnp.int32, (128, width), 0)
    lane = lax.broadcasted_iota(jnp.int32, (128, width), 1)
    same, cross = lane % M12, lane % (2 * M12) < M12
    straight = x == same + jnp.where(cross, 0, M12)
    turned = x == same + jnp.where(cross, M12, 0)
    tiles = (
        jnp.where(straight, jnp.where(cross, 1.0, -1.0), 0.0).astype(BF16),
        jnp.where(turned, 1.0, 0.0).astype(BF16),
    )
    row = lax.broadcasted_iota(jnp.int32, (count, width), 0)
    lane = lax.broadcasted_iota(jnp.int32, (count, width), 1)
    reach = 2 * (row % 4) + (row // 4) % SUPPORT - 2 - lane // (2 * M12)
    target = lax.broadcasted_iota(jnp.int32, (rows, count), 0)
    source = lax.broadcasted_iota(jnp.int32, (rows, count), 1)
    key = target - 16 * (source // 20) - 2 * (source % 4)
    total = jnp.zeros((rows, width), F32)
    for half in range(2):
        for ri in range(2):
            spread = dot(halves[half], tiles[ri])
            spread = jnp.where(reach == -8 * half, spread, 0.0).astype(BF16)
            collect = jnp.where(key == 8 * half + ri, 1.0, 0.0).astype(BF16)
            total = total + dot(collect, spread)
    p_ref[...] = total
    copy.wait()


def row_of_share(column):
    return 16 * (column % 16) + column // 16


def middle_body(band_ref, r_ref, p_ref, w_ref, mine_ref, other_ref, gs_ref, out_ref, sg_ref):
    keep = low_half((M16, 128))
    for o in range(HOUT):
        for i in range(2):
            first = r_ref[2 * o + i, 0, 0:M16, :].astype(F32)
            second = r_ref[2 * o + i, 1, 0:M16, :].astype(F32)
            cols = slice(128 * i, 128 * (i + 1))
            gs_ref[32 * o : 32 * o + 16, cols] = jnp.where(keep, first, swap64(second)).astype(BF16)
            gs_ref[32 * o + 16 : 32 * o + 32, cols] = jnp.where(keep, swap64(first), second).astype(BF16)
    used = M12 * 16
    gs = dot(one_hot((used, 256), row_of_share), gs_ref[...]).astype(BF16)
    width = HIN * 2 * M12
    x = jnp.concatenate(
        [r_ref[:, h, M16:CHUNK_MID, :].reshape(width, 128) for h in range(2)], axis=1
    )
    lane_mode = lax.broadcasted_iota(jnp.int32, (16, width), 1) % M12
    diagonal = (
        lax.broadcasted_iota(jnp.int32, (width, used), 0) % M12
        == lax.broadcasted_iota(jnp.int32, (width, used), 1) // 16
    )
    spread = one_hot((16, used), lambda column: column % 16)
    low = band_ref[0, 0] == 0

    for k in range(K):
        placed = p_ref[16 * k : 16 * (k + 1), :]
        blocks = [jnp.where(lane_mode == m, placed, 0.0).astype(BF16) for m in range(M12)]
        mixed = dot(jnp.concatenate(blocks, axis=0), x).astype(BF16)
        out_now = dot(mixed, w_ref[k])
        grad = lax.dot_general(mixed, gs, (((0,), (0,)), ((), ())), preferred_element_type=F32)
        where_to = (slice(None), slice(CHUNK_MID + 16 * k, CHUNK_MID + 16 * (k + 1)), slice(None))
        shape = (LANES, 16, 128)
        mine_ref[where_to] = jnp.where(low, grad[:, :128], grad[:, 128:]).astype(BF16).reshape(shape)
        other_ref[where_to] = jnp.where(low, grad[:, 128:], grad[:, :128]).astype(BF16).reshape(shape)
        back = lax.dot_general(gs, w_ref[k], (((1,), (1,)), ((), ())), preferred_element_type=F32)
        grown = lax.dot_general(
            placed.astype(BF16), spread, (((0,), (0,)), ((), ())), preferred_element_type=F32
        )
        sg_now = dot(jnp.where(diagonal, grown, 0.0).astype(BF16), back.astype(BF16))
        if k == 0:
            out_ref[...] = out_now
            sg_ref[...] = sg_now
        else:
            out_ref[...] += out_now
            sg_ref[...] += sg_now

    ordered = lax.dot_general(
        one_hot((used, 256), row_of_share),
        out_ref[...].astype(BF16),
        (((0,), (0,)), ((), ())),
        preferred_element_type=F32,
    )

    def output_rows(n):
        o, q = n // 4, n % 4
        cols = slice(128 * (q // 2), 128 * (q // 2 + 1))
        re = ordered[32 * o : 32 * o + 16, cols]
        im = ordered[32 * o + 16 : 32 * o + 32, cols]
        return jnp.where(keep, re, swap64(im)) if q % 2 == 0 else jnp.where(keep, swap64(re), im)

    def field_rows(n):
        r, h = n // 2, n % 2
        return sg_ref[24 * r : 24 * (r + 1), 128 * h : 128 * (h + 1)]

    for a in range(LANES):
        for rows, make in ((slice(0, M16), output_rows), (slice(M16, CHUNK_MID), field_rows)):
            first, second = make(a), make(a + LANES)
            mine_ref[a, rows, :] = jnp.where(low, first, second).astype(BF16)
            other_ref[a, rows, :] = jnp.where(low, second, first).astype(BF16)


def merge_body(band_ref, mine_ref, got_ref, o_hbm, o_ref, sems):
    low = band_ref[0, 0] == 0
    copies = []
    for a in range(LANES):
        mine, got = mine_ref[a, 0:CHUNK_MID, :].astype(F32), got_ref[a, 0:CHUNK_MID, :].astype(F32)
        o_ref[a, 0:CHUNK_MID, :] = jnp.where(low, mine, got).astype(BF16)
        o_ref[a, CHUNK_MID : 2 * CHUNK_MID, :] = jnp.where(low, got, mine).astype(BF16)
        mine, got = mine_ref[a, CHUNK_MID:, :].astype(F32), got_ref[a, CHUNK_MID:, :].astype(F32)
        o_ref[a, 2 * CHUNK_MID :, :] = (mine + got).astype(BF16)
        if a % 4 == 3:
            part = slice(a - 3, a + 1)
            copies.append(pltpu.make_async_copy(o_ref.at[part], o_hbm.at[part], sems.at[a // 4]))
            copies[-1].start()
    for copy in copies:
        copy.wait()


def fields_body(r_ref, w_ref, v_ref, o_ref):
    fields, outs = [], []
    for e in range(BANDS):
        start = CHUNK_MID * e
        sg = r_ref[:, start + M16 : start + CHUNK_MID, :].reshape(LANES * 2 * M12, 128)
        fields.append(dot(w_ref[e], sg))
        c = r_ref[:, start : start + M16, :].reshape(LANES * M16, 128).astype(F32)
        turned = swap64(c)
        keep = low_half(c.shape)
        both = jnp.concatenate([jnp.where(keep, c, turned), jnp.where(keep, turned, c)], axis=0).astype(BF16)
        got = dot(v_ref[e], both)
        count = HALF * VROWS
        outs.append(jnp.where(low_half((count, 128)), got[:count], got[count:]))
    for side in range(2):
        lanes = slice(HALF * side, HALF * (side + 1))
        field = fields[0] + fields[1] if side == 0 else fields[0] - fields[1]
        o_ref[lanes, 0:WROWS, :] = field.astype(BF16).reshape(HALF, WROWS, 128)
        out = outs[0] + outs[1] if side == 0 else outs[0] - outs[1]
        o_ref[lanes, WROWS:CHUNK_IN, :] = out.astype(BF16).reshape(HALF, VROWS, 128)


def unpack_body(r_ref, f_ref, c_ref, flat_ref):
    for j in range(6):
        count = min(128, 8 * WPART - 128 * j)
        halves = [
            jnp.concatenate([r_ref[2 * r + h, 16 * j : 16 * (j + 1), :] for r in range(8)], axis=0)
            for h in range(2)
        ]
        order = one_hot((128, count), row_of_latitude)
        block = lax.dot_general(
            order, jnp.concatenate(halves, axis=1), (((0,), (0,)), ((), ())), preferred_element_type=F32
        )
        f_ref[128 * j : 128 * j + count, :] = block.astype(BF16)
    keep = low_half((VROWS, 128))
    for o in range(4):
        for i in range(2):
            even = r_ref[4 * o + 2 * i, WROWS:CHUNK_IN, :].astype(F32)
            odd = r_ref[4 * o + 2 * i + 1, WROWS:CHUNK_IN, :].astype(F32)
            cols = slice(128 * i, 128 * (i + 1))
            flat_ref[48 * o : 48 * o + 24, cols] = jnp.where(keep, even, swap64(odd))
            flat_ref[48 * o + 24 : 48 * o + 48, cols] = jnp.where(keep, swap64(even), odd)
    rows = lax.dot_general(
        one_hot((192, 192), row_of_output),
        flat_ref[...].astype(BF16),
        (((0,), (0,)), ((), ())),
        preferred_element_type=F32,
    )
    for v in range(VPART):
        c_ref[v] = rows[4 * v : 4 * (v + 1), :].astype(BF16)


def swap_bands(value):
    return lax.ppermute(value, "polar", [(0, 1), (1, 0)])


def local(fields, basis_spectra, support, weights, out_grad):
    band = lax.axis_index("polar").astype(jnp.int32)
    low = band == 0
    spot = jnp.stack([band, lax.axis_index("azimuth").astype(jnp.int32)]).reshape(1, 2)
    wide, narrow = factor_tables()
    dma = pltpu.SemaphoreType.DMA
    (sent,) = call(
        pack_body,
        [HBM, HBM],
        [((LANES, CHUNK_IN, 128), BF16)],
        scratch=[
            pltpu.VMEM((8 * WPART, C), BF16),
            pltpu.VMEM((VPART, 4, C), BF16),
            pltpu.VMEM((192, C), F32),
            pltpu.VMEM((LANES, CHUNK_IN, 128), BF16),
            dma((7,)),
            dma((4,)),
        ],
        out_place=HBM,
    )(
        in_hbm(jnp.swapaxes(fields[0], 0, 1).reshape(8 * WPART, C)), in_hbm(jnp.swapaxes(out_grad[0], 0, 1))
    )
    landed = lax.all_to_all(sent, "azimuth", split_axis=0, concat_axis=0, tiled=True)

    filters, limits, sent = lax.optimization_barrier((basis_spectra, support, sent))
    mine, other = call(
        filter_body,
        [SMEM, SMEM, HBM],
        [((K * SUPPORT * 4, 128), BF16)] * 2,
        scratch=[pltpu.VMEM((K * SUPPORT, 4, WOUT), BF16), pltpu.VMEM((184, WOUT), F32), dma((1,))],
    )(spot, limits, in_hbm(jnp.swapaxes(filters, 1, 2).reshape(K * SUPPORT, 4, WOUT)))
    got = swap_bands(other)
    factors = [a for a in wide + narrow]
    held = [pltpu.VMEM(a.shape, F32) for a in factors]
    factors, sent = lax.optimization_barrier(([jnp.asarray(a) for a in factors], sent))
    flat, inv_t = call(
        flipped_table_body,
        [HBM] * 8,
        [((2, 384, 768), BF16), ((2, 512, 384), BF16)],
        nbytes=5 << 20,
        scratch=held + [pltpu.VMEM((2, 768, 384), BF16), pltpu.VMEM((2, 384, 512), BF16), dma((8,))],
    )(*[in_hbm(a) for a in factors])

    landed, mine, got = lax.optimization_barrier((landed, mine, got))
    (sent,) = call(spectra_body, [VMEM] * 3, [((SHARES, CHUNK_MID, 128), BF16)], flops=300 << 20)(landed, flat, inv_t)
    landed = lax.all_to_all(sent, JOINT, split_axis=0, concat_axis=0, tiled=True)
    mine, got, sent = lax.optimization_barrier((mine, got, sent))
    placed, staged = call(
        mixing_body, [SMEM, VMEM, VMEM, HBM], [((K * 16, HIN * 2 * M12), F32), ((K, C, C), BF16)], scratch=[dma((1,))]
    )(spot, mine, got, in_hbm(weights))

    chunk = (LANES, CHUNK_MID + 16 * K, 128)
    mine, other = call(
        middle_body,
        [SMEM, VMEM, VMEM, VMEM],
        [(chunk, BF16), (chunk, BF16)],
        flops=2 << 30,
        nbytes=3 << 20,
        scratch=[
            pltpu.VMEM((256, 256), BF16),
            pltpu.VMEM((192, 256), F32),
            pltpu.VMEM((384, 256), F32),
        ],
    )(spot, landed.reshape(HIN, 2, CHUNK_MID, 128), placed, staged)
    got = swap_bands(other)
    (sent,) = call(
        merge_body,
        [SMEM, VMEM, VMEM],
        [((LANES, CHUNK_OUT, 128), BF16)],
        nbytes=2 << 20,
        scratch=[pltpu.VMEM((LANES, CHUNK_OUT, 128), BF16), dma((4,))],
        out_place=HBM,
    )(spot, mine, got)
    landed = lax.all_to_all(sent, "azimuth", split_axis=0, concat_axis=0, tiled=True)

    factors, sent = lax.optimization_barrier((factors, sent))
    tall, inv = call(
        table_body,
        [HBM] * 8,
        [((2, 768, 384), BF16), ((2, 384, 512), BF16)],
        nbytes=5 << 20,
        scratch=held + [dma((8,))],
    )(*[in_hbm(a) for a in factors])

    landed, tall, inv = lax.optimization_barrier((landed, tall, inv))

    members = lax.axis_size("ens")

    def send(value, offset_even, offset_odd):
        offsets = (offset_even, offset_odd)
        pairs = [(i, (i + offsets[i % 2]) % members) for i in range(members)]
        return lax.ppermute(value, "ens", pairs)

    half = jnp.sum(landed[:, 2 * CHUNK_MID :, :].astype(F32), axis=0).astype(BF16)
    got = send(half, 1, -1)
    pair = (half.astype(F32) + got.astype(F32)).astype(BF16)
    beside = send(pair, -1, 1)
    across = send(beside, 2, -2)
    behind = send(beside, 1, -1)
    half = (pair.astype(F32) + across.astype(F32)) + (beside.astype(F32) + behind.astype(F32))
    far = swap_bands(half)
    (sent,) = call(fields_body, [VMEM] * 3, [((LANES, CHUNK_IN, 128), BF16)], flops=300 << 20)(landed, tall, inv)
    landed = lax.all_to_all(sent, "azimuth", split_axis=0, concat_axis=0, tiled=True)
    field_grad, conv_out = call(
        unpack_body, [VMEM], [((8 * WPART, C), BF16), ((VPART, 4, C), BF16)], scratch=[pltpu.VMEM((192, C), F32)]
    )(landed)
    weight_grad = jnp.concatenate([jnp.where(low, half, far), jnp.where(low, far, half)], axis=1)
    field_grad = jnp.swapaxes(field_grad.reshape(WPART, 8, C), 0, 1)
    return (jnp.swapaxes(conv_out, 0, 1)[None], field_grad[None], weight_grad.reshape(K, 16, C))


def solution(mesh):
    placed = (
        P("ens", "polar", "azimuth", None),
        P(None, "polar", None, None),
        P("polar", None),
        P(),
        P("ens", "polar", "azimuth", None),
    )
    return jax.shard_map(
        local,
        mesh=mesh,
        in_specs=placed,
        out_specs=(
            P("ens", "polar", "azimuth", None),
            P("ens", "polar", "azimuth", None),
            P(None, "azimuth", None),
        ),
        check_vma=False,
    )
```

```python
import math

import jax
import jax.numpy as jnp
import numpy as np
from jax import lax
from jax.experimental import pallas as pl
from jax.experimental.pallas import tpu as pltpu
from jax.sharding import PartitionSpec as P


WIN, WOUT, MODES = 1440, 720, 360
K, C, SUPPORT = 9, 256, 5
HOUT, HIN = 8, 16
LANES, BANDS = 16, 2
SHARES = LANES * BANDS
HALF = LANES // 2
M12, M16 = 12, 16
WPART, WROWS = 90, 96
VPART, VROWS = 45, 24
CHUNK_IN = WROWS + VROWS
CHUNK_MID = M16 + 2 * M12
CHUNK_OUT = 2 * CHUNK_MID + 16 * K
F32, BF16 = jnp.float32, jnp.bfloat16
JOINT = ("polar", "azimuth")


def factor_tables():
    def build(slots, part, steps, period, scale):
        mode_all, keep, imag = slots
        parts = []
        for e in range(BANDS):
            mode = mode_all + e
            ok = keep & (mode < MODES)
            alpha = 2 * math.pi * ((mode[None, :] * (part * np.arange(HALF)[:, None])) % period) / period
            beta = 2 * math.pi * ((mode[None, :] * steps[:, None]) % period) / period
            ok = ok[None, :] & (steps[:, None] < part)
            size = np.where(mode == 0, 1.0, 2.0)[None, :] / WIN if scale else 1.0
            parts.append(
                (
                    np.where(imag[None, :], -np.sin(alpha), np.cos(alpha)),
                    np.where(imag[None, :], -np.cos(alpha), -np.sin(alpha)),
                    np.where(ok, size * np.cos(beta), 0.0),
                    np.where(ok, size * np.sin(beta), 0.0),
                )
            )
        return [np.stack(group).astype(np.float32) for group in zip(*parts)]

    a, ri, i = np.meshgrid(np.arange(LANES), np.arange(2), np.arange(M12), indexing="ij")
    slots = ((2 * (M12 * a + i)).reshape(-1), np.ones(a.size, bool), ri.reshape(-1) == 1)
    wide = build(slots, WPART, np.arange(WROWS), WIN, False)
    ri, a, i = np.meshgrid(np.arange(2), np.arange(LANES), np.arange(M16), indexing="ij")
    slots = ((2 * (M12 * a + i)).reshape(-1), i.reshape(-1) < M12, ri.reshape(-1) == 1)
    narrow = build(slots, VPART, np.arange(2 * VROWS), WOUT, True)
    return wide, narrow


HBM = pl.BlockSpec(memory_space=pltpu.HBM)
VMEM = pl.BlockSpec(memory_space=pltpu.VMEM)
SMEM = pl.BlockSpec(memory_space=pltpu.SMEM)


def call(body, places, outs, flops=0, scratch=(), nbytes=1 << 20, vmem=16, out_places=None):
    return pl.pallas_call(
        body,
        out_shape=[jax.ShapeDtypeStruct(*o) if isinstance(o, tuple) else o for o in outs],
        in_specs=places,
        out_specs=out_places or [VMEM] * len(outs),
        scratch_shapes=list(scratch),
        compiler_params=pltpu.CompilerParams(vmem_limit_bytes=vmem << 20),
        cost_estimate=pl.CostEstimate(flops=flops, bytes_accessed=nbytes, transcendentals=0),
    )


def in_hbm(value):
    return pltpu.with_memory_space_constraint(value, pltpu.HBM)


def fetch(sources, targets, sems):
    copies = [pltpu.make_async_copy(s, t, sems.at[n]) for n, (s, t) in enumerate(zip(sources, targets))]
    for copy in copies:
        copy.start()
    return copies


def low_half(shape):
    return lax.broadcasted_iota(jnp.int32, shape, len(shape) - 1) < 64


def swap64(value):
    return pltpu.roll(value, 64, value.ndim - 1)


def dot(a, b):
    return jnp.dot(a, b, preferred_element_type=F32)


def one_hot(shape, row_of_column):
    row = lax.broadcasted_iota(jnp.int32, shape, 0)
    column = lax.broadcasted_iota(jnp.int32, shape, 1)
    return jnp.where(row == row_of_column(column), 1.0, 0.0).astype(BF16)


def row_of_latitude(column):
    return 16 * (column % 8) + column // 8


def row_of_output(column):
    return 48 * (column % 4) + column // 4


def pack_body(f_hbm, g_hbm, o_ref, f_ref, g_ref, flat_ref, sems):
    copies = fetch((f_hbm, g_hbm), (f_ref, g_ref), sems)
    copies[0].wait()
    for j in range(6):
        count = min(128, 8 * WPART - 128 * j)
        order = one_hot((128, count), row_of_latitude)
        block = dot(order, f_ref[128 * j : 128 * j + count, :]).astype(BF16)
        for r in range(8):
            for h in range(2):
                piece = block[16 * r : 16 * (r + 1), 128 * h : 128 * (h + 1)]
                o_ref[2 * r + h, 16 * j : 16 * (j + 1), :] = piece
    copies[1].wait()
    for v in range(VPART):
        flat_ref[4 * v : 4 * (v + 1), :] = g_ref[v].astype(F32)
    flat_ref[4 * VPART : 192, :] = jnp.zeros((192 - 4 * VPART, C), F32)
    rows = dot(one_hot((192, 192), row_of_output), flat_ref[...].astype(BF16))
    keep = low_half((VROWS, 128))
    for o in range(4):
        for i in range(2):
            cols = slice(128 * i, 128 * (i + 1))
            top, bottom = rows[48 * o : 48 * o + 24, cols], rows[48 * o + 24 : 48 * o + 48, cols]
            even = jnp.where(keep, top, swap64(bottom))
            odd = jnp.where(keep, swap64(top), bottom)
            o_ref[4 * o + 2 * i, WROWS:CHUNK_IN, :] = even.astype(BF16)
            o_ref[4 * o + 2 * i + 1, WROWS:CHUNK_IN, :] = odd.astype(BF16)


def flip(source, target, rows, columns):
    for i in range(rows // 128):
        for j in range(columns // 128):
            piece = source[128 * i : 128 * (i + 1), 128 * j : 128 * (j + 1)].astype(F32)
            target[128 * j : 128 * (j + 1), 128 * i : 128 * (i + 1)] = piece.T.astype(BF16)


def fill_tables(w, v, w_ref, v_ref):
    for e in range(BANDS):
        for b in range(HALF):
            one, two = w[0][e, b : b + 1, :], w[1][e, b : b + 1, :]
            block = one * w[2][e] + two * w[3][e]
            w_ref[e, WROWS * b : WROWS * (b + 1), :] = block.astype(BF16)
            one, two = v[0][e, b : b + 1, :], v[1][e, b : b + 1, :]
            for part in range(2):
                rows = slice(VROWS * part, VROWS * (part + 1))
                block = one * v[2][e, rows, :] + two * v[3][e, rows, :]
                start = VROWS * (HALF * part + b)
                v_ref[e, start : start + VROWS, :] = block.astype(BF16)


def table_body(*refs):
    factors, (w_ref, v_hbm) = refs[:8], refs[8:10]
    held, (v_ref, sems) = refs[10:18], refs[18:]
    for copy in fetch(factors, held, sems):
        copy.wait()
    fill_tables(held[:4], held[4:], w_ref, v_ref)
    (copy,) = fetch((v_ref,), (v_hbm,), sems)
    copy.wait()


def flipped_table_body(*refs):
    factors, (wt_ref, vt_ref) = refs[:8], refs[8:10]
    held, (w_ref, v_ref, sems) = refs[10:18], refs[18:]
    for copy in fetch(factors, held, sems):
        copy.wait()
    fill_tables(held[:4], held[4:], w_ref, v_ref)
    for e in range(BANDS):
        flip(w_ref.at[e], wt_ref.at[e], HALF * WROWS, 2 * LANES * M12)
        flip(v_ref.at[e], vt_ref.at[e], 2 * HALF * VROWS, 2 * LANES * M16)


def spectra_body(r_ref, wt_ref, vt_ref, o_ref):
    left = r_ref[0:HALF, 0:WROWS, :].reshape(HALF * WROWS, 128).astype(F32)
    right = r_ref[HALF:LANES, 0:WROWS, :].reshape(HALF * WROWS, 128).astype(F32)
    g_left = r_ref[0:HALF, WROWS:CHUNK_IN, :].reshape(HALF * VROWS, 128).astype(F32)
    g_right = r_ref[HALF:LANES, WROWS:CHUNK_IN, :].reshape(HALF * VROWS, 128).astype(F32)
    keep = low_half((HALF * VROWS, 128))
    for e in range(BANDS):
        x = (left + right if e == 0 else left - right).astype(BF16)
        g = g_left + g_right if e == 0 else g_left - g_right
        turned = swap64(g)
        both = jnp.concatenate([jnp.where(keep, g, turned), jnp.where(keep, turned, g)], axis=0).astype(BF16)
        shares = slice(LANES * e, LANES * (e + 1))
        o_ref[shares, M16:CHUNK_MID, :] = dot(wt_ref[e], x).astype(BF16).reshape(LANES, 2 * M12, 128)
        got = dot(vt_ref[e], both)
        count = LANES * M16
        out = jnp.where(low_half((count, 128)), got[:count], got[count:])
        o_ref[shares, 0:M16, :] = out.astype(BF16).reshape(LANES, M16, 128)


def filter_body(spot_ref, support_ref, p_hbm, mine_ref, other_ref, p_ref, flat_ref, sems):
    (copy,) = fetch((p_hbm,), (p_ref,), sems)
    rows = K * SUPPORT * 4
    band, start = spot_ref[0, 0], 2 * M12 * spot_ref[0, 1]
    line = lax.broadcasted_iota(jnp.int32, (WOUT, 128), 0)
    slot = lax.broadcasted_iota(jnp.int32, (WOUT, 128), 1)
    place = slot % 64
    parity = jnp.where(slot < 64, band, 1 - band)
    mode = start + 2 * (place % M12) + parity
    hit = (line == mode + MODES * (place // M12)) & (place < 2 * M12) & (mode < MODES)
    chosen = jnp.where(hit, 1.0, 0.0).astype(BF16)
    row = lax.broadcasted_iota(jnp.int32, (rows, 128), 0)
    window, output = (row // 4) % SUPPORT, row % 4
    first = jnp.zeros((rows, 128), jnp.int32)
    last = jnp.zeros((rows, 128), jnp.int32)
    for o in range(4):
        first = jnp.where(output == o, support_ref[o, 0], first)
        last = jnp.where(output == o, support_ref[o, 1], last)
    copy.wait()
    for n in range(K * SUPPORT):
        flat_ref[4 * n : 4 * (n + 1), :] = p_ref[n].astype(F32)
    got = dot(flat_ref[0:rows, :].astype(BF16), chosen)
    got = jnp.where((window >= first) & (window <= last), got, 0.0)
    mine_ref[...] = got.astype(BF16)
    other_ref[...] = swap64(got).astype(BF16)


def mixing_body(spot_ref, mine_ref, got_ref, w_hbm, p_ref, w_ref, sems):
    (copy,) = fetch((w_hbm,), (w_ref,), sems)
    rows, width, count = K * 16, HIN * 2 * M12, K * SUPPORT * 4
    low = spot_ref[0, 0] == 0
    mine, got = mine_ref[...].astype(F32), got_ref[...].astype(F32)
    halves = (jnp.where(low, mine, got).astype(BF16), jnp.where(low, got, mine).astype(BF16))
    x = lax.broadcasted_iota(jnp.int32, (128, width), 0)
    lane = lax.broadcasted_iota(jnp.int32, (128, width), 1)
    same, cross = lane % M12, lane % (2 * M12) < M12
    straight = x == same + jnp.where(cross, 0, M12)
    turned = x == same + jnp.where(cross, M12, 0)
    tiles = (
        jnp.where(straight, jnp.where(cross, 1.0, -1.0), 0.0).astype(BF16),
        jnp.where(turned, 1.0, 0.0).astype(BF16),
    )
    row = lax.broadcasted_iota(jnp.int32, (count, width), 0)
    lane = lax.broadcasted_iota(jnp.int32, (count, width), 1)
    reach = 2 * (row % 4) + (row // 4) % SUPPORT - 2 - lane // (2 * M12)
    target = lax.broadcasted_iota(jnp.int32, (rows, count), 0)
    source = lax.broadcasted_iota(jnp.int32, (rows, count), 1)
    key = target - 16 * (source // 20) - 2 * (source % 4)
    total = jnp.zeros((rows, width), F32)
    for half in range(2):
        for ri in range(2):
            spread = dot(halves[half], tiles[ri])
            spread = jnp.where(reach == -8 * half, spread, 0.0).astype(BF16)
            collect = jnp.where(key == 8 * half + ri, 1.0, 0.0).astype(BF16)
            total = total + dot(collect, spread)
    p_ref[...] = total
    copy.wait()


def row_of_share(column):
    return 16 * (column % 16) + column // 16


def middle_body(band_ref, r_ref, p_ref, w_ref, mine_ref, other_ref, gs_ref, out_ref, sg_ref):
    keep = low_half((M16, 128))
    for o in range(HOUT):
        for i in range(2):
            first = r_ref[2 * o + i, 0, 0:M16, :].astype(F32)
            second = r_ref[2 * o + i, 1, 0:M16, :].astype(F32)
            cols = slice(128 * i, 128 * (i + 1))
            gs_ref[32 * o : 32 * o + 16, cols] = jnp.where(keep, first, swap64(second)).astype(BF16)
            gs_ref[32 * o + 16 : 32 * o + 32, cols] = jnp.where(keep, swap64(first), second).astype(BF16)
    used = M12 * 16
    gs = dot(one_hot((used, 256), row_of_share), gs_ref[...]).astype(BF16)
    width = HIN * 2 * M12
    x = jnp.concatenate(
        [r_ref[:, h, M16:CHUNK_MID, :].reshape(width, 128) for h in range(2)], axis=1
    )
    lane_mode = lax.broadcasted_iota(jnp.int32, (16, width), 1) % M12
    diagonal = (
        lax.broadcasted_iota(jnp.int32, (width, used), 0) % M12
        == lax.broadcasted_iota(jnp.int32, (width, used), 1) // 16
    )
    spread = one_hot((16, used), lambda column: column % 16)
    low = band_ref[0, 0] == 0

    for k in range(K):
        placed = p_ref[16 * k : 16 * (k + 1), :]
        blocks = [jnp.where(lane_mode == m, placed, 0.0).astype(BF16) for m in range(M12)]
        mixed = dot(jnp.concatenate(blocks, axis=0), x).astype(BF16)
        out_now = dot(mixed, w_ref[k])
        grad = lax.dot_general(mixed, gs, (((0,), (0,)), ((), ())), preferred_element_type=F32)
        where_to = (slice(None), slice(CHUNK_MID + 16 * k, CHUNK_MID + 16 * (k + 1)), slice(None))
        shape = (LANES, 16, 128)
        mine_ref[where_to] = jnp.where(low, grad[:, :128], grad[:, 128:]).astype(BF16).reshape(shape)
        other_ref[where_to] = jnp.where(low, grad[:, 128:], grad[:, :128]).astype(BF16).reshape(shape)
        back = lax.dot_general(gs, w_ref[k], (((1,), (1,)), ((), ())), preferred_element_type=F32)
        grown = lax.dot_general(
            placed.astype(BF16), spread, (((0,), (0,)), ((), ())), preferred_element_type=F32
        )
        sg_now = dot(jnp.where(diagonal, grown, 0.0).astype(BF16), back.astype(BF16))
        if k == 0:
            out_ref[...] = out_now
            sg_ref[...] = sg_now
        else:
            out_ref[...] += out_now
            sg_ref[...] += sg_now

    ordered = lax.dot_general(
        one_hot((used, 256), row_of_share),
        out_ref[...].astype(BF16),
        (((0,), (0,)), ((), ())),
        preferred_element_type=F32,
    )

    def output_rows(n):
        o, q = n // 4, n % 4
        cols = slice(128 * (q // 2), 128 * (q // 2 + 1))
        re = ordered[32 * o : 32 * o + 16, cols]
        im = ordered[32 * o + 16 : 32 * o + 32, cols]
        return jnp.where(keep, re, swap64(im)) if q % 2 == 0 else jnp.where(keep, swap64(re), im)

    def field_rows(n):
        r, h = n // 2, n % 2
        return sg_ref[24 * r : 24 * (r + 1), 128 * h : 128 * (h + 1)]

    for a in range(LANES):
        for rows, make in ((slice(0, M16), output_rows), (slice(M16, CHUNK_MID), field_rows)):
            first, second = make(a), make(a + LANES)
            mine_ref[a, rows, :] = jnp.where(low, first, second).astype(BF16)
            other_ref[a, rows, :] = jnp.where(low, second, first).astype(BF16)


def merge_body(band_ref, mine_ref, got_ref, o_ref):
    low = band_ref[0, 0] == 0
    for a in range(LANES):
        mine, got = mine_ref[a, 0:CHUNK_MID, :].astype(F32), got_ref[a, 0:CHUNK_MID, :].astype(F32)
        o_ref[a, 0:CHUNK_MID, :] = jnp.where(low, mine, got).astype(BF16)
        o_ref[a, CHUNK_MID : 2 * CHUNK_MID, :] = jnp.where(low, got, mine).astype(BF16)
        mine, got = mine_ref[a, CHUNK_MID:, :].astype(F32), got_ref[a, CHUNK_MID:, :].astype(F32)
        o_ref[a, 2 * CHUNK_MID :, :] = (mine + got).astype(BF16)


def fields_body(r_ref, w_ref, v_hbm, o_ref, v_ref, sems):
    (copy,) = fetch((v_hbm,), (v_ref,), sems)
    fields, outs = [], []
    for e in range(BANDS):
        start = CHUNK_MID * e
        sg = r_ref[:, start + M16 : start + CHUNK_MID, :].reshape(LANES * 2 * M12, 128)
        fields.append(dot(w_ref[e], sg))
    for side in range(2):
        lanes = slice(HALF * side, HALF * (side + 1))
        field = fields[0] + fields[1] if side == 0 else fields[0] - fields[1]
        o_ref[lanes, 0:WROWS, :] = field.astype(BF16).reshape(HALF, WROWS, 128)
    copy.wait()
    for e in range(BANDS):
        start = CHUNK_MID * e
        c = r_ref[:, start : start + M16, :].reshape(LANES * M16, 128).astype(F32)
        turned = swap64(c)
        keep = low_half(c.shape)
        both = jnp.concatenate([jnp.where(keep, c, turned), jnp.where(keep, turned, c)], axis=0).astype(BF16)
        got = dot(v_ref[e], both)
        count = HALF * VROWS
        outs.append(jnp.where(low_half((count, 128)), got[:count], got[count:]))
    for side in range(2):
        lanes = slice(HALF * side, HALF * (side + 1))
        out = outs[0] + outs[1] if side == 0 else outs[0] - outs[1]
        o_ref[lanes, WROWS:CHUNK_IN, :] = out.astype(BF16).reshape(HALF, VROWS, 128)


def unpack_body(r_ref, f_ref, c_ref, flat_ref):
    for j in range(6):
        count = min(128, 8 * WPART - 128 * j)
        halves = [
            jnp.concatenate([r_ref[2 * r + h, 16 * j : 16 * (j + 1), :] for r in range(8)], axis=0)
            for h in range(2)
        ]
        order = one_hot((128, count), row_of_latitude)
        block = lax.dot_general(
            order, jnp.concatenate(halves, axis=1), (((0,), (0,)), ((), ())), preferred_element_type=F32
        )
        f_ref[128 * j : 128 * j + count, :] = block.astype(BF16)
    keep = low_half((VROWS, 128))
    for o in range(4):
        for i in range(2):
            even = r_ref[4 * o + 2 * i, WROWS:CHUNK_IN, :].astype(F32)
            odd = r_ref[4 * o + 2 * i + 1, WROWS:CHUNK_IN, :].astype(F32)
            cols = slice(128 * i, 128 * (i + 1))
            flat_ref[48 * o : 48 * o + 24, cols] = jnp.where(keep, even, swap64(odd))
            flat_ref[48 * o + 24 : 48 * o + 48, cols] = jnp.where(keep, swap64(even), odd)
    rows = lax.dot_general(
        one_hot((192, 192), row_of_output),
        flat_ref[...].astype(BF16),
        (((0,), (0,)), ((), ())),
        preferred_element_type=F32,
    )
    for v in range(VPART):
        c_ref[v] = rows[4 * v : 4 * (v + 1), :].astype(BF16)


def swap_bands(value):
    return lax.ppermute(value, "polar", [(0, 1), (1, 0)])


def local(fields, basis_spectra, support, weights, out_grad):
    band = lax.axis_index("polar").astype(jnp.int32)
    low = band == 0
    spot = jnp.stack([band, lax.axis_index("azimuth").astype(jnp.int32)]).reshape(1, 2)
    wide, narrow = factor_tables()
    dma = pltpu.SemaphoreType.DMA
    (sent,) = call(
        pack_body,
        [HBM, HBM],
        [((LANES, CHUNK_IN, 128), BF16)],
        scratch=[
            pltpu.VMEM((8 * WPART, C), BF16),
            pltpu.VMEM((VPART, 4, C), BF16),
            pltpu.VMEM((192, C), F32),
            dma((2,)),
        ],
    )(
        in_hbm(jnp.swapaxes(fields[0], 0, 1).reshape(8 * WPART, C)), in_hbm(jnp.swapaxes(out_grad[0], 0, 1))
    )
    landed = lax.all_to_all(sent, "azimuth", split_axis=0, concat_axis=0, tiled=True)

    filters, limits, sent = lax.optimization_barrier((basis_spectra, support, sent))
    mine, other = call(
        filter_body,
        [SMEM, SMEM, HBM],
        [((K * SUPPORT * 4, 128), BF16)] * 2,
        scratch=[pltpu.VMEM((K * SUPPORT, 4, WOUT), BF16), pltpu.VMEM((184, WOUT), F32), dma((1,))],
    )(spot, limits, in_hbm(jnp.swapaxes(filters, 1, 2).reshape(K * SUPPORT, 4, WOUT)))
    got = swap_bands(other)
    factors = [a for a in wide + narrow]
    held = [pltpu.VMEM(a.shape, F32) for a in factors]
    factors, sent = lax.optimization_barrier(([jnp.asarray(a) for a in factors], sent))
    flat, inv_t = call(
        flipped_table_body,
        [HBM] * 8,
        [((2, 384, 768), BF16), ((2, 512, 384), BF16)],
        nbytes=5 << 20,
        scratch=held + [pltpu.VMEM((2, 768, 384), BF16), pltpu.VMEM((2, 384, 512), BF16), dma((8,))],
    )(*[in_hbm(a) for a in factors])

    landed, mine, got = lax.optimization_barrier((landed, mine, got))
    (sent,) = call(spectra_body, [VMEM] * 3, [((SHARES, CHUNK_MID, 128), BF16)], flops=300 << 20)(landed, flat, inv_t)
    landed = lax.all_to_all(sent, JOINT, split_axis=0, concat_axis=0, tiled=True)
    mine, got, sent = lax.optimization_barrier((mine, got, sent))
    placed, staged = call(
        mixing_body, [SMEM, VMEM, VMEM, HBM], [((K * 16, HIN * 2 * M12), F32), ((K, C, C), BF16)], scratch=[dma((1,))]
    )(spot, mine, got, in_hbm(weights))

    chunk = (LANES, CHUNK_MID + 16 * K, 128)
    mine, other = call(
        middle_body,
        [SMEM, VMEM, VMEM, VMEM],
        [(chunk, BF16), (chunk, BF16)],
        flops=2 << 30,
        nbytes=3 << 20,
        scratch=[
            pltpu.VMEM((256, 256), BF16),
            pltpu.VMEM((192, 256), F32),
            pltpu.VMEM((384, 256), F32),
        ],
    )(spot, landed.reshape(HIN, 2, CHUNK_MID, 128), placed, staged)
    factors, mine, other = lax.optimization_barrier((factors, mine, other))
    got = swap_bands(other)
    tall, inv = call(
        table_body,
        [HBM] * 8,
        [((2, 768, 384), BF16), pltpu.HBM((2, 384, 512), BF16)],
        nbytes=5 << 20,
        scratch=held + [pltpu.VMEM((2, 384, 512), BF16), dma((8,))],
        out_places=[VMEM, HBM],
    )(*[in_hbm(a) for a in factors])
    got, tall, inv = lax.optimization_barrier((got, tall, inv))
    (sent,) = call(merge_body, [SMEM, VMEM, VMEM], [((LANES, CHUNK_OUT, 128), BF16)], nbytes=2 << 20)(spot, mine, got)
    landed = lax.all_to_all(sent, "azimuth", split_axis=0, concat_axis=0, tiled=True)

    members = lax.axis_size("ens")

    def send(value, offset_even, offset_odd):
        offsets = (offset_even, offset_odd)
        pairs = [(i, (i + offsets[i % 2]) % members) for i in range(members)]
        return lax.ppermute(value, "ens", pairs)

    half = jnp.sum(landed[:, 2 * CHUNK_MID :, :].astype(F32), axis=0).astype(BF16)
    got = send(half, 1, -1)
    pair = (half.astype(F32) + got.astype(F32)).astype(BF16)
    beside = send(pair, -1, 1)
    across = send(beside, 2, -2)
    behind = send(beside, 1, -1)
    half = (pair.astype(F32) + across.astype(F32)) + (beside.astype(F32) + behind.astype(F32))
    far = swap_bands(half)
    (sent,) = call(
        fields_body,
        [VMEM, VMEM, HBM],
        [((LANES, CHUNK_IN, 128), BF16)],
        flops=300 << 20,
        scratch=[pltpu.VMEM((2, 384, 512), BF16), dma((1,))],
    )(landed, tall, in_hbm(inv))
    landed = lax.all_to_all(sent, "azimuth", split_axis=0, concat_axis=0, tiled=True)
    field_grad, conv_out = call(
        unpack_body, [VMEM], [((8 * WPART, C), BF16), ((VPART, 4, C), BF16)], scratch=[pltpu.VMEM((192, C), F32)]
    )(landed)
    weight_grad = jnp.concatenate([jnp.where(low, half, far), jnp.where(low, far, half)], axis=1)
    field_grad = jnp.swapaxes(field_grad.reshape(WPART, 8, C), 0, 1)
    return (jnp.swapaxes(conv_out, 0, 1)[None], field_grad[None], weight_grad.reshape(K, 16, C))


def solution(mesh):
    placed = (
        P("ens", "polar", "azimuth", None),
        P(None, "polar", None, None),
        P("polar", None),
        P(),
        P("ens", "polar", "azimuth", None),
    )
    return jax.shard_map(
        local,
        mesh=mesh,
        in_specs=placed,
        out_specs=(
            P("ens", "polar", "azimuth", None),
            P("ens", "polar", "azimuth", None),
            P(None, "azimuth", None),
        ),
        check_vma=False,
    )
```

```python
import math

import jax
import jax.numpy as jnp
import numpy as np
from jax import lax
from jax.experimental import pallas as pl
from jax.experimental.pallas import tpu as pltpu
from jax.sharding import PartitionSpec as P


WIN, WOUT, MODES = 1440, 720, 360
K, C, SUPPORT = 9, 256, 5
HOUT, HIN = 8, 16
LANES, BANDS = 16, 2
SHARES = LANES * BANDS
HALF = LANES // 2
M12, M16 = 12, 16
WPART, WROWS = 90, 96
VPART, VROWS = 45, 24
CHUNK_IN = WROWS + VROWS
CHUNK_MID = M16 + 2 * M12
CHUNK_OUT = 2 * CHUNK_MID + 16 * K
F32, BF16 = jnp.float32, jnp.bfloat16
JOINT = ("polar", "azimuth")


def factor_tables():
    def build(slots, part, steps, period, scale):
        mode_all, keep, imag = slots
        parts = []
        for e in range(BANDS):
            mode = mode_all + e
            ok = keep & (mode < MODES)
            alpha = 2 * math.pi * ((mode[None, :] * (part * np.arange(HALF)[:, None])) % period) / period
            beta = 2 * math.pi * ((mode[None, :] * steps[:, None]) % period) / period
            ok = ok[None, :] & (steps[:, None] < part)
            size = np.where(mode == 0, 1.0, 2.0)[None, :] / WIN if scale else 1.0
            parts.append(
                (
                    np.where(imag[None, :], -np.sin(alpha), np.cos(alpha)),
                    np.where(imag[None, :], -np.cos(alpha), -np.sin(alpha)),
                    np.where(ok, size * np.cos(beta), 0.0),
                    np.where(ok, size * np.sin(beta), 0.0),
                )
            )
        return [np.stack(group).astype(np.float32) for group in zip(*parts)]

    a, ri, i = np.meshgrid(np.arange(LANES), np.arange(2), np.arange(M12), indexing="ij")
    slots = ((2 * (M12 * a + i)).reshape(-1), np.ones(a.size, bool), ri.reshape(-1) == 1)
    wide = build(slots, WPART, np.arange(WROWS), WIN, False)
    ri, a, i = np.meshgrid(np.arange(2), np.arange(LANES), np.arange(M16), indexing="ij")
    slots = ((2 * (M12 * a + i)).reshape(-1), i.reshape(-1) < M12, ri.reshape(-1) == 1)
    narrow = build(slots, VPART, np.arange(2 * VROWS), WOUT, True)
    return wide, narrow


HBM = pl.BlockSpec(memory_space=pltpu.HBM)
VMEM = pl.BlockSpec(memory_space=pltpu.VMEM)
SMEM = pl.BlockSpec(memory_space=pltpu.SMEM)


def call(body, places, outs, flops=0, scratch=(), nbytes=1 << 20, vmem=16, out_places=None):
    return pl.pallas_call(
        body,
        out_shape=[jax.ShapeDtypeStruct(*o) if isinstance(o, tuple) else o for o in outs],
        in_specs=places,
        out_specs=out_places or [VMEM] * len(outs),
        scratch_shapes=list(scratch),
        compiler_params=pltpu.CompilerParams(vmem_limit_bytes=vmem << 20),
        cost_estimate=pl.CostEstimate(flops=flops, bytes_accessed=nbytes, transcendentals=0),
    )


def in_hbm(value):
    return pltpu.with_memory_space_constraint(value, pltpu.HBM)


def fetch(sources, targets, sems):
    copies = [pltpu.make_async_copy(s, t, sems.at[n]) for n, (s, t) in enumerate(zip(sources, targets))]
    for copy in copies:
        copy.start()
    return copies


def low_half(shape):
    return lax.broadcasted_iota(jnp.int32, shape, len(shape) - 1) < 64


def swap64(value):
    return pltpu.roll(value, 64, value.ndim - 1)


def dot(a, b):
    return jnp.dot(a, b, preferred_element_type=F32)


def one_hot(shape, row_of_column):
    row = lax.broadcasted_iota(jnp.int32, shape, 0)
    column = lax.broadcasted_iota(jnp.int32, shape, 1)
    return jnp.where(row == row_of_column(column), 1.0, 0.0).astype(BF16)


def row_of_latitude(column):
    return 16 * (column % 8) + column // 8


def row_of_output(column):
    return 48 * (column % 4) + column // 4


def pack_body(f_hbm, g_hbm, o_ref, f_ref, g_ref, flat_ref, sems):
    copies = fetch((f_hbm, g_hbm), (f_ref, g_ref), sems)
    copies[0].wait()
    for j in range(6):
        count = min(128, 8 * WPART - 128 * j)
        order = one_hot((128, count), row_of_latitude)
        block = dot(order, f_ref[128 * j : 128 * j + count, :]).astype(BF16)
        for r in range(8):
            for h in range(2):
                piece = block[16 * r : 16 * (r + 1), 128 * h : 128 * (h + 1)]
                o_ref[2 * r + h, 16 * j : 16 * (j + 1), :] = piece
    copies[1].wait()
    for v in range(VPART):
        flat_ref[4 * v : 4 * (v + 1), :] = g_ref[v].astype(F32)
    flat_ref[4 * VPART : 192, :] = jnp.zeros((192 - 4 * VPART, C), F32)
    rows = dot(one_hot((192, 192), row_of_output), flat_ref[...].astype(BF16))
    keep = low_half((VROWS, 128))
    for o in range(4):
        for i in range(2):
            cols = slice(128 * i, 128 * (i + 1))
            top, bottom = rows[48 * o : 48 * o + 24, cols], rows[48 * o + 24 : 48 * o + 48, cols]
            even = jnp.where(keep, top, swap64(bottom))
            odd = jnp.where(keep, swap64(top), bottom)
            o_ref[4 * o + 2 * i, WROWS:CHUNK_IN, :] = even.astype(BF16)
            o_ref[4 * o + 2 * i + 1, WROWS:CHUNK_IN, :] = odd.astype(BF16)


def flip(source, target, rows, columns):
    for i in range(rows // 128):
        for j in range(columns // 128):
            piece = source[128 * i : 128 * (i + 1), 128 * j : 128 * (j + 1)].astype(F32)
            target[128 * j : 128 * (j + 1), 128 * i : 128 * (i + 1)] = piece.T.astype(BF16)


def fill_wide(w, w_ref):
    for e in range(BANDS):
        for b in range(HALF):
            one, two = w[0][e, b : b + 1, :], w[1][e, b : b + 1, :]
            block = one * w[2][e] + two * w[3][e]
            w_ref[e, WROWS * b : WROWS * (b + 1), :] = block.astype(BF16)


def fill_narrow(v, v_ref):
    for e in range(BANDS):
        for b in range(HALF):
            one, two = v[0][e, b : b + 1, :], v[1][e, b : b + 1, :]
            for part in range(2):
                rows = slice(VROWS * part, VROWS * (part + 1))
                block = one * v[2][e, rows, :] + two * v[3][e, rows, :]
                start = VROWS * (HALF * part + b)
                v_ref[e, start : start + VROWS, :] = block.astype(BF16)


def table_body(*refs):
    factors, (w_ref, v_hbm) = refs[:8], refs[8:10]
    held, (v_ref, sems, out_sem) = refs[10:18], refs[18:]
    copies = fetch(factors[4:] + factors[:4], held[4:] + held[:4], sems)
    for copy in copies[:4]:
        copy.wait()
    fill_narrow(held[4:], v_ref)
    (out,) = fetch((v_ref,), (v_hbm,), out_sem)
    for copy in copies[4:]:
        copy.wait()
    fill_wide(held[:4], w_ref)
    out.wait()


def flipped_table_body(*refs):
    factors, (wt_ref, vt_ref) = refs[:8], refs[8:10]
    held, (w_ref, v_ref, sems) = refs[10:18], refs[18:]
    for copy in fetch(factors, held, sems):
        copy.wait()
    fill_wide(held[:4], w_ref)
    fill_narrow(held[4:], v_ref)
    for e in range(BANDS):
        flip(w_ref.at[e], wt_ref.at[e], HALF * WROWS, 2 * LANES * M12)
        flip(v_ref.at[e], vt_ref.at[e], 2 * HALF * VROWS, 2 * LANES * M16)


def spectra_body(r_ref, wt_ref, vt_ref, o_ref):
    left = r_ref[0:HALF, 0:WROWS, :].reshape(HALF * WROWS, 128).astype(F32)
    right = r_ref[HALF:LANES, 0:WROWS, :].reshape(HALF * WROWS, 128).astype(F32)
    g_left = r_ref[0:HALF, WROWS:CHUNK_IN, :].reshape(HALF * VROWS, 128).astype(F32)
    g_right = r_ref[HALF:LANES, WROWS:CHUNK_IN, :].reshape(HALF * VROWS, 128).astype(F32)
    keep = low_half((HALF * VROWS, 128))
    for e in range(BANDS):
        x = (left + right if e == 0 else left - right).astype(BF16)
        g = g_left + g_right if e == 0 else g_left - g_right
        turned = swap64(g)
        both = jnp.concatenate([jnp.where(keep, g, turned), jnp.where(keep, turned, g)], axis=0).astype(BF16)
        shares = slice(LANES * e, LANES * (e + 1))
        o_ref[shares, M16:CHUNK_MID, :] = dot(wt_ref[e], x).astype(BF16).reshape(LANES, 2 * M12, 128)
        got = dot(vt_ref[e], both)
        count = LANES * M16
        out = jnp.where(low_half((count, 128)), got[:count], got[count:])
        o_ref[shares, 0:M16, :] = out.astype(BF16).reshape(LANES, M16, 128)


def filter_body(spot_ref, support_ref, p_hbm, mine_ref, other_ref, p_ref, flat_ref, sems):
    (copy,) = fetch((p_hbm,), (p_ref,), sems)
    rows = K * SUPPORT * 4
    band, start = spot_ref[0, 0], 2 * M12 * spot_ref[0, 1]
    line = lax.broadcasted_iota(jnp.int32, (WOUT, 128), 0)
    slot = lax.broadcasted_iota(jnp.int32, (WOUT, 128), 1)
    place = slot % 64
    parity = jnp.where(slot < 64, band, 1 - band)
    mode = start + 2 * (place % M12) + parity
    hit = (line == mode + MODES * (place // M12)) & (place < 2 * M12) & (mode < MODES)
    chosen = jnp.where(hit, 1.0, 0.0).astype(BF16)
    row = lax.broadcasted_iota(jnp.int32, (rows, 128), 0)
    window, output = (row // 4) % SUPPORT, row % 4
    first = jnp.zeros((rows, 128), jnp.int32)
    last = jnp.zeros((rows, 128), jnp.int32)
    for o in range(4):
        first = jnp.where(output == o, support_ref[o, 0], first)
        last = jnp.where(output == o, support_ref[o, 1], last)
    copy.wait()
    for n in range(K * SUPPORT):
        flat_ref[4 * n : 4 * (n + 1), :] = p_ref[n].astype(F32)
    got = dot(flat_ref[0:rows, :].astype(BF16), chosen)
    got = jnp.where((window >= first) & (window <= last), got, 0.0)
    mine_ref[...] = got.astype(BF16)
    other_ref[...] = swap64(got).astype(BF16)


def mixing_body(spot_ref, mine_ref, got_ref, w_hbm, p_ref, w_ref, sems):
    (copy,) = fetch((w_hbm,), (w_ref,), sems)
    rows, width, count = K * 16, HIN * 2 * M12, K * SUPPORT * 4
    low = spot_ref[0, 0] == 0
    mine, got = mine_ref[...].astype(F32), got_ref[...].astype(F32)
    halves = (jnp.where(low, mine, got).astype(BF16), jnp.where(low, got, mine).astype(BF16))
    x = lax.broadcasted_iota(jnp.int32, (128, width), 0)
    lane = lax.broadcasted_iota(jnp.int32, (128, width), 1)
    same, cross = lane % M12, lane % (2 * M12) < M12
    straight = x == same + jnp.where(cross, 0, M12)
    turned = x == same + jnp.where(cross, M12, 0)
    tiles = (
        jnp.where(straight, jnp.where(cross, 1.0, -1.0), 0.0).astype(BF16),
        jnp.where(turned, 1.0, 0.0).astype(BF16),
    )
    row = lax.broadcasted_iota(jnp.int32, (count, width), 0)
    lane = lax.broadcasted_iota(jnp.int32, (count, width), 1)
    reach = 2 * (row % 4) + (row // 4) % SUPPORT - 2 - lane // (2 * M12)
    target = lax.broadcasted_iota(jnp.int32, (rows, count), 0)
    source = lax.broadcasted_iota(jnp.int32, (rows, count), 1)
    key = target - 16 * (source // 20) - 2 * (source % 4)
    total = jnp.zeros((rows, width), F32)
    for half in range(2):
        for ri in range(2):
            spread = dot(halves[half], tiles[ri])
            spread = jnp.where(reach == -8 * half, spread, 0.0).astype(BF16)
            collect = jnp.where(key == 8 * half + ri, 1.0, 0.0).astype(BF16)
            total = total + dot(collect, spread)
    p_ref[...] = total
    copy.wait()


def row_of_share(column):
    return 16 * (column % 16) + column // 16


def middle_body(band_ref, r_ref, p_ref, w_ref, mine_ref, other_ref, gs_ref, out_ref, sg_ref):
    keep = low_half((M16, 128))
    for o in range(HOUT):
        for i in range(2):
            first = r_ref[2 * o + i, 0, 0:M16, :].astype(F32)
            second = r_ref[2 * o + i, 1, 0:M16, :].astype(F32)
            cols = slice(128 * i, 128 * (i + 1))
            gs_ref[32 * o : 32 * o + 16, cols] = jnp.where(keep, first, swap64(second)).astype(BF16)
            gs_ref[32 * o + 16 : 32 * o + 32, cols] = jnp.where(keep, swap64(first), second).astype(BF16)
    used = M12 * 16
    gs = dot(one_hot((used, 256), row_of_share), gs_ref[...]).astype(BF16)
    width = HIN * 2 * M12
    x = jnp.concatenate(
        [r_ref[:, h, M16:CHUNK_MID, :].reshape(width, 128) for h in range(2)], axis=1
    )
    lane_mode = lax.broadcasted_iota(jnp.int32, (16, width), 1) % M12
    diagonal = (
        lax.broadcasted_iota(jnp.int32, (width, used), 0) % M12
        == lax.broadcasted_iota(jnp.int32, (width, used), 1) // 16
    )
    spread = one_hot((16, used), lambda column: column % 16)
    low = band_ref[0, 0] == 0

    for k in range(K):
        placed = p_ref[16 * k : 16 * (k + 1), :]
        blocks = [jnp.where(lane_mode == m, placed, 0.0).astype(BF16) for m in range(M12)]
        mixed = dot(jnp.concatenate(blocks, axis=0), x).astype(BF16)
        out_now = dot(mixed, w_ref[k])
        grad = lax.dot_general(mixed, gs, (((0,), (0,)), ((), ())), preferred_element_type=F32)
        where_to = (slice(None), slice(CHUNK_MID + 16 * k, CHUNK_MID + 16 * (k + 1)), slice(None))
        shape = (LANES, 16, 128)
        mine_ref[where_to] = jnp.where(low, grad[:, :128], grad[:, 128:]).astype(BF16).reshape(shape)
        other_ref[where_to] = jnp.where(low, grad[:, 128:], grad[:, :128]).astype(BF16).reshape(shape)
        back = lax.dot_general(gs, w_ref[k], (((1,), (1,)), ((), ())), preferred_element_type=F32)
        grown = lax.dot_general(
            placed.astype(BF16), spread, (((0,), (0,)), ((), ())), preferred_element_type=F32
        )
        sg_now = dot(jnp.where(diagonal, grown, 0.0).astype(BF16), back.astype(BF16))
        if k == 0:
            out_ref[...] = out_now
            sg_ref[...] = sg_now
        else:
            out_ref[...] += out_now
            sg_ref[...] += sg_now

    ordered = lax.dot_general(
        one_hot((used, 256), row_of_share),
        out_ref[...].astype(BF16),
        (((0,), (0,)), ((), ())),
        preferred_element_type=F32,
    )

    def output_rows(n):
        o, q = n // 4, n % 4
        cols = slice(128 * (q // 2), 128 * (q // 2 + 1))
        re = ordered[32 * o : 32 * o + 16, cols]
        im = ordered[32 * o + 16 : 32 * o + 32, cols]
        return jnp.where(keep, re, swap64(im)) if q % 2 == 0 else jnp.where(keep, swap64(re), im)

    def field_rows(n):
        r, h = n // 2, n % 2
        return sg_ref[24 * r : 24 * (r + 1), 128 * h : 128 * (h + 1)]

    for a in range(LANES):
        for rows, make in ((slice(0, M16), output_rows), (slice(M16, CHUNK_MID), field_rows)):
            first, second = make(a), make(a + LANES)
            mine_ref[a, rows, :] = jnp.where(low, first, second).astype(BF16)
            other_ref[a, rows, :] = jnp.where(low, second, first).astype(BF16)


def merge_body(band_ref, mine_ref, got_ref, o_ref):
    low = band_ref[0, 0] == 0
    for a in range(LANES):
        mine, got = mine_ref[a, 0:CHUNK_MID, :].astype(F32), got_ref[a, 0:CHUNK_MID, :].astype(F32)
        o_ref[a, 0:CHUNK_MID, :] = jnp.where(low, mine, got).astype(BF16)
        o_ref[a, CHUNK_MID : 2 * CHUNK_MID, :] = jnp.where(low, got, mine).astype(BF16)
        mine, got = mine_ref[a, CHUNK_MID:, :].astype(F32), got_ref[a, CHUNK_MID:, :].astype(F32)
        o_ref[a, 2 * CHUNK_MID :, :] = (mine + got).astype(BF16)


def fields_body(r_ref, w_ref, v_hbm, o_ref, v_ref, sems):
    copies = fetch((v_hbm.at[0], v_hbm.at[1]), (v_ref.at[0], v_ref.at[1]), sems)
    fields, outs = [], []
    for e in range(BANDS):
        start = CHUNK_MID * e
        sg = r_ref[:, start + M16 : start + CHUNK_MID, :].reshape(LANES * 2 * M12, 128)
        fields.append(dot(w_ref[e], sg))
    for side in range(2):
        lanes = slice(HALF * side, HALF * (side + 1))
        field = fields[0] + fields[1] if side == 0 else fields[0] - fields[1]
        o_ref[lanes, 0:WROWS, :] = field.astype(BF16).reshape(HALF, WROWS, 128)
    for e in range(BANDS):
        copies[e].wait()
        start = CHUNK_MID * e
        c = r_ref[:, start : start + M16, :].reshape(LANES * M16, 128).astype(F32)
        turned = swap64(c)
        keep = low_half(c.shape)
        both = jnp.concatenate([jnp.where(keep, c, turned), jnp.where(keep, turned, c)], axis=0).astype(BF16)
        got = dot(v_ref[e], both)
        count = HALF * VROWS
        outs.append(jnp.where(low_half((count, 128)), got[:count], got[count:]))
    for side in range(2):
        lanes = slice(HALF * side, HALF * (side + 1))
        out = outs[0] + outs[1] if side == 0 else outs[0] - outs[1]
        o_ref[lanes, WROWS:CHUNK_IN, :] = out.astype(BF16).reshape(HALF, VROWS, 128)


def unpack_body(r_ref, f_ref, c_ref, flat_ref):
    for j in range(6):
        count = min(128, 8 * WPART - 128 * j)
        halves = [
            jnp.concatenate([r_ref[2 * r + h, 16 * j : 16 * (j + 1), :] for r in range(8)], axis=0)
            for h in range(2)
        ]
        order = one_hot((128, count), row_of_latitude)
        block = lax.dot_general(
            order, jnp.concatenate(halves, axis=1), (((0,), (0,)), ((), ())), preferred_element_type=F32
        )
        f_ref[128 * j : 128 * j + count, :] = block.astype(BF16)
    keep = low_half((VROWS, 128))
    for o in range(4):
        for i in range(2):
            even = r_ref[4 * o + 2 * i, WROWS:CHUNK_IN, :].astype(F32)
            odd = r_ref[4 * o + 2 * i + 1, WROWS:CHUNK_IN, :].astype(F32)
            cols = slice(128 * i, 128 * (i + 1))
            flat_ref[48 * o : 48 * o + 24, cols] = jnp.where(keep, even, swap64(odd))
            flat_ref[48 * o + 24 : 48 * o + 48, cols] = jnp.where(keep, swap64(even), odd)
    rows = lax.dot_general(
        one_hot((192, 192), row_of_output),
        flat_ref[...].astype(BF16),
        (((0,), (0,)), ((), ())),
        preferred_element_type=F32,
    )
    for v in range(VPART):
        c_ref[v] = rows[4 * v : 4 * (v + 1), :].astype(BF16)


def swap_bands(value):
    return lax.ppermute(value, "polar", [(0, 1), (1, 0)])


def local(fields, basis_spectra, support, weights, out_grad):
    band = lax.axis_index("polar").astype(jnp.int32)
    low = band == 0
    spot = jnp.stack([band, lax.axis_index("azimuth").astype(jnp.int32)]).reshape(1, 2)
    wide, narrow = factor_tables()
    dma = pltpu.SemaphoreType.DMA
    (sent,) = call(
        pack_body,
        [HBM, HBM],
        [((LANES, CHUNK_IN, 128), BF16)],
        scratch=[
            pltpu.VMEM((8 * WPART, C), BF16),
            pltpu.VMEM((VPART, 4, C), BF16),
            pltpu.VMEM((192, C), F32),
            dma((2,)),
        ],
    )(
        in_hbm(jnp.swapaxes(fields[0], 0, 1).reshape(8 * WPART, C)), in_hbm(jnp.swapaxes(out_grad[0], 0, 1))
    )
    landed = lax.all_to_all(sent, "azimuth", split_axis=0, concat_axis=0, tiled=True)

    filters, limits, sent = lax.optimization_barrier((basis_spectra, support, sent))
    mine, other = call(
        filter_body,
        [SMEM, SMEM, HBM],
        [((K * SUPPORT * 4, 128), BF16)] * 2,
        scratch=[pltpu.VMEM((K * SUPPORT, 4, WOUT), BF16), pltpu.VMEM((184, WOUT), F32), dma((1,))],
    )(spot, limits, in_hbm(jnp.swapaxes(filters, 1, 2).reshape(K * SUPPORT, 4, WOUT)))
    got = swap_bands(other)
    factors = [a for a in wide + narrow]
    held = [pltpu.VMEM(a.shape, F32) for a in factors]
    factors, sent = lax.optimization_barrier(([jnp.asarray(a) for a in factors], sent))
    flat, inv_t = call(
        flipped_table_body,
        [HBM] * 8,
        [((2, 384, 768), BF16), ((2, 512, 384), BF16)],
        nbytes=5 << 20,
        scratch=held + [pltpu.VMEM((2, 768, 384), BF16), pltpu.VMEM((2, 384, 512), BF16), dma((8,))],
    )(*[in_hbm(a) for a in factors])

    landed, mine, got = lax.optimization_barrier((landed, mine, got))
    (sent,) = call(spectra_body, [VMEM] * 3, [((SHARES, CHUNK_MID, 128), BF16)], flops=300 << 20)(landed, flat, inv_t)
    landed = lax.all_to_all(sent, JOINT, split_axis=0, concat_axis=0, tiled=True)
    mine, got, sent = lax.optimization_barrier((mine, got, sent))
    placed, staged = call(
        mixing_body, [SMEM, VMEM, VMEM, HBM], [((K * 16, HIN * 2 * M12), F32), ((K, C, C), BF16)], scratch=[dma((1,))]
    )(spot, mine, got, in_hbm(weights))

    chunk = (LANES, CHUNK_MID + 16 * K, 128)
    mine, other = call(
        middle_body,
        [SMEM, VMEM, VMEM, VMEM],
        [(chunk, BF16), (chunk, BF16)],
        flops=2 << 30,
        nbytes=3 << 20,
        scratch=[
            pltpu.VMEM((256, 256), BF16),
            pltpu.VMEM((192, 256), F32),
            pltpu.VMEM((384, 256), F32),
        ],
    )(spot, landed.reshape(HIN, 2, CHUNK_MID, 128), placed, staged)
    factors, mine, other = lax.optimization_barrier((factors, mine, other))
    got = swap_bands(other)
    tall, inv = call(
        table_body,
        [HBM] * 8,
        [((2, 768, 384), BF16), pltpu.HBM((2, 384, 512), BF16)],
        nbytes=5 << 20,
        scratch=held + [pltpu.VMEM((2, 384, 512), BF16), dma((8,)), dma((1,))],
        out_places=[VMEM, HBM],
    )(*[in_hbm(a) for a in factors])
    got, tall, inv = lax.optimization_barrier((got, tall, inv))
    (sent,) = call(merge_body, [SMEM, VMEM, VMEM], [((LANES, CHUNK_OUT, 128), BF16)], nbytes=2 << 20)(spot, mine, got)
    landed = lax.all_to_all(sent, "azimuth", split_axis=0, concat_axis=0, tiled=True)

    members = lax.axis_size("ens")

    def send(value, offset_even, offset_odd):
        offsets = (offset_even, offset_odd)
        pairs = [(i, (i + offsets[i % 2]) % members) for i in range(members)]
        return lax.ppermute(value, "ens", pairs)

    half = jnp.sum(landed[:, 2 * CHUNK_MID :, :].astype(F32), axis=0).astype(BF16)
    got = send(half, 1, -1)
    pair = (half.astype(F32) + got.astype(F32)).astype(BF16)
    beside = send(pair, -1, 1)
    behind = send(pair, -2, 2)
    across = send(beside, 2, -2)
    half = (pair.astype(F32) + across.astype(F32)) + (beside.astype(F32) + behind.astype(F32))
    far = swap_bands(half)
    (sent,) = call(
        fields_body,
        [VMEM, VMEM, HBM],
        [((LANES, CHUNK_IN, 128), BF16)],
        flops=300 << 20,
        scratch=[pltpu.VMEM((2, 384, 512), BF16), dma((2,))],
    )(landed, tall, in_hbm(inv))
    landed = lax.all_to_all(sent, "azimuth", split_axis=0, concat_axis=0, tiled=True)
    field_grad, conv_out = call(
        unpack_body, [VMEM], [((8 * WPART, C), BF16), ((VPART, 4, C), BF16)], scratch=[pltpu.VMEM((192, C), F32)]
    )(landed)
    weight_grad = jnp.concatenate([jnp.where(low, half, far), jnp.where(low, far, half)], axis=1)
    field_grad = jnp.swapaxes(field_grad.reshape(WPART, 8, C), 0, 1)
    return (jnp.swapaxes(conv_out, 0, 1)[None], field_grad[None], weight_grad.reshape(K, 16, C))


def solution(mesh):
    placed = (
        P("ens", "polar", "azimuth", None),
        P(None, "polar", None, None),
        P("polar", None),
        P(),
        P("ens", "polar", "azimuth", None),
    )
    return jax.shard_map(
        local,
        mesh=mesh,
        in_specs=placed,
        out_specs=(
            P("ens", "polar", "azimuth", None),
            P("ens", "polar", "azimuth", None),
            P(None, "azimuth", None),
        ),
        check_vma=False,
    )
```

```python
import math

import jax
import jax.numpy as jnp
import numpy as np
from jax import lax
from jax.experimental import pallas as pl
from jax.experimental.pallas import tpu as pltpu
from jax.sharding import PartitionSpec as P


WIN, WOUT, MODES = 1440, 720, 360
K, C, SUPPORT = 9, 256, 5
HOUT, HIN = 8, 16
LANES, BANDS = 16, 2
SHARES = LANES * BANDS
HALF = LANES // 2
M12, M16 = 12, 16
WPART, WROWS = 90, 96
VPART, VROWS = 45, 24
CHUNK_IN = WROWS + VROWS
CHUNK_MID = M16 + 2 * M12
CHUNK_OUT = 2 * CHUNK_MID + 16 * K
F32, BF16 = jnp.float32, jnp.bfloat16
JOINT = ("polar", "azimuth")


def factor_tables():
    def build(slots, part, steps, period, scale):
        mode_all, keep, imag = slots
        parts = []
        for e in range(BANDS):
            mode = mode_all + e
            ok = keep & (mode < MODES)
            alpha = 2 * math.pi * ((mode[None, :] * (part * np.arange(HALF)[:, None])) % period) / period
            beta = 2 * math.pi * ((mode[None, :] * steps[:, None]) % period) / period
            ok = ok[None, :] & (steps[:, None] < part)
            size = np.where(mode == 0, 1.0, 2.0)[None, :] / WIN if scale else 1.0
            parts.append(
                (
                    np.where(imag[None, :], -np.sin(alpha), np.cos(alpha)),
                    np.where(imag[None, :], -np.cos(alpha), -np.sin(alpha)),
                    np.where(ok, size * np.cos(beta), 0.0),
                    np.where(ok, size * np.sin(beta), 0.0),
                )
            )
        return [np.stack(group).astype(np.float32) for group in zip(*parts)]

    a, ri, i = np.meshgrid(np.arange(LANES), np.arange(2), np.arange(M12), indexing="ij")
    slots = ((2 * (M12 * a + i)).reshape(-1), np.ones(a.size, bool), ri.reshape(-1) == 1)
    wide = build(slots, WPART, np.arange(WROWS), WIN, False)
    ri, a, i = np.meshgrid(np.arange(2), np.arange(LANES), np.arange(M16), indexing="ij")
    slots = ((2 * (M12 * a + i)).reshape(-1), i.reshape(-1) < M12, ri.reshape(-1) == 1)
    narrow = build(slots, VPART, np.arange(2 * VROWS), WOUT, True)
    return wide, narrow


HBM = pl.BlockSpec(memory_space=pltpu.HBM)
VMEM = pl.BlockSpec(memory_space=pltpu.VMEM)
SMEM = pl.BlockSpec(memory_space=pltpu.SMEM)


def call(body, places, outs, flops=0, scratch=(), nbytes=1 << 20, vmem=16, out_places=None):
    return pl.pallas_call(
        body,
        out_shape=[jax.ShapeDtypeStruct(*o) if isinstance(o, tuple) else o for o in outs],
        in_specs=places,
        out_specs=out_places or [VMEM] * len(outs),
        scratch_shapes=list(scratch),
        compiler_params=pltpu.CompilerParams(vmem_limit_bytes=vmem << 20),
        cost_estimate=pl.CostEstimate(flops=flops, bytes_accessed=nbytes, transcendentals=0),
    )


def in_hbm(value):
    return pltpu.with_memory_space_constraint(value, pltpu.HBM)


def fetch(sources, targets, sems):
    copies = [pltpu.make_async_copy(s, t, sems.at[n]) for n, (s, t) in enumerate(zip(sources, targets))]
    for copy in copies:
        copy.start()
    return copies


def low_half(shape):
    return lax.broadcasted_iota(jnp.int32, shape, len(shape) - 1) < 64


def swap64(value):
    return pltpu.roll(value, 64, value.ndim - 1)


def dot(a, b):
    return jnp.dot(a, b, preferred_element_type=F32)


def one_hot(shape, row_of_column):
    row = lax.broadcasted_iota(jnp.int32, shape, 0)
    column = lax.broadcasted_iota(jnp.int32, shape, 1)
    return jnp.where(row == row_of_column(column), 1.0, 0.0).astype(BF16)


def row_of_latitude(column):
    return 16 * (column % 8) + column // 8


def row_of_output(column):
    return 48 * (column % 4) + column // 4


def pack_body(f_hbm, g_hbm, o_ref, f_ref, g_ref, flat_ref, sems):
    copies = fetch((g_hbm, f_hbm), (g_ref, f_ref), sems)
    copies[0].wait()
    for v in range(VPART):
        flat_ref[4 * v : 4 * (v + 1), :] = g_ref[v].astype(F32)
    flat_ref[4 * VPART : 192, :] = jnp.zeros((192 - 4 * VPART, C), F32)
    rows = dot(one_hot((192, 192), row_of_output), flat_ref[...].astype(BF16))
    keep = low_half((VROWS, 128))
    for o in range(4):
        for i in range(2):
            cols = slice(128 * i, 128 * (i + 1))
            top, bottom = rows[48 * o : 48 * o + 24, cols], rows[48 * o + 24 : 48 * o + 48, cols]
            even = jnp.where(keep, top, swap64(bottom))
            odd = jnp.where(keep, swap64(top), bottom)
            o_ref[4 * o + 2 * i, WROWS:CHUNK_IN, :] = even.astype(BF16)
            o_ref[4 * o + 2 * i + 1, WROWS:CHUNK_IN, :] = odd.astype(BF16)
    copies[1].wait()
    for j in range(6):
        count = min(128, 8 * WPART - 128 * j)
        order = one_hot((128, count), row_of_latitude)
        block = dot(order, f_ref[128 * j : 128 * j + count, :]).astype(BF16)
        for r in range(8):
            for h in range(2):
                piece = block[16 * r : 16 * (r + 1), 128 * h : 128 * (h + 1)]
                o_ref[2 * r + h, 16 * j : 16 * (j + 1), :] = piece


def flip(source, target, rows, columns):
    for i in range(rows // 128):
        for j in range(columns // 128):
            piece = source[128 * i : 128 * (i + 1), 128 * j : 128 * (j + 1)].astype(F32)
            target[128 * j : 128 * (j + 1), 128 * i : 128 * (i + 1)] = piece.T.astype(BF16)


def fill_wide(w, w_ref):
    for e in range(BANDS):
        for b in range(HALF):
            one, two = w[0][e, b : b + 1, :], w[1][e, b : b + 1, :]
            block = one * w[2][e] + two * w[3][e]
            w_ref[e, WROWS * b : WROWS * (b + 1), :] = block.astype(BF16)


def fill_narrow(v, v_ref):
    for e in range(BANDS):
        for b in range(HALF):
            one, two = v[0][e, b : b + 1, :], v[1][e, b : b + 1, :]
            for part in range(2):
                rows = slice(VROWS * part, VROWS * (part + 1))
                block = one * v[2][e, rows, :] + two * v[3][e, rows, :]
                start = VROWS * (HALF * part + b)
                v_ref[e, start : start + VROWS, :] = block.astype(BF16)


def table_body(*refs):
    factors, (w_ref, v_hbm) = refs[:8], refs[8:10]
    held, (v_ref, sems, out_sem) = refs[10:18], refs[18:]
    copies = fetch(factors[4:] + factors[:4], held[4:] + held[:4], sems)
    for copy in copies[:4]:
        copy.wait()
    fill_narrow(held[4:], v_ref)
    (out,) = fetch((v_ref,), (v_hbm,), out_sem)
    for copy in copies[4:]:
        copy.wait()
    fill_wide(held[:4], w_ref)
    out.wait()


def flipped_table_body(*refs):
    factors, (wt_ref, vt_ref) = refs[:8], refs[8:10]
    held, (w_ref, v_ref, sems) = refs[10:18], refs[18:]
    for copy in fetch(factors, held, sems):
        copy.wait()
    fill_wide(held[:4], w_ref)
    fill_narrow(held[4:], v_ref)
    for e in range(BANDS):
        flip(w_ref.at[e], wt_ref.at[e], HALF * WROWS, 2 * LANES * M12)
        flip(v_ref.at[e], vt_ref.at[e], 2 * HALF * VROWS, 2 * LANES * M16)


def spectra_body(r_ref, wt_ref, vt_ref, o_ref):
    left = r_ref[0:HALF, 0:WROWS, :].reshape(HALF * WROWS, 128).astype(F32)
    right = r_ref[HALF:LANES, 0:WROWS, :].reshape(HALF * WROWS, 128).astype(F32)
    g_left = r_ref[0:HALF, WROWS:CHUNK_IN, :].reshape(HALF * VROWS, 128).astype(F32)
    g_right = r_ref[HALF:LANES, WROWS:CHUNK_IN, :].reshape(HALF * VROWS, 128).astype(F32)
    keep = low_half((HALF * VROWS, 128))
    for e in range(BANDS):
        x = (left + right if e == 0 else left - right).astype(BF16)
        g = g_left + g_right if e == 0 else g_left - g_right
        turned = swap64(g)
        both = jnp.concatenate([jnp.where(keep, g, turned), jnp.where(keep, turned, g)], axis=0).astype(BF16)
        shares = slice(LANES * e, LANES * (e + 1))
        o_ref[shares, M16:CHUNK_MID, :] = dot(wt_ref[e], x).astype(BF16).reshape(LANES, 2 * M12, 128)
        got = dot(vt_ref[e], both)
        count = LANES * M16
        out = jnp.where(low_half((count, 128)), got[:count], got[count:])
        o_ref[shares, 0:M16, :] = out.astype(BF16).reshape(LANES, M16, 128)


def filter_body(spot_ref, support_ref, p_hbm, mine_ref, other_ref, p_ref, flat_ref, sems):
    (copy,) = fetch((p_hbm,), (p_ref,), sems)
    rows = K * SUPPORT * 4
    band, start = spot_ref[0, 0], 2 * M12 * spot_ref[0, 1]
    line = lax.broadcasted_iota(jnp.int32, (WOUT, 128), 0)
    slot = lax.broadcasted_iota(jnp.int32, (WOUT, 128), 1)
    place = slot % 64
    parity = jnp.where(slot < 64, band, 1 - band)
    mode = start + 2 * (place % M12) + parity
    hit = (line == mode + MODES * (place // M12)) & (place < 2 * M12) & (mode < MODES)
    chosen = jnp.where(hit, 1.0, 0.0).astype(BF16)
    row = lax.broadcasted_iota(jnp.int32, (rows, 128), 0)
    window, output = (row // 4) % SUPPORT, row % 4
    first = jnp.zeros((rows, 128), jnp.int32)
    last = jnp.zeros((rows, 128), jnp.int32)
    for o in range(4):
        first = jnp.where(output == o, support_ref[o, 0], first)
        last = jnp.where(output == o, support_ref[o, 1], last)
    copy.wait()
    for n in range(K * SUPPORT):
        flat_ref[4 * n : 4 * (n + 1), :] = p_ref[n].astype(F32)
    got = dot(flat_ref[0:rows, :].astype(BF16), chosen)
    got = jnp.where((window >= first) & (window <= last), got, 0.0)
    mine_ref[...] = got.astype(BF16)
    other_ref[...] = swap64(got).astype(BF16)


def mixing_body(spot_ref, mine_ref, got_ref, w_hbm, p_ref, w_ref, sems):
    (copy,) = fetch((w_hbm,), (w_ref,), sems)
    rows, width, count = K * 16, HIN * 2 * M12, K * SUPPORT * 4
    low = spot_ref[0, 0] == 0
    mine, got = mine_ref[...].astype(F32), got_ref[...].astype(F32)
    halves = (jnp.where(low, mine, got).astype(BF16), jnp.where(low, got, mine).astype(BF16))
    x = lax.broadcasted_iota(jnp.int32, (128, width), 0)
    lane = lax.broadcasted_iota(jnp.int32, (128, width), 1)
    same, cross = lane % M12, lane % (2 * M12) < M12
    straight = x == same + jnp.where(cross, 0, M12)
    turned = x == same + jnp.where(cross, M12, 0)
    tiles = (
        jnp.where(straight, jnp.where(cross, 1.0, -1.0), 0.0).astype(BF16),
        jnp.where(turned, 1.0, 0.0).astype(BF16),
    )
    row = lax.broadcasted_iota(jnp.int32, (count, width), 0)
    lane = lax.broadcasted_iota(jnp.int32, (count, width), 1)
    reach = 2 * (row % 4) + (row // 4) % SUPPORT - 2 - lane // (2 * M12)
    target = lax.broadcasted_iota(jnp.int32, (rows, count), 0)
    source = lax.broadcasted_iota(jnp.int32, (rows, count), 1)
    key = target - 16 * (source // 20) - 2 * (source % 4)
    total = jnp.zeros((rows, width), F32)
    for half in range(2):
        for ri in range(2):
            spread = dot(halves[half], tiles[ri])
            spread = jnp.where(reach == -8 * half, spread, 0.0).astype(BF16)
            collect = jnp.where(key == 8 * half + ri, 1.0, 0.0).astype(BF16)
            total = total + dot(collect, spread)
    p_ref[...] = total
    copy.wait()


def row_of_share(column):
    return 16 * (column % 16) + column // 16


def middle_body(band_ref, r_ref, p_ref, w_ref, mine_ref, other_ref, gs_ref, out_ref, sg_ref):
    keep = low_half((M16, 128))
    for o in range(HOUT):
        for i in range(2):
            first = r_ref[2 * o + i, 0, 0:M16, :].astype(F32)
            second = r_ref[2 * o + i, 1, 0:M16, :].astype(F32)
            cols = slice(128 * i, 128 * (i + 1))
            gs_ref[32 * o : 32 * o + 16, cols] = jnp.where(keep, first, swap64(second)).astype(BF16)
            gs_ref[32 * o + 16 : 32 * o + 32, cols] = jnp.where(keep, swap64(first), second).astype(BF16)
    used = M12 * 16
    gs = dot(one_hot((used, 256), row_of_share), gs_ref[...]).astype(BF16)
    width = HIN * 2 * M12
    x = jnp.concatenate(
        [r_ref[:, h, M16:CHUNK_MID, :].reshape(width, 128) for h in range(2)], axis=1
    )
    lane_mode = lax.broadcasted_iota(jnp.int32, (16, width), 1) % M12
    diagonal = (
        lax.broadcasted_iota(jnp.int32, (width, used), 0) % M12
        == lax.broadcasted_iota(jnp.int32, (width, used), 1) // 16
    )
    spread = one_hot((16, used), lambda column: column % 16)
    low = band_ref[0, 0] == 0

    for k in range(K):
        placed = p_ref[16 * k : 16 * (k + 1), :]
        blocks = [jnp.where(lane_mode == m, placed, 0.0).astype(BF16) for m in range(M12)]
        mixed = dot(jnp.concatenate(blocks, axis=0), x).astype(BF16)
        out_now = dot(mixed, w_ref[k])
        grad = lax.dot_general(mixed, gs, (((0,), (0,)), ((), ())), preferred_element_type=F32)
        where_to = (slice(None), slice(CHUNK_MID + 16 * k, CHUNK_MID + 16 * (k + 1)), slice(None))
        shape = (LANES, 16, 128)
        mine_ref[where_to] = jnp.where(low, grad[:, :128], grad[:, 128:]).astype(BF16).reshape(shape)
        other_ref[where_to] = jnp.where(low, grad[:, 128:], grad[:, :128]).astype(BF16).reshape(shape)
        back = lax.dot_general(gs, w_ref[k], (((1,), (1,)), ((), ())), preferred_element_type=F32)
        grown = lax.dot_general(
            placed.astype(BF16), spread, (((0,), (0,)), ((), ())), preferred_element_type=F32
        )
        sg_now = dot(jnp.where(diagonal, grown, 0.0).astype(BF16), back.astype(BF16))
        if k == 0:
            out_ref[...] = out_now
            sg_ref[...] = sg_now
        else:
            out_ref[...] += out_now
            sg_ref[...] += sg_now

    ordered = lax.dot_general(
        one_hot((used, 256), row_of_share),
        out_ref[...].astype(BF16),
        (((0,), (0,)), ((), ())),
        preferred_element_type=F32,
    )

    def output_rows(n):
        o, q = n // 4, n % 4
        cols = slice(128 * (q // 2), 128 * (q // 2 + 1))
        re = ordered[32 * o : 32 * o + 16, cols]
        im = ordered[32 * o + 16 : 32 * o + 32, cols]
        return jnp.where(keep, re, swap64(im)) if q % 2 == 0 else jnp.where(keep, swap64(re), im)

    def field_rows(n):
        r, h = n // 2, n % 2
        return sg_ref[24 * r : 24 * (r + 1), 128 * h : 128 * (h + 1)]

    for a in range(LANES):
        for rows, make in ((slice(0, M16), output_rows), (slice(M16, CHUNK_MID), field_rows)):
            first, second = make(a), make(a + LANES)
            mine_ref[a, rows, :] = jnp.where(low, first, second).astype(BF16)
            other_ref[a, rows, :] = jnp.where(low, second, first).astype(BF16)


def merge_body(band_ref, mine_ref, got_ref, o_ref):
    low = band_ref[0, 0] == 0
    for a in range(LANES):
        mine, got = mine_ref[a, 0:CHUNK_MID, :].astype(F32), got_ref[a, 0:CHUNK_MID, :].astype(F32)
        o_ref[a, 0:CHUNK_MID, :] = jnp.where(low, mine, got).astype(BF16)
        o_ref[a, CHUNK_MID : 2 * CHUNK_MID, :] = jnp.where(low, got, mine).astype(BF16)
        mine, got = mine_ref[a, CHUNK_MID:, :].astype(F32), got_ref[a, CHUNK_MID:, :].astype(F32)
        o_ref[a, 2 * CHUNK_MID :, :] = (mine + got).astype(BF16)


def fields_body(r_ref, w_ref, v_hbm, o_ref, v_ref, sems):
    (copy,) = fetch((v_hbm,), (v_ref,), sems)
    fields, outs = [], []
    for e in range(BANDS):
        start = CHUNK_MID * e
        sg = r_ref[:, start + M16 : start + CHUNK_MID, :].reshape(LANES * 2 * M12, 128)
        fields.append(dot(w_ref[e], sg))
    for side in range(2):
        lanes = slice(HALF * side, HALF * (side + 1))
        field = fields[0] + fields[1] if side == 0 else fields[0] - fields[1]
        o_ref[lanes, 0:WROWS, :] = field.astype(BF16).reshape(HALF, WROWS, 128)
    copy.wait()
    for e in range(BANDS):
        start = CHUNK_MID * e
        c = r_ref[:, start : start + M16, :].reshape(LANES * M16, 128).astype(F32)
        turned = swap64(c)
        keep = low_half(c.shape)
        both = jnp.concatenate([jnp.where(keep, c, turned), jnp.where(keep, turned, c)], axis=0).astype(BF16)
        got = dot(v_ref[e], both)
        count = HALF * VROWS
        outs.append(jnp.where(low_half((count, 128)), got[:count], got[count:]))
    for side in range(2):
        lanes = slice(HALF * side, HALF * (side + 1))
        out = outs[0] + outs[1] if side == 0 else outs[0] - outs[1]
        o_ref[lanes, WROWS:CHUNK_IN, :] = out.astype(BF16).reshape(HALF, VROWS, 128)


def unpack_body(r_ref, f_ref, c_ref, flat_ref):
    for j in range(6):
        count = min(128, 8 * WPART - 128 * j)
        halves = [
            jnp.concatenate([r_ref[2 * r + h, 16 * j : 16 * (j + 1), :] for r in range(8)], axis=0)
            for h in range(2)
        ]
        order = one_hot((128, count), row_of_latitude)
        block = lax.dot_general(
            order, jnp.concatenate(halves, axis=1), (((0,), (0,)), ((), ())), preferred_element_type=F32
        )
        f_ref[128 * j : 128 * j + count, :] = block.astype(BF16)
    keep = low_half((VROWS, 128))
    for o in range(4):
        for i in range(2):
            even = r_ref[4 * o + 2 * i, WROWS:CHUNK_IN, :].astype(F32)
            odd = r_ref[4 * o + 2 * i + 1, WROWS:CHUNK_IN, :].astype(F32)
            cols = slice(128 * i, 128 * (i + 1))
            flat_ref[48 * o : 48 * o + 24, cols] = jnp.where(keep, even, swap64(odd))
            flat_ref[48 * o + 24 : 48 * o + 48, cols] = jnp.where(keep, swap64(even), odd)
    rows = lax.dot_general(
        one_hot((192, 192), row_of_output),
        flat_ref[...].astype(BF16),
        (((0,), (0,)), ((), ())),
        preferred_element_type=F32,
    )
    for v in range(VPART):
        c_ref[v] = rows[4 * v : 4 * (v + 1), :].astype(BF16)


def place_body(band_ref, half_ref, far_ref, o_ref):
    low = band_ref[0, 0] == 0
    half, far = half_ref[...], far_ref[...]
    o_ref[:, 0:128] = jnp.where(low, half, far)
    o_ref[:, 128:256] = jnp.where(low, far, half)


def swap_bands(value):
    return lax.ppermute(value, "polar", [(0, 1), (1, 0)])


def local(fields, basis_spectra, support, weights, out_grad):
    band = lax.axis_index("polar").astype(jnp.int32)
    spot = jnp.stack([band, lax.axis_index("azimuth").astype(jnp.int32)]).reshape(1, 2)
    wide, narrow = factor_tables()
    dma = pltpu.SemaphoreType.DMA
    (sent,) = call(
        pack_body,
        [HBM, HBM],
        [((LANES, CHUNK_IN, 128), BF16)],
        scratch=[
            pltpu.VMEM((8 * WPART, C), BF16),
            pltpu.VMEM((VPART, 4, C), BF16),
            pltpu.VMEM((192, C), F32),
            dma((2,)),
        ],
    )(
        in_hbm(jnp.swapaxes(fields[0], 0, 1).reshape(8 * WPART, C)), in_hbm(jnp.swapaxes(out_grad[0], 0, 1))
    )
    landed = lax.all_to_all(sent, "azimuth", split_axis=0, concat_axis=0, tiled=True)

    filters, limits, sent = lax.optimization_barrier((basis_spectra, support, sent))
    mine, other = call(
        filter_body,
        [SMEM, SMEM, HBM],
        [((K * SUPPORT * 4, 128), BF16)] * 2,
        scratch=[pltpu.VMEM((K * SUPPORT, 4, WOUT), BF16), pltpu.VMEM((184, WOUT), F32), dma((1,))],
    )(spot, limits, in_hbm(jnp.swapaxes(filters, 1, 2).reshape(K * SUPPORT, 4, WOUT)))
    got = swap_bands(other)
    factors = [a for a in wide + narrow]
    held = [pltpu.VMEM(a.shape, F32) for a in factors]
    factors, sent = lax.optimization_barrier(([jnp.asarray(a) for a in factors], sent))
    flat, inv_t = call(
        flipped_table_body,
        [HBM] * 8,
        [((2, 384, 768), BF16), ((2, 512, 384), BF16)],
        nbytes=5 << 20,
        scratch=held + [pltpu.VMEM((2, 768, 384), BF16), pltpu.VMEM((2, 384, 512), BF16), dma((8,))],
    )(*[in_hbm(a) for a in factors])

    landed, mine, got = lax.optimization_barrier((landed, mine, got))
    (sent,) = call(spectra_body, [VMEM] * 3, [((SHARES, CHUNK_MID, 128), BF16)], flops=300 << 20)(landed, flat, inv_t)
    landed = lax.all_to_all(sent, JOINT, split_axis=0, concat_axis=0, tiled=True)
    mine, got, sent = lax.optimization_barrier((mine, got, sent))
    placed, staged = call(
        mixing_body, [SMEM, VMEM, VMEM, HBM], [((K * 16, HIN * 2 * M12), F32), ((K, C, C), BF16)], scratch=[dma((1,))]
    )(spot, mine, got, in_hbm(weights))

    chunk = (LANES, CHUNK_MID + 16 * K, 128)
    mine, other = call(
        middle_body,
        [SMEM, VMEM, VMEM, VMEM],
        [(chunk, BF16), (chunk, BF16)],
        flops=2 << 30,
        nbytes=3 << 20,
        scratch=[
            pltpu.VMEM((256, 256), BF16),
            pltpu.VMEM((192, 256), F32),
            pltpu.VMEM((384, 256), F32),
        ],
    )(spot, landed.reshape(HIN, 2, CHUNK_MID, 128), placed, staged)
    factors, mine, other = lax.optimization_barrier((factors, mine, other))
    got = swap_bands(other)
    tall, inv = call(
        table_body,
        [HBM] * 8,
        [((2, 768, 384), BF16), pltpu.HBM((2, 384, 512), BF16)],
        nbytes=5 << 20,
        scratch=held + [pltpu.VMEM((2, 384, 512), BF16), dma((8,)), dma((1,))],
        out_places=[VMEM, HBM],
    )(*[in_hbm(a) for a in factors])
    got, tall, inv = lax.optimization_barrier((got, tall, inv))
    (sent,) = call(merge_body, [SMEM, VMEM, VMEM], [((LANES, CHUNK_OUT, 128), BF16)], nbytes=2 << 20)(spot, mine, got)
    landed = lax.all_to_all(sent, "azimuth", split_axis=0, concat_axis=0, tiled=True)

    members = lax.axis_size("ens")

    def send(value, offset_even, offset_odd):
        offsets = (offset_even, offset_odd)
        pairs = [(i, (i + offsets[i % 2]) % members) for i in range(members)]
        return lax.ppermute(value, "ens", pairs)

    half = jnp.sum(landed[:, 2 * CHUNK_MID :, :].astype(F32), axis=0).astype(BF16)
    got = send(half, 1, -1)
    pair = (half.astype(F32) + got.astype(F32)).astype(BF16)
    beside = send(pair, -1, 1)
    across = send(beside, 2, -2)
    behind = send(beside, 1, -1)
    half = (pair.astype(F32) + across.astype(F32)) + (beside.astype(F32) + behind.astype(F32))
    far = swap_bands(half)
    (sent,) = call(
        fields_body,
        [VMEM, VMEM, HBM],
        [((LANES, CHUNK_IN, 128), BF16)],
        flops=300 << 20,
        scratch=[pltpu.VMEM((2, 384, 512), BF16), dma((1,))],
    )(landed, tall, in_hbm(inv))
    landed = lax.all_to_all(sent, "azimuth", split_axis=0, concat_axis=0, tiled=True)
    field_grad, conv_out = call(
        unpack_body, [VMEM], [((8 * WPART, C), BF16), ((VPART, 4, C), BF16)], scratch=[pltpu.VMEM((192, C), F32)]
    )(landed)
    (weight_grad,) = call(place_body, [SMEM, VMEM, VMEM], [((K * 16, C), F32)])(spot, half, far)
    field_grad = jnp.swapaxes(field_grad.reshape(WPART, 8, C), 0, 1)
    return (jnp.swapaxes(conv_out, 0, 1)[None], field_grad[None], weight_grad.reshape(K, 16, C))


def solution(mesh):
    placed = (
        P("ens", "polar", "azimuth", None),
        P(None, "polar", None, None),
        P("polar", None),
        P(),
        P("ens", "polar", "azimuth", None),
    )
    return jax.shard_map(
        local,
        mesh=mesh,
        in_specs=placed,
        out_specs=(
            P("ens", "polar", "azimuth", None),
            P("ens", "polar", "azimuth", None),
            P(None, "azimuth", None),
        ),
        check_vma=False,
    )
```

```python
import math

import jax
import jax.numpy as jnp
import numpy as np
from jax import lax
from jax.experimental import pallas as pl
from jax.experimental.pallas import tpu as pltpu
from jax.sharding import PartitionSpec as P


WIN, WOUT, MODES = 1440, 720, 360
K, C, SUPPORT = 9, 256, 5
HOUT, HIN = 8, 16
LANES, BANDS = 16, 2
SHARES = LANES * BANDS
HALF = LANES // 2
M12, M16 = 12, 16
WPART, WROWS = 90, 96
VPART, VROWS = 45, 24
CHUNK_IN = WROWS + VROWS
CHUNK_MID = M16 + 2 * M12
CHUNK_OUT = 2 * CHUNK_MID + 16 * K
F32, BF16 = jnp.float32, jnp.bfloat16
JOINT = ("polar", "azimuth")


def factor_tables():
    def build(slots, part, steps, period, scale):
        mode_all, keep, imag = slots
        parts = []
        for e in range(BANDS):
            mode = mode_all + e
            ok = keep & (mode < MODES)
            alpha = 2 * math.pi * ((mode[None, :] * (part * np.arange(HALF)[:, None])) % period) / period
            beta = 2 * math.pi * ((mode[None, :] * steps[:, None]) % period) / period
            ok = ok[None, :] & (steps[:, None] < part)
            size = np.where(mode == 0, 1.0, 2.0)[None, :] / WIN if scale else 1.0
            parts.append(
                (
                    np.where(imag[None, :], -np.sin(alpha), np.cos(alpha)),
                    np.where(imag[None, :], -np.cos(alpha), -np.sin(alpha)),
                    np.where(ok, size * np.cos(beta), 0.0),
                    np.where(ok, size * np.sin(beta), 0.0),
                )
            )
        return [np.stack(group).astype(np.float32) for group in zip(*parts)]

    a, ri, i = np.meshgrid(np.arange(LANES), np.arange(2), np.arange(M12), indexing="ij")
    slots = ((2 * (M12 * a + i)).reshape(-1), np.ones(a.size, bool), ri.reshape(-1) == 1)
    wide = build(slots, WPART, np.arange(WROWS), WIN, False)
    ri, a, i = np.meshgrid(np.arange(2), np.arange(LANES), np.arange(M16), indexing="ij")
    slots = ((2 * (M12 * a + i)).reshape(-1), i.reshape(-1) < M12, ri.reshape(-1) == 1)
    narrow = build(slots, VPART, np.arange(2 * VROWS), WOUT, True)
    return wide, narrow


HBM = pl.BlockSpec(memory_space=pltpu.HBM)
VMEM = pl.BlockSpec(memory_space=pltpu.VMEM)
SMEM = pl.BlockSpec(memory_space=pltpu.SMEM)


def call(body, places, outs, flops=0, scratch=(), nbytes=1 << 20, vmem=16, out_places=None):
    return pl.pallas_call(
        body,
        out_shape=[jax.ShapeDtypeStruct(*o) if isinstance(o, tuple) else o for o in outs],
        in_specs=places,
        out_specs=out_places or [VMEM] * len(outs),
        scratch_shapes=list(scratch),
        compiler_params=pltpu.CompilerParams(vmem_limit_bytes=vmem << 20),
        cost_estimate=pl.CostEstimate(flops=flops, bytes_accessed=nbytes, transcendentals=0),
    )


def in_hbm(value):
    return pltpu.with_memory_space_constraint(value, pltpu.HBM)


def fetch(sources, targets, sems):
    copies = [pltpu.make_async_copy(s, t, sems.at[n]) for n, (s, t) in enumerate(zip(sources, targets))]
    for copy in copies:
        copy.start()
    return copies


def low_half(shape):
    return lax.broadcasted_iota(jnp.int32, shape, len(shape) - 1) < 64


def swap64(value):
    return pltpu.roll(value, 64, value.ndim - 1)


def dot(a, b):
    return jnp.dot(a, b, preferred_element_type=F32)


def one_hot(shape, row_of_column):
    row = lax.broadcasted_iota(jnp.int32, shape, 0)
    column = lax.broadcasted_iota(jnp.int32, shape, 1)
    return jnp.where(row == row_of_column(column), 1.0, 0.0).astype(BF16)


def row_of_latitude(column):
    return 16 * (column % 8) + column // 8


def row_of_output(column):
    return 48 * (column % 4) + column // 4


def pack_body(f_hbm, g_hbm, o_ref, f_ref, g_ref, flat_ref, sems):
    copies = fetch((g_hbm, f_hbm), (g_ref, f_ref), sems)
    copies[0].wait()
    for v in range(VPART):
        flat_ref[4 * v : 4 * (v + 1), :] = g_ref[v].astype(F32)
    flat_ref[4 * VPART : 192, :] = jnp.zeros((192 - 4 * VPART, C), F32)
    rows = dot(one_hot((192, 192), row_of_output), flat_ref[...].astype(BF16))
    keep = low_half((VROWS, 128))
    for o in range(4):
        for i in range(2):
            cols = slice(128 * i, 128 * (i + 1))
            top, bottom = rows[48 * o : 48 * o + 24, cols], rows[48 * o + 24 : 48 * o + 48, cols]
            even = jnp.where(keep, top, swap64(bottom))
            odd = jnp.where(keep, swap64(top), bottom)
            o_ref[4 * o + 2 * i, WROWS:CHUNK_IN, :] = even.astype(BF16)
            o_ref[4 * o + 2 * i + 1, WROWS:CHUNK_IN, :] = odd.astype(BF16)
    copies[1].wait()
    for j in range(6):
        count = min(128, 8 * WPART - 128 * j)
        order = one_hot((128, count), row_of_latitude)
        block = dot(order, f_ref[128 * j : 128 * j + count, :]).astype(BF16)
        for r in range(8):
            for h in range(2):
                piece = block[16 * r : 16 * (r + 1), 128 * h : 128 * (h + 1)]
                o_ref[2 * r + h, 16 * j : 16 * (j + 1), :] = piece


def flip(source, target, rows, columns):
    for i in range(rows // 128):
        for j in range(columns // 128):
            piece = source[128 * i : 128 * (i + 1), 128 * j : 128 * (j + 1)].astype(F32)
            target[128 * j : 128 * (j + 1), 128 * i : 128 * (i + 1)] = piece.T.astype(BF16)


def fill_wide(w, w_ref):
    for e in range(BANDS):
        for b in range(HALF):
            one, two = w[0][e, b : b + 1, :], w[1][e, b : b + 1, :]
            block = one * w[2][e] + two * w[3][e]
            w_ref[e, WROWS * b : WROWS * (b + 1), :] = block.astype(BF16)


def fill_narrow(v, v_ref):
    for e in range(BANDS):
        for b in range(HALF):
            one, two = v[0][e, b : b + 1, :], v[1][e, b : b + 1, :]
            for part in range(2):
                rows = slice(VROWS * part, VROWS * (part + 1))
                block = one * v[2][e, rows, :] + two * v[3][e, rows, :]
                start = VROWS * (HALF * part + b)
                v_ref[e, start : start + VROWS, :] = block.astype(BF16)


def table_body(*refs):
    factors, (w_ref, v_hbm) = refs[:8], refs[8:10]
    held, (v_ref, sems, out_sem) = refs[10:18], refs[18:]
    copies = fetch(factors[4:] + factors[:4], held[4:] + held[:4], sems)
    for copy in copies[:4]:
        copy.wait()
    fill_narrow(held[4:], v_ref)
    (out,) = fetch((v_ref,), (v_hbm,), out_sem)
    for copy in copies[4:]:
        copy.wait()
    fill_wide(held[:4], w_ref)
    out.wait()


def flipped_table_body(*refs):
    factors, (wt_ref, vt_ref) = refs[:8], refs[8:10]
    held, (w_ref, v_ref, sems) = refs[10:18], refs[18:]
    for copy in fetch(factors, held, sems):
        copy.wait()
    fill_wide(held[:4], w_ref)
    fill_narrow(held[4:], v_ref)
    for e in range(BANDS):
        flip(w_ref.at[e], wt_ref.at[e], HALF * WROWS, 2 * LANES * M12)
        flip(v_ref.at[e], vt_ref.at[e], 2 * HALF * VROWS, 2 * LANES * M16)


def spectra_body(r_ref, wt_ref, vt_ref, o_ref):
    left = r_ref[0:HALF, 0:WROWS, :].reshape(HALF * WROWS, 128).astype(F32)
    right = r_ref[HALF:LANES, 0:WROWS, :].reshape(HALF * WROWS, 128).astype(F32)
    g_left = r_ref[0:HALF, WROWS:CHUNK_IN, :].reshape(HALF * VROWS, 128).astype(F32)
    g_right = r_ref[HALF:LANES, WROWS:CHUNK_IN, :].reshape(HALF * VROWS, 128).astype(F32)
    keep = low_half((HALF * VROWS, 128))
    for e in range(BANDS):
        x = (left + right if e == 0 else left - right).astype(BF16)
        g = g_left + g_right if e == 0 else g_left - g_right
        turned = swap64(g)
        both = jnp.concatenate([jnp.where(keep, g, turned), jnp.where(keep, turned, g)], axis=0).astype(BF16)
        shares = slice(LANES * e, LANES * (e + 1))
        o_ref[shares, M16:CHUNK_MID, :] = dot(wt_ref[e], x).astype(BF16).reshape(LANES, 2 * M12, 128)
        got = dot(vt_ref[e], both)
        count = LANES * M16
        out = jnp.where(low_half((count, 128)), got[:count], got[count:])
        o_ref[shares, 0:M16, :] = out.astype(BF16).reshape(LANES, M16, 128)


def filter_body(spot_ref, support_ref, p_hbm, mine_ref, other_ref, p_ref, flat_ref, sems):
    (copy,) = fetch((p_hbm,), (p_ref,), sems)
    rows = K * SUPPORT * 4
    band, start = spot_ref[0, 0], 2 * M12 * spot_ref[0, 1]
    line = lax.broadcasted_iota(jnp.int32, (WOUT, 128), 0)
    slot = lax.broadcasted_iota(jnp.int32, (WOUT, 128), 1)
    place = slot % 64
    parity = jnp.where(slot < 64, band, 1 - band)
    mode = start + 2 * (place % M12) + parity
    hit = (line == mode + MODES * (place // M12)) & (place < 2 * M12) & (mode < MODES)
    chosen = jnp.where(hit, 1.0, 0.0).astype(BF16)
    row = lax.broadcasted_iota(jnp.int32, (rows, 128), 0)
    window, output = (row // 4) % SUPPORT, row % 4
    first = jnp.zeros((rows, 128), jnp.int32)
    last = jnp.zeros((rows, 128), jnp.int32)
    for o in range(4):
        first = jnp.where(output == o, support_ref[o, 0], first)
        last = jnp.where(output == o, support_ref[o, 1], last)
    copy.wait()
    for n in range(K * SUPPORT):
        flat_ref[4 * n : 4 * (n + 1), :] = p_ref[n].astype(F32)
    got = dot(flat_ref[0:rows, :].astype(BF16), chosen)
    got = jnp.where((window >= first) & (window <= last), got, 0.0)
    mine_ref[...] = got.astype(BF16)
    other_ref[...] = swap64(got).astype(BF16)


def mixing_body(spot_ref, mine_ref, got_ref, w_hbm, p_ref, w_ref, sems):
    (copy,) = fetch((w_hbm,), (w_ref,), sems)
    rows, width, count = K * 16, HIN * 2 * M12, K * SUPPORT * 4
    low = spot_ref[0, 0] == 0
    mine, got = mine_ref[...].astype(F32), got_ref[...].astype(F32)
    halves = (jnp.where(low, mine, got).astype(BF16), jnp.where(low, got, mine).astype(BF16))
    x = lax.broadcasted_iota(jnp.int32, (128, width), 0)
    lane = lax.broadcasted_iota(jnp.int32, (128, width), 1)
    same, cross = lane % M12, lane % (2 * M12) < M12
    straight = x == same + jnp.where(cross, 0, M12)
    turned = x == same + jnp.where(cross, M12, 0)
    tiles = (
        jnp.where(straight, jnp.where(cross, 1.0, -1.0), 0.0).astype(BF16),
        jnp.where(turned, 1.0, 0.0).astype(BF16),
    )
    row = lax.broadcasted_iota(jnp.int32, (count, width), 0)
    lane = lax.broadcasted_iota(jnp.int32, (count, width), 1)
    reach = 2 * (row % 4) + (row // 4) % SUPPORT - 2 - lane // (2 * M12)
    target = lax.broadcasted_iota(jnp.int32, (rows, count), 0)
    source = lax.broadcasted_iota(jnp.int32, (rows, count), 1)
    key = target - 16 * (source // 20) - 2 * (source % 4)
    total = jnp.zeros((rows, width), F32)
    for half in range(2):
        for ri in range(2):
            spread = dot(halves[half], tiles[ri])
            spread = jnp.where(reach == -8 * half, spread, 0.0).astype(BF16)
            collect = jnp.where(key == 8 * half + ri, 1.0, 0.0).astype(BF16)
            total = total + dot(collect, spread)
    p_ref[...] = total
    copy.wait()


def row_of_share(column):
    return 16 * (column % 16) + column // 16


def middle_body(band_ref, r_ref, p_ref, w_ref, mine_ref, other_ref, gs_ref, out_ref, sg_ref):
    keep = low_half((M16, 128))
    for o in range(HOUT):
        for i in range(2):
            first = r_ref[2 * o + i, 0, 0:M16, :].astype(F32)
            second = r_ref[2 * o + i, 1, 0:M16, :].astype(F32)
            cols = slice(128 * i, 128 * (i + 1))
            gs_ref[32 * o : 32 * o + 16, cols] = jnp.where(keep, first, swap64(second)).astype(BF16)
            gs_ref[32 * o + 16 : 32 * o + 32, cols] = jnp.where(keep, swap64(first), second).astype(BF16)
    used = M12 * 16
    low = band_ref[0, 0] == 0
    ordered = dot(one_hot((used, 256), row_of_share), gs_ref[...])
    gs = ordered.astype(BF16)
    left, right = ordered[:, :128], ordered[:, 128:]
    turned = jnp.concatenate([jnp.where(low, left, right), jnp.where(low, right, left)], axis=1).astype(BF16)
    width = HIN * 2 * M12
    x = jnp.concatenate(
        [r_ref[:, h, M16:CHUNK_MID, :].reshape(width, 128) for h in range(2)], axis=1
    )
    lane_mode = lax.broadcasted_iota(jnp.int32, (16, width), 1) % M12
    diagonal = (
        lax.broadcasted_iota(jnp.int32, (width, used), 0) % M12
        == lax.broadcasted_iota(jnp.int32, (width, used), 1) // 16
    )
    spread = one_hot((16, used), lambda column: column % 16)
    for k in range(K):
        placed = p_ref[16 * k : 16 * (k + 1), :]
        blocks = [jnp.where(lane_mode == m, placed, 0.0).astype(BF16) for m in range(M12)]
        mixed = dot(jnp.concatenate(blocks, axis=0), x).astype(BF16)
        out_now = dot(mixed, w_ref[k])
        grad = lax.dot_general(mixed, turned, (((0,), (0,)), ((), ())), preferred_element_type=F32)
        where_to = (slice(None), slice(CHUNK_MID + 16 * k, CHUNK_MID + 16 * (k + 1)), slice(None))
        shape = (LANES, 16, 128)
        mine_ref[where_to] = grad[:, :128].astype(BF16).reshape(shape)
        other_ref[where_to] = grad[:, 128:].astype(BF16).reshape(shape)
        back = lax.dot_general(gs, w_ref[k], (((1,), (1,)), ((), ())), preferred_element_type=F32)
        grown = lax.dot_general(
            placed.astype(BF16), spread, (((0,), (0,)), ((), ())), preferred_element_type=F32
        )
        sg_now = dot(jnp.where(diagonal, grown, 0.0).astype(BF16), back.astype(BF16))
        if k == 0:
            out_ref[...] = out_now
            sg_ref[...] = sg_now
        else:
            out_ref[...] += out_now
            sg_ref[...] += sg_now

    ordered = lax.dot_general(
        one_hot((used, 256), row_of_share),
        out_ref[...].astype(BF16),
        (((0,), (0,)), ((), ())),
        preferred_element_type=F32,
    )

    def output_rows(n):
        o, q = n // 4, n % 4
        cols = slice(128 * (q // 2), 128 * (q // 2 + 1))
        re = ordered[32 * o : 32 * o + 16, cols]
        im = ordered[32 * o + 16 : 32 * o + 32, cols]
        return jnp.where(keep, re, swap64(im)) if q % 2 == 0 else jnp.where(keep, swap64(re), im)

    def field_rows(n):
        r, h = n // 2, n % 2
        return sg_ref[24 * r : 24 * (r + 1), 128 * h : 128 * (h + 1)]

    for a in range(LANES):
        for rows, make in ((slice(0, M16), output_rows), (slice(M16, CHUNK_MID), field_rows)):
            first, second = make(a), make(a + LANES)
            mine_ref[a, rows, :] = jnp.where(low, first, second).astype(BF16)
            other_ref[a, rows, :] = jnp.where(low, second, first).astype(BF16)


def merge_body(band_ref, mine_ref, got_ref, o_ref):
    low = band_ref[0, 0] == 0
    for a in range(LANES):
        mine, got = mine_ref[a, 0:CHUNK_MID, :].astype(F32), got_ref[a, 0:CHUNK_MID, :].astype(F32)
        o_ref[a, 0:CHUNK_MID, :] = jnp.where(low, mine, got).astype(BF16)
        o_ref[a, CHUNK_MID : 2 * CHUNK_MID, :] = jnp.where(low, got, mine).astype(BF16)
        mine, got = mine_ref[a, CHUNK_MID:, :].astype(F32), got_ref[a, CHUNK_MID:, :].astype(F32)
        o_ref[a, 2 * CHUNK_MID :, :] = (mine + got).astype(BF16)


def fields_body(r_ref, w_ref, v_hbm, o_ref, v_ref, sems):
    (copy,) = fetch((v_hbm,), (v_ref,), sems)
    fields, outs = [], []
    for e in range(BANDS):
        start = CHUNK_MID * e
        sg = r_ref[:, start + M16 : start + CHUNK_MID, :].reshape(LANES * 2 * M12, 128)
        fields.append(dot(w_ref[e], sg))
    for side in range(2):
        lanes = slice(HALF * side, HALF * (side + 1))
        field = fields[0] + fields[1] if side == 0 else fields[0] - fields[1]
        o_ref[lanes, 0:WROWS, :] = field.astype(BF16).reshape(HALF, WROWS, 128)
    copy.wait()
    for e in range(BANDS):
        start = CHUNK_MID * e
        c = r_ref[:, start : start + M16, :].reshape(LANES * M16, 128).astype(F32)
        turned = swap64(c)
        keep = low_half(c.shape)
        both = jnp.concatenate([jnp.where(keep, c, turned), jnp.where(keep, turned, c)], axis=0).astype(BF16)
        got = dot(v_ref[e], both)
        count = HALF * VROWS
        outs.append(jnp.where(low_half((count, 128)), got[:count], got[count:]))
    for side in range(2):
        lanes = slice(HALF * side, HALF * (side + 1))
        out = outs[0] + outs[1] if side == 0 else outs[0] - outs[1]
        o_ref[lanes, WROWS:CHUNK_IN, :] = out.astype(BF16).reshape(HALF, VROWS, 128)


def unpack_body(r_ref, f_ref, c_ref, flat_ref):
    for j in range(6):
        count = min(128, 8 * WPART - 128 * j)
        halves = [
            jnp.concatenate([r_ref[2 * r + h, 16 * j : 16 * (j + 1), :] for r in range(8)], axis=0)
            for h in range(2)
        ]
        order = one_hot((128, count), row_of_latitude)
        block = lax.dot_general(
            order, jnp.concatenate(halves, axis=1), (((0,), (0,)), ((), ())), preferred_element_type=F32
        )
        f_ref[128 * j : 128 * j + count, :] = block.astype(BF16)
    keep = low_half((VROWS, 128))
    for o in range(4):
        for i in range(2):
            even = r_ref[4 * o + 2 * i, WROWS:CHUNK_IN, :].astype(F32)
            odd = r_ref[4 * o + 2 * i + 1, WROWS:CHUNK_IN, :].astype(F32)
            cols = slice(128 * i, 128 * (i + 1))
            flat_ref[48 * o : 48 * o + 24, cols] = jnp.where(keep, even, swap64(odd))
            flat_ref[48 * o + 24 : 48 * o + 48, cols] = jnp.where(keep, swap64(even), odd)
    rows = lax.dot_general(
        one_hot((192, 192), row_of_output),
        flat_ref[...].astype(BF16),
        (((0,), (0,)), ((), ())),
        preferred_element_type=F32,
    )
    for v in range(VPART):
        c_ref[v] = rows[4 * v : 4 * (v + 1), :].astype(BF16)


def swap_bands(value):
    return lax.ppermute(value, "polar", [(0, 1), (1, 0)])


def local(fields, basis_spectra, support, weights, out_grad):
    band = lax.axis_index("polar").astype(jnp.int32)
    low = band == 0
    spot = jnp.stack([band, lax.axis_index("azimuth").astype(jnp.int32)]).reshape(1, 2)
    wide, narrow = factor_tables()
    dma = pltpu.SemaphoreType.DMA
    (sent,) = call(
        pack_body,
        [HBM, HBM],
        [((LANES, CHUNK_IN, 128), BF16)],
        scratch=[
            pltpu.VMEM((8 * WPART, C), BF16),
            pltpu.VMEM((VPART, 4, C), BF16),
            pltpu.VMEM((192, C), F32),
            dma((2,)),
        ],
    )(
        in_hbm(jnp.swapaxes(fields[0], 0, 1).reshape(8 * WPART, C)), in_hbm(jnp.swapaxes(out_grad[0], 0, 1))
    )
    landed = lax.all_to_all(sent, "azimuth", split_axis=0, concat_axis=0, tiled=True)

    filters, limits, sent = lax.optimization_barrier((basis_spectra, support, sent))
    mine, other = call(
        filter_body,
        [SMEM, SMEM, HBM],
        [((K * SUPPORT * 4, 128), BF16)] * 2,
        scratch=[pltpu.VMEM((K * SUPPORT, 4, WOUT), BF16), pltpu.VMEM((184, WOUT), F32), dma((1,))],
    )(spot, limits, in_hbm(jnp.swapaxes(filters, 1, 2).reshape(K * SUPPORT, 4, WOUT)))
    got = swap_bands(other)
    factors = [a for a in wide + narrow]
    held = [pltpu.VMEM(a.shape, F32) for a in factors]
    factors, sent = lax.optimization_barrier(([jnp.asarray(a) for a in factors], sent))
    flat, inv_t = call(
        flipped_table_body,
        [HBM] * 8,
        [((2, 384, 768), BF16), ((2, 512, 384), BF16)],
        nbytes=5 << 20,
        scratch=held + [pltpu.VMEM((2, 768, 384), BF16), pltpu.VMEM((2, 384, 512), BF16), dma((8,))],
    )(*[in_hbm(a) for a in factors])

    landed, mine, got = lax.optimization_barrier((landed, mine, got))
    (sent,) = call(spectra_body, [VMEM] * 3, [((SHARES, CHUNK_MID, 128), BF16)], flops=300 << 20)(landed, flat, inv_t)
    landed = lax.all_to_all(sent, JOINT, split_axis=0, concat_axis=0, tiled=True)
    mine, got, sent = lax.optimization_barrier((mine, got, sent))
    placed, staged = call(
        mixing_body, [SMEM, VMEM, VMEM, HBM], [((K * 16, HIN * 2 * M12), F32), ((K, C, C), BF16)], scratch=[dma((1,))]
    )(spot, mine, got, in_hbm(weights))

    chunk = (LANES, CHUNK_MID + 16 * K, 128)
    mine, other = call(
        middle_body,
        [SMEM, VMEM, VMEM, VMEM],
        [(chunk, BF16), (chunk, BF16)],
        flops=2 << 30,
        nbytes=3 << 20,
        scratch=[
            pltpu.VMEM((256, 256), BF16),
            pltpu.VMEM((192, 256), F32),
            pltpu.VMEM((384, 256), F32),
        ],
    )(spot, landed.reshape(HIN, 2, CHUNK_MID, 128), placed, staged)
    factors, mine, other = lax.optimization_barrier((factors, mine, other))
    got = swap_bands(other)
    tall, inv = call(
        table_body,
        [HBM] * 8,
        [((2, 768, 384), BF16), pltpu.HBM((2, 384, 512), BF16)],
        nbytes=5 << 20,
        scratch=held + [pltpu.VMEM((2, 384, 512), BF16), dma((8,)), dma((1,))],
        out_places=[VMEM, HBM],
    )(*[in_hbm(a) for a in factors])
    got, tall, inv = lax.optimization_barrier((got, tall, inv))
    (sent,) = call(merge_body, [SMEM, VMEM, VMEM], [((LANES, CHUNK_OUT, 128), BF16)], nbytes=2 << 20)(spot, mine, got)
    landed = lax.all_to_all(sent, "azimuth", split_axis=0, concat_axis=0, tiled=True)

    members = lax.axis_size("ens")

    def send(value, offset_even, offset_odd):
        offsets = (offset_even, offset_odd)
        pairs = [(i, (i + offsets[i % 2]) % members) for i in range(members)]
        return lax.ppermute(value, "ens", pairs)

    half = jnp.sum(landed[:, 2 * CHUNK_MID :, :].astype(F32), axis=0).astype(BF16)
    got = send(half, 1, -1)
    pair = (half.astype(F32) + got.astype(F32)).astype(BF16)
    beside = send(pair, -1, 1)
    across = send(beside, 2, -2)
    behind = send(beside, 1, -1)
    half = (pair.astype(F32) + across.astype(F32)) + (beside.astype(F32) + behind.astype(F32))
    far = swap_bands(half)
    (sent,) = call(
        fields_body,
        [VMEM, VMEM, HBM],
        [((LANES, CHUNK_IN, 128), BF16)],
        flops=300 << 20,
        scratch=[pltpu.VMEM((2, 384, 512), BF16), dma((1,))],
    )(landed, tall, in_hbm(inv))
    landed = lax.all_to_all(sent, "azimuth", split_axis=0, concat_axis=0, tiled=True)
    field_grad, conv_out = call(
        unpack_body, [VMEM], [((8 * WPART, C), BF16), ((VPART, 4, C), BF16)], scratch=[pltpu.VMEM((192, C), F32)]
    )(landed)
    weight_grad = jnp.concatenate([jnp.where(low, half, far), jnp.where(low, far, half)], axis=1)
    field_grad = jnp.swapaxes(field_grad.reshape(WPART, 8, C), 0, 1)
    return (jnp.swapaxes(conv_out, 0, 1)[None], field_grad[None], weight_grad.reshape(K, 16, C))


def solution(mesh):
    placed = (
        P("ens", "polar", "azimuth", None),
        P(None, "polar", None, None),
        P("polar", None),
        P(),
        P("ens", "polar", "azimuth", None),
    )
    return jax.shard_map(
        local,
        mesh=mesh,
        in_specs=placed,
        out_specs=(
            P("ens", "polar", "azimuth", None),
            P("ens", "polar", "azimuth", None),
            P(None, "azimuth", None),
        ),
        check_vma=False,
    )
```

```python
import math

import jax
import jax.numpy as jnp
import numpy as np
from jax import lax
from jax.experimental import pallas as pl
from jax.experimental.pallas import tpu as pltpu
from jax.sharding import PartitionSpec as P


WIN, WOUT, MODES = 1440, 720, 360
K, C, SUPPORT = 9, 256, 5
HOUT, HIN = 8, 16
LANES, BANDS = 16, 2
SHARES = LANES * BANDS
HALF = LANES // 2
M12, M16 = 12, 16
WPART, WROWS = 90, 96
VPART, VROWS = 45, 24
CHUNK_IN = WROWS + VROWS
CHUNK_MID = M16 + 2 * M12
CHUNK_OUT = 2 * CHUNK_MID + 16 * K
F32, BF16 = jnp.float32, jnp.bfloat16
JOINT = ("polar", "azimuth")


def factor_tables():
    def build(slots, part, steps, period, scale):
        mode_all, keep, imag = slots
        parts = []
        for e in range(BANDS):
            mode = mode_all + e
            ok = keep & (mode < MODES)
            alpha = 2 * math.pi * ((mode[None, :] * (part * np.arange(HALF)[:, None])) % period) / period
            beta = 2 * math.pi * ((mode[None, :] * steps[:, None]) % period) / period
            ok = ok[None, :] & (steps[:, None] < part)
            size = np.where(mode == 0, 1.0, 2.0)[None, :] / WIN if scale else 1.0
            parts.append(
                (
                    np.where(imag[None, :], -np.sin(alpha), np.cos(alpha)),
                    np.where(imag[None, :], -np.cos(alpha), -np.sin(alpha)),
                    np.where(ok, size * np.cos(beta), 0.0),
                    np.where(ok, size * np.sin(beta), 0.0),
                )
            )
        return [np.stack(group).astype(np.float32) for group in zip(*parts)]

    a, ri, i = np.meshgrid(np.arange(LANES), np.arange(2), np.arange(M12), indexing="ij")
    slots = ((2 * (M12 * a + i)).reshape(-1), np.ones(a.size, bool), ri.reshape(-1) == 1)
    wide = build(slots, WPART, np.arange(WROWS), WIN, False)
    ri, a, i = np.meshgrid(np.arange(2), np.arange(LANES), np.arange(M16), indexing="ij")
    slots = ((2 * (M12 * a + i)).reshape(-1), i.reshape(-1) < M12, ri.reshape(-1) == 1)
    narrow = build(slots, VPART, np.arange(2 * VROWS), WOUT, True)
    return wide, narrow


HBM = pl.BlockSpec(memory_space=pltpu.HBM)
VMEM = pl.BlockSpec(memory_space=pltpu.VMEM)
SMEM = pl.BlockSpec(memory_space=pltpu.SMEM)


def call(body, places, outs, flops=0, scratch=(), nbytes=1 << 20, vmem=16, out_places=None):
    return pl.pallas_call(
        body,
        out_shape=[jax.ShapeDtypeStruct(*o) if isinstance(o, tuple) else o for o in outs],
        in_specs=places,
        out_specs=out_places or [VMEM] * len(outs),
        scratch_shapes=list(scratch),
        compiler_params=pltpu.CompilerParams(vmem_limit_bytes=vmem << 20),
        cost_estimate=pl.CostEstimate(flops=flops, bytes_accessed=nbytes, transcendentals=0),
    )


def in_hbm(value):
    return pltpu.with_memory_space_constraint(value, pltpu.HBM)


def fetch(sources, targets, sems):
    copies = [pltpu.make_async_copy(s, t, sems.at[n]) for n, (s, t) in enumerate(zip(sources, targets))]
    for copy in copies:
        copy.start()
    return copies


def low_half(shape):
    return lax.broadcasted_iota(jnp.int32, shape, len(shape) - 1) < 64


def swap64(value):
    return pltpu.roll(value, 64, value.ndim - 1)


def dot(a, b):
    return jnp.dot(a, b, preferred_element_type=F32)


def one_hot(shape, row_of_column):
    row = lax.broadcasted_iota(jnp.int32, shape, 0)
    column = lax.broadcasted_iota(jnp.int32, shape, 1)
    return jnp.where(row == row_of_column(column), 1.0, 0.0).astype(BF16)


def row_of_latitude(column):
    return 16 * (column % 8) + column // 8


def row_of_output(column):
    return 48 * (column % 4) + column // 4


def pack_body(f_hbm, g_hbm, o_ref, f_ref, g_ref, flat_ref, sems):
    copies = fetch((g_hbm, f_hbm), (g_ref, f_ref), sems)
    copies[0].wait()
    for v in range(VPART):
        flat_ref[4 * v : 4 * (v + 1), :] = g_ref[v].astype(F32)
    flat_ref[4 * VPART : 192, :] = jnp.zeros((192 - 4 * VPART, C), F32)
    rows = dot(one_hot((192, 192), row_of_output), flat_ref[...].astype(BF16))
    keep = low_half((VROWS, 128))
    for o in range(4):
        for i in range(2):
            cols = slice(128 * i, 128 * (i + 1))
            top, bottom = rows[48 * o : 48 * o + 24, cols], rows[48 * o + 24 : 48 * o + 48, cols]
            even = jnp.where(keep, top, swap64(bottom))
            odd = jnp.where(keep, swap64(top), bottom)
            o_ref[4 * o + 2 * i, WROWS:CHUNK_IN, :] = even.astype(BF16)
            o_ref[4 * o + 2 * i + 1, WROWS:CHUNK_IN, :] = odd.astype(BF16)
    copies[1].wait()
    for j in range(6):
        count = min(128, 8 * WPART - 128 * j)
        order = one_hot((128, count), row_of_latitude)
        block = dot(order, f_ref[128 * j : 128 * j + count, :]).astype(BF16)
        for r in range(8):
            for h in range(2):
                piece = block[16 * r : 16 * (r + 1), 128 * h : 128 * (h + 1)]
                o_ref[2 * r + h, 16 * j : 16 * (j + 1), :] = piece


def flip(source, target, rows, columns):
    for i in range(rows // 128):
        for j in range(columns // 128):
            piece = source[128 * i : 128 * (i + 1), 128 * j : 128 * (j + 1)].astype(F32)
            target[128 * j : 128 * (j + 1), 128 * i : 128 * (i + 1)] = piece.T.astype(BF16)


def fill_wide(w, w_ref):
    for e in range(BANDS):
        for b in range(HALF):
            one, two = w[0][e, b : b + 1, :], w[1][e, b : b + 1, :]
            block = one * w[2][e] + two * w[3][e]
            w_ref[e, WROWS * b : WROWS * (b + 1), :] = block.astype(BF16)


def fill_narrow(v, v_ref):
    for e in range(BANDS):
        for b in range(HALF):
            one, two = v[0][e, b : b + 1, :], v[1][e, b : b + 1, :]
            for part in range(2):
                rows = slice(VROWS * part, VROWS * (part + 1))
                block = one * v[2][e, rows, :] + two * v[3][e, rows, :]
                start = VROWS * (HALF * part + b)
                v_ref[e, start : start + VROWS, :] = block.astype(BF16)


def table_body(*refs):
    factors, (w_ref, v_hbm) = refs[:8], refs[8:10]
    held, (v_ref, sems, out_sem) = refs[10:18], refs[18:]
    copies = fetch(factors[4:] + factors[:4], held[4:] + held[:4], sems)
    for copy in copies[:4]:
        copy.wait()
    fill_narrow(held[4:], v_ref)
    (out,) = fetch((v_ref,), (v_hbm,), out_sem)
    for copy in copies[4:]:
        copy.wait()
    fill_wide(held[:4], w_ref)
    out.wait()


def flipped_table_body(*refs):
    factors, (wt_ref, vt_ref) = refs[:8], refs[8:10]
    held, (w_ref, v_ref, sems) = refs[10:18], refs[18:]
    for copy in fetch(factors, held, sems):
        copy.wait()
    fill_wide(held[:4], w_ref)
    fill_narrow(held[4:], v_ref)
    for e in range(BANDS):
        flip(w_ref.at[e], wt_ref.at[e], HALF * WROWS, 2 * LANES * M12)
        flip(v_ref.at[e], vt_ref.at[e], 2 * HALF * VROWS, 2 * LANES * M16)


def spectra_body(r_ref, wt_ref, vt_ref, o_ref):
    left = r_ref[0:HALF, 0:WROWS, :].reshape(HALF * WROWS, 128).astype(F32)
    right = r_ref[HALF:LANES, 0:WROWS, :].reshape(HALF * WROWS, 128).astype(F32)
    g_left = r_ref[0:HALF, WROWS:CHUNK_IN, :].reshape(HALF * VROWS, 128).astype(F32)
    g_right = r_ref[HALF:LANES, WROWS:CHUNK_IN, :].reshape(HALF * VROWS, 128).astype(F32)
    keep = low_half((HALF * VROWS, 128))
    for e in range(BANDS):
        x = (left + right if e == 0 else left - right).astype(BF16)
        g = g_left + g_right if e == 0 else g_left - g_right
        turned = swap64(g)
        both = jnp.concatenate([jnp.where(keep, g, turned), jnp.where(keep, turned, g)], axis=0).astype(BF16)
        shares = slice(LANES * e, LANES * (e + 1))
        o_ref[shares, M16:CHUNK_MID, :] = dot(wt_ref[e], x).astype(BF16).reshape(LANES, 2 * M12, 128)
        got = dot(vt_ref[e], both)
        count = LANES * M16
        out = jnp.where(low_half((count, 128)), got[:count], got[count:])
        o_ref[shares, 0:M16, :] = out.astype(BF16).reshape(LANES, M16, 128)


def filter_body(spot_ref, support_ref, p_hbm, mine_ref, other_ref, p_ref, flat_ref, sems):
    (copy,) = fetch((p_hbm,), (p_ref,), sems)
    rows = K * SUPPORT * 4
    band, start = spot_ref[0, 0], 2 * M12 * spot_ref[0, 1]
    line = lax.broadcasted_iota(jnp.int32, (WOUT, 128), 0)
    slot = lax.broadcasted_iota(jnp.int32, (WOUT, 128), 1)
    place = slot % 64
    parity = jnp.where(slot < 64, band, 1 - band)
    mode = start + 2 * (place % M12) + parity
    hit = (line == mode + MODES * (place // M12)) & (place < 2 * M12) & (mode < MODES)
    chosen = jnp.where(hit, 1.0, 0.0).astype(BF16)
    row = lax.broadcasted_iota(jnp.int32, (rows, 128), 0)
    window, output = (row // 4) % SUPPORT, row % 4
    first = jnp.zeros((rows, 128), jnp.int32)
    last = jnp.zeros((rows, 128), jnp.int32)
    for o in range(4):
        first = jnp.where(output == o, support_ref[o, 0], first)
        last = jnp.where(output == o, support_ref[o, 1], last)
    copy.wait()
    for n in range(K * SUPPORT):
        flat_ref[4 * n : 4 * (n + 1), :] = p_ref[n].astype(F32)
    got = dot(flat_ref[0:rows, :].astype(BF16), chosen)
    got = jnp.where((window >= first) & (window <= last), got, 0.0)
    mine_ref[...] = got.astype(BF16)
    other_ref[...] = swap64(got).astype(BF16)


def mixing_body(spot_ref, mine_ref, got_ref, w_hbm, p_ref, w_ref, sems):
    (copy,) = fetch((w_hbm,), (w_ref,), sems)
    rows, width, count = K * 16, HIN * 2 * M12, K * SUPPORT * 4
    low = spot_ref[0, 0] == 0
    mine, got = mine_ref[...].astype(F32), got_ref[...].astype(F32)
    halves = (jnp.where(low, mine, got).astype(BF16), jnp.where(low, got, mine).astype(BF16))
    x = lax.broadcasted_iota(jnp.int32, (128, width), 0)
    lane = lax.broadcasted_iota(jnp.int32, (128, width), 1)
    same, cross = lane % M12, lane % (2 * M12) < M12
    straight = x == same + jnp.where(cross, 0, M12)
    turned = x == same + jnp.where(cross, M12, 0)
    tiles = (
        jnp.where(straight, jnp.where(cross, 1.0, -1.0), 0.0).astype(BF16),
        jnp.where(turned, 1.0, 0.0).astype(BF16),
    )
    row = lax.broadcasted_iota(jnp.int32, (count, width), 0)
    lane = lax.broadcasted_iota(jnp.int32, (count, width), 1)
    reach = 2 * (row % 4) + (row // 4) % SUPPORT - 2 - lane // (2 * M12)
    target = lax.broadcasted_iota(jnp.int32, (rows, count), 0)
    source = lax.broadcasted_iota(jnp.int32, (rows, count), 1)
    key = target - 16 * (source // 20) - 2 * (source % 4)
    total = jnp.zeros((rows, width), F32)
    for half in range(2):
        for ri in range(2):
            spread = dot(halves[half], tiles[ri])
            spread = jnp.where(reach == -8 * half, spread, 0.0).astype(BF16)
            collect = jnp.where(key == 8 * half + ri, 1.0, 0.0).astype(BF16)
            total = total + dot(collect, spread)
    p_ref[...] = total
    copy.wait()


def row_of_share(column):
    return 16 * (column % 16) + column // 16


def middle_body(band_ref, r_ref, p_ref, w_ref, mine_ref, other_ref, gs_ref, sg_ref, mixed_ref, back_ref, at_ref):
    keep = low_half((M16, 128))
    for o in range(HOUT):
        for i in range(2):
            first = r_ref[2 * o + i, 0, 0:M16, :].astype(F32)
            second = r_ref[2 * o + i, 1, 0:M16, :].astype(F32)
            cols = slice(128 * i, 128 * (i + 1))
            gs_ref[32 * o : 32 * o + 16, cols] = jnp.where(keep, first, swap64(second)).astype(BF16)
            gs_ref[32 * o + 16 : 32 * o + 32, cols] = jnp.where(keep, swap64(first), second).astype(BF16)
    used = M12 * 16
    low = band_ref[0, 0] == 0
    ordered = dot(one_hot((used, 256), row_of_share), gs_ref[...])
    gs = ordered.astype(BF16)
    left, right = ordered[:, :128], ordered[:, 128:]
    turned = jnp.concatenate([jnp.where(low, left, right), jnp.where(low, right, left)], axis=1).astype(BF16)
    width = HIN * 2 * M12
    x = jnp.concatenate(
        [r_ref[:, h, M16:CHUNK_MID, :].reshape(width, 128) for h in range(2)], axis=1
    )
    lane_mode = lax.broadcasted_iota(jnp.int32, (16, width), 1) % M12
    for k in range(0, K, 2):
        pair = min(2, K - k)
        row = lax.broadcasted_iota(jnp.int32, (16 * pair, used * pair), 0)
        column = lax.broadcasted_iota(jnp.int32, (16 * pair, used * pair), 1)
        spread = jnp.where(row == 16 * (column // used) + column % 16, 1.0, 0.0).astype(BF16)
        row = lax.broadcasted_iota(jnp.int32, (width, used * pair), 0) % M12
        column = (lax.broadcasted_iota(jnp.int32, (width, used * pair), 1) // 16) % M12
        grown = lax.dot_general(
            p_ref[16 * k : 16 * (k + pair), :].astype(BF16),
            spread,
            (((0,), (0,)), ((), ())),
            preferred_element_type=F32,
        )
        at_ref[:, used * k : used * (k + pair)] = jnp.where(row == column, grown, 0.0).astype(BF16)
    for k in range(K):
        placed = p_ref[16 * k : 16 * (k + 1), :]
        blocks = [jnp.where(lane_mode == m, placed, 0.0).astype(BF16) for m in range(M12)]
        mixed = dot(jnp.concatenate(blocks, axis=0), x).astype(BF16)
        mixed_ref[:, C * k : C * (k + 1)] = mixed
        grad = lax.dot_general(mixed, turned, (((0,), (0,)), ((), ())), preferred_element_type=F32)
        where_to = (slice(None), slice(CHUNK_MID + 16 * k, CHUNK_MID + 16 * (k + 1)), slice(None))
        shape = (LANES, 16, 128)
        mine_ref[where_to] = grad[:, :128].astype(BF16).reshape(shape)
        other_ref[where_to] = grad[:, 128:].astype(BF16).reshape(shape)
        back = lax.dot_general(gs, w_ref[k], (((1,), (1,)), ((), ())), preferred_element_type=F32)
        back_ref[used * k : used * (k + 1), :] = back.astype(BF16)
    out = dot(mixed_ref[...], w_ref[...].reshape(K * C, C)).astype(BF16)
    sg_ref[...] = dot(at_ref[...], back_ref[...])
    ordered = lax.dot_general(
        one_hot((used, 256), row_of_share),
        out,
        (((0,), (0,)), ((), ())),
        preferred_element_type=F32,
    )

    def output_rows(n):
        o, q = n // 4, n % 4
        cols = slice(128 * (q // 2), 128 * (q // 2 + 1))
        re = ordered[32 * o : 32 * o + 16, cols]
        im = ordered[32 * o + 16 : 32 * o + 32, cols]
        return jnp.where(keep, re, swap64(im)) if q % 2 == 0 else jnp.where(keep, swap64(re), im)

    def field_rows(n):
        r, h = n // 2, n % 2
        return sg_ref[24 * r : 24 * (r + 1), 128 * h : 128 * (h + 1)]

    for a in range(LANES):
        for rows, make in ((slice(0, M16), output_rows), (slice(M16, CHUNK_MID), field_rows)):
            first, second = make(a), make(a + LANES)
            mine_ref[a, rows, :] = jnp.where(low, first, second).astype(BF16)
            other_ref[a, rows, :] = jnp.where(low, second, first).astype(BF16)


def merge_body(band_ref, mine_ref, got_ref, o_ref):
    low = band_ref[0, 0] == 0
    for a in range(LANES):
        mine, got = mine_ref[a, 0:CHUNK_MID, :].astype(F32), got_ref[a, 0:CHUNK_MID, :].astype(F32)
        o_ref[a, 0:CHUNK_MID, :] = jnp.where(low, mine, got).astype(BF16)
        o_ref[a, CHUNK_MID : 2 * CHUNK_MID, :] = jnp.where(low, got, mine).astype(BF16)
        mine, got = mine_ref[a, CHUNK_MID:, :].astype(F32), got_ref[a, CHUNK_MID:, :].astype(F32)
        o_ref[a, 2 * CHUNK_MID :, :] = (mine + got).astype(BF16)


def fields_body(r_ref, w_ref, v_hbm, o_ref, v_ref, sems):
    (copy,) = fetch((v_hbm,), (v_ref,), sems)
    fields, outs = [], []
    for e in range(BANDS):
        start = CHUNK_MID * e
        sg = r_ref[:, start + M16 : start + CHUNK_MID, :].reshape(LANES * 2 * M12, 128)
        fields.append(dot(w_ref[e], sg))
    for side in range(2):
        lanes = slice(HALF * side, HALF * (side + 1))
        field = fields[0] + fields[1] if side == 0 else fields[0] - fields[1]
        o_ref[lanes, 0:WROWS, :] = field.astype(BF16).reshape(HALF, WROWS, 128)
    copy.wait()
    for e in range(BANDS):
        start = CHUNK_MID * e
        c = r_ref[:, start : start + M16, :].reshape(LANES * M16, 128).astype(F32)
        turned = swap64(c)
        keep = low_half(c.shape)
        both = jnp.concatenate([jnp.where(keep, c, turned), jnp.where(keep, turned, c)], axis=0).astype(BF16)
        got = dot(v_ref[e], both)
        count = HALF * VROWS
        outs.append(jnp.where(low_half((count, 128)), got[:count], got[count:]))
    for side in range(2):
        lanes = slice(HALF * side, HALF * (side + 1))
        out = outs[0] + outs[1] if side == 0 else outs[0] - outs[1]
        o_ref[lanes, WROWS:CHUNK_IN, :] = out.astype(BF16).reshape(HALF, VROWS, 128)


def unpack_body(r_ref, f_ref, c_ref, flat_ref):
    for j in range(6):
        count = min(128, 8 * WPART - 128 * j)
        halves = [
            jnp.concatenate([r_ref[2 * r + h, 16 * j : 16 * (j + 1), :] for r in range(8)], axis=0)
            for h in range(2)
        ]
        order = one_hot((128, count), row_of_latitude)
        block = lax.dot_general(
            order, jnp.concatenate(halves, axis=1), (((0,), (0,)), ((), ())), preferred_element_type=F32
        )
        f_ref[128 * j : 128 * j + count, :] = block.astype(BF16)
    keep = low_half((VROWS, 128))
    for o in range(4):
        for i in range(2):
            even = r_ref[4 * o + 2 * i, WROWS:CHUNK_IN, :].astype(F32)
            odd = r_ref[4 * o + 2 * i + 1, WROWS:CHUNK_IN, :].astype(F32)
            cols = slice(128 * i, 128 * (i + 1))
            flat_ref[48 * o : 48 * o + 24, cols] = jnp.where(keep, even, swap64(odd))
            flat_ref[48 * o + 24 : 48 * o + 48, cols] = jnp.where(keep, swap64(even), odd)
    rows = lax.dot_general(
        one_hot((192, 192), row_of_output),
        flat_ref[...].astype(BF16),
        (((0,), (0,)), ((), ())),
        preferred_element_type=F32,
    )
    for v in range(VPART):
        c_ref[v] = rows[4 * v : 4 * (v + 1), :].astype(BF16)


def swap_bands(value):
    return lax.ppermute(value, "polar", [(0, 1), (1, 0)])


def local(fields, basis_spectra, support, weights, out_grad):
    band = lax.axis_index("polar").astype(jnp.int32)
    low = band == 0
    spot = jnp.stack([band, lax.axis_index("azimuth").astype(jnp.int32)]).reshape(1, 2)
    wide, narrow = factor_tables()
    dma = pltpu.SemaphoreType.DMA
    (sent,) = call(
        pack_body,
        [HBM, HBM],
        [((LANES, CHUNK_IN, 128), BF16)],
        scratch=[
            pltpu.VMEM((8 * WPART, C), BF16),
            pltpu.VMEM((VPART, 4, C), BF16),
            pltpu.VMEM((192, C), F32),
            dma((2,)),
        ],
    )(
        in_hbm(jnp.swapaxes(fields[0], 0, 1).reshape(8 * WPART, C)), in_hbm(jnp.swapaxes(out_grad[0], 0, 1))
    )
    landed = lax.all_to_all(sent, "azimuth", split_axis=0, concat_axis=0, tiled=True)

    filters, limits, sent = lax.optimization_barrier((basis_spectra, support, sent))
    mine, other = call(
        filter_body,
        [SMEM, SMEM, HBM],
        [((K * SUPPORT * 4, 128), BF16)] * 2,
        scratch=[pltpu.VMEM((K * SUPPORT, 4, WOUT), BF16), pltpu.VMEM((184, WOUT), F32), dma((1,))],
    )(spot, limits, in_hbm(jnp.swapaxes(filters, 1, 2).reshape(K * SUPPORT, 4, WOUT)))
    got = swap_bands(other)
    factors = [a for a in wide + narrow]
    held = [pltpu.VMEM(a.shape, F32) for a in factors]
    factors, sent = lax.optimization_barrier(([jnp.asarray(a) for a in factors], sent))
    flat, inv_t = call(
        flipped_table_body,
        [HBM] * 8,
        [((2, 384, 768), BF16), ((2, 512, 384), BF16)],
        nbytes=5 << 20,
        scratch=held + [pltpu.VMEM((2, 768, 384), BF16), pltpu.VMEM((2, 384, 512), BF16), dma((8,))],
    )(*[in_hbm(a) for a in factors])

    landed, mine, got = lax.optimization_barrier((landed, mine, got))
    (sent,) = call(spectra_body, [VMEM] * 3, [((SHARES, CHUNK_MID, 128), BF16)], flops=300 << 20)(landed, flat, inv_t)
    landed = lax.all_to_all(sent, JOINT, split_axis=0, concat_axis=0, tiled=True)
    mine, got, sent = lax.optimization_barrier((mine, got, sent))
    placed, staged = call(
        mixing_body, [SMEM, VMEM, VMEM, HBM], [((K * 16, HIN * 2 * M12), F32), ((K, C, C), BF16)], scratch=[dma((1,))]
    )(spot, mine, got, in_hbm(weights))

    chunk = (LANES, CHUNK_MID + 16 * K, 128)
    mine, other = call(
        middle_body,
        [SMEM, VMEM, VMEM, VMEM],
        [(chunk, BF16), (chunk, BF16)],
        flops=2 << 30,
        nbytes=3 << 20,
        scratch=[
            pltpu.VMEM((256, 256), BF16),
            pltpu.VMEM((384, 256), F32),
            pltpu.VMEM((192, K * C), BF16),
            pltpu.VMEM((K * 192, 256), BF16),
            pltpu.VMEM((384, K * 192), BF16),
        ],
    )(spot, landed.reshape(HIN, 2, CHUNK_MID, 128), placed, staged)
    factors, mine, other = lax.optimization_barrier((factors, mine, other))
    got = swap_bands(other)
    tall, inv = call(
        table_body,
        [HBM] * 8,
        [((2, 768, 384), BF16), pltpu.HBM((2, 384, 512), BF16)],
        nbytes=5 << 20,
        scratch=held + [pltpu.VMEM((2, 384, 512), BF16), dma((8,)), dma((1,))],
        out_places=[VMEM, HBM],
    )(*[in_hbm(a) for a in factors])
    got, tall, inv = lax.optimization_barrier((got, tall, inv))
    (sent,) = call(merge_body, [SMEM, VMEM, VMEM], [((LANES, CHUNK_OUT, 128), BF16)], nbytes=2 << 20)(spot, mine, got)
    landed = lax.all_to_all(sent, "azimuth", split_axis=0, concat_axis=0, tiled=True)

    members = lax.axis_size("ens")

    def send(value, offset_even, offset_odd):
        offsets = (offset_even, offset_odd)
        pairs = [(i, (i + offsets[i % 2]) % members) for i in range(members)]
        return lax.ppermute(value, "ens", pairs)

    half = jnp.sum(landed[:, 2 * CHUNK_MID :, :].astype(F32), axis=0).astype(BF16)
    got = send(half, 1, -1)
    pair = (half.astype(F32) + got.astype(F32)).astype(BF16)
    beside = send(pair, -1, 1)
    across = send(beside, 2, -2)
    behind = send(beside, 1, -1)
    half = (pair.astype(F32) + across.astype(F32)) + (beside.astype(F32) + behind.astype(F32))
    far = swap_bands(half)
    (sent,) = call(
        fields_body,
        [VMEM, VMEM, HBM],
        [((LANES, CHUNK_IN, 128), BF16)],
        flops=300 << 20,
        scratch=[pltpu.VMEM((2, 384, 512), BF16), dma((1,))],
    )(landed, tall, in_hbm(inv))
    landed = lax.all_to_all(sent, "azimuth", split_axis=0, concat_axis=0, tiled=True)
    field_grad, conv_out = call(
        unpack_body, [VMEM], [((8 * WPART, C), BF16), ((VPART, 4, C), BF16)], scratch=[pltpu.VMEM((192, C), F32)]
    )(landed)
    weight_grad = jnp.concatenate([jnp.where(low, half, far), jnp.where(low, far, half)], axis=1)
    field_grad = jnp.swapaxes(field_grad.reshape(WPART, 8, C), 0, 1)
    return (jnp.swapaxes(conv_out, 0, 1)[None], field_grad[None], weight_grad.reshape(K, 16, C))


def solution(mesh):
    placed = (
        P("ens", "polar", "azimuth", None),
        P(None, "polar", None, None),
        P("polar", None),
        P(),
        P("ens", "polar", "azimuth", None),
    )
    return jax.shard_map(
        local,
        mesh=mesh,
        in_specs=placed,
        out_specs=(
            P("ens", "polar", "azimuth", None),
            P("ens", "polar", "azimuth", None),
            P(None, "azimuth", None),
        ),
        check_vma=False,
    )
```
